32 devices in a mesh: tm: 16 (over z, y, core), video: 2 (over x).
Axes of the slice: x: 2, y: 2, z: 4, core: 2. Of those that a mesh axis runs over, the one named last changes fastest.
Arguments:
- memory: bfloat16 [2, 16, 1, 64, 768], P('video', 'tm'), may hold values from -24 to 24
- frames: float32 [2, 16, 1, 128, 768], P('video', 'tm'), may hold values from -6 to 6
- mem_cot: bfloat16 [2, 16, 1, 64, 768], P('video', 'tm'), may hold values from -3 to 3
- slot_used: int32 [2, 16, 1], P('video', 'tm'), may hold values 0 or 1
- key_bias: float32 [2, 16, 1, 12, 128], P('video', 'tm'), may hold values from -6 to 300
- start_offset: int32 [2, 1], P('video'), may hold values from 0 to 2047
- norm_gain: float32 [768], replicated, may hold values from 0.5 to 1.5
- w_query: bfloat16 [768, 768], replicated, may hold values from -0.21875 to 0.21875
- w_key: bfloat16 [768, 768], replicated, may hold values from -0.21875 to 0.21875
- w_value: bfloat16 [768, 768], replicated, may hold values from -0.21875 to 0.21875
- w_out: bfloat16 [768, 768], replicated, may hold values from -0.21875 to 0.21875
Outputs:
- grad_memory: float32 [2, 16, 1, 64, 768], P('video', 'tm')
- grad_query: float32 [768, 768], P('tm', 'video')
- grad_key: float32 [768, 768], P('tm', 'video')
- grad_value: float32 [768, 768], P('tm', 'video')
- grad_out: float32 [768, 768], P('tm', 'video')
- grad_gain: float32 [768], replicated
The draws below stay inside these ranges and needn't reach their ends.
All inputs are finite; a program needn't handle non-finite values. No bound on the sum of `slot_used` on one device may be relied on, other than what follows from the above.
Results may differ from the reference program's by a relative error of at most 0.019.
Values sent between devices are 32-bit elements; how exact they have to be, the bound alone decides.
A program may use at most 64 MiB of HBM per device.

```python
import math
import jax
import jax.numpy as jnp
from jax import lax

D = 768
H = 12
HD = 64
R = 64
L = 128
STREAMS = 1
GROUPS = 2
OWNERS = 16


def draw_memory(key, part):
    full_shape = (GROUPS, OWNERS, STREAMS, R, D)
    key_noise, key_rows, key_cols = jax.random.split(key, 3)
    gaussian = jax.random.normal(key_noise, full_shape, jnp.float32)
    row_scale = jnp.exp(jax.random.uniform(key_rows, full_shape[:4] + (1,), jnp.float32, math.log(0.3), math.log(3.0)))
    column_scale = jnp.exp(jax.random.uniform(key_cols, (D,), jnp.float32, math.log(0.3), math.log(3.0)))
    values_drawn = gaussian * row_scale * column_scale
    return jnp.clip(values_drawn, -24.0, 24.0).astype(jnp.bfloat16)


def draw_key_bias(key, part):
    full_shape = (GROUPS, OWNERS, STREAMS, H, L)
    key_noise = jax.random.fold_in(key, 0)
    values_drawn = jnp.clip(jax.random.normal(key_noise, full_shape, jnp.float32), -6.0, 6.0)
    return values_drawn


def with_ends(entries, stream_key, least, top_value):
    shape = entries.shape
    index_at = [jax.random.randint(jax.random.fold_in(stream_key, axis), (), 0, shape[axis]) for axis in range(len(shape))]
    entries = entries.at[tuple(index_at)].set(least)
    longest = shape.index(max(shape))
    index_at[longest] = (index_at[longest] + 1) % shape[longest]
    return entries.at[tuple(index_at)].set(top_value)


def block_levels(stream_key, shape, cuts, low, high):
    def one(dim, blocks):
        heights = jax.random.uniform(jax.random.fold_in(jax.random.fold_in(stream_key, 6), dim), (blocks,), jnp.float32, low / len(cuts), high / len(cuts))
        return jnp.repeat(jnp.exp(heights), shape[dim] // blocks).reshape((-1,) + (1,) * (len(shape) - dim - 1))

    loudness = one(*cuts[0])
    for cut in cuts[1:]:
        loudness = loudness * one(*cut)
    return loudness


def normal_values(key, dims, scale, bound, cuts=(), kind=jnp.bfloat16):
    result = jax.random.normal(key, dims, jnp.float32) * scale
    if len(cuts) > 0:
        result = block_levels(key, dims, cuts, -0.22, 0.18) * result
    return jnp.clip(result, min=-bound, max=bound).astype(kind)


def setup_inputs(seed: int = 0) -> dict:
    key_list = jax.random.split(jax.random.key(seed), 12)
    return {
        "memory": draw_memory(jax.random.fold_in(key_list[11], 71), 0),
        "frames": normal_values(key_list[1], (GROUPS, OWNERS, STREAMS, L, D), 1.0, 6.0, ((0, 2), (1, 16)), jnp.float32),
        "mem_cot": normal_values(key_list[2], (GROUPS, OWNERS, STREAMS, R, D), 0.5, 3.0, ((0, 2), (1, 16))),
        "slot_used": with_ends((jax.random.randint(key_list[3], (GROUPS, OWNERS, STREAMS), 0, 4) < 3).astype(jnp.int32), jax.random.fold_in(key_list[3], 1), 0, 1),
        "key_bias": draw_key_bias(jax.random.fold_in(key_list[11], 71), 0),
        "start_offset": jax.random.randint(key_list[5], (GROUPS, STREAMS), 0, L * OWNERS).astype(jnp.int32),
        "norm_gain": jnp.clip(1.0 + 0.1 * jax.random.normal(key_list[6], (D,), jnp.float32), 0.5, 1.5),
        "w_query": normal_values(key_list[7], (D, D), D ** -0.5, 0.21875),
        "w_key": normal_values(key_list[8], (D, D), D ** -0.5, 0.21875),
        "w_value": normal_values(key_list[9], (D, D), D ** -0.5, 0.21875),
        "w_out": normal_values(key_list[10], (D, D), D ** -0.5, 0.21875),
    }


NORM_EPSILON = 1e-06

def product(form, left, right):
    return jnp.einsum(form, left.astype(jnp.float32), right.astype(jnp.float32), precision=lax.Precision.HIGHEST)

def encoding(offsets, position, clip_len, features):
    within = jnp.arange(clip_len, dtype=jnp.int32)
    frame_time = offsets[:, None] + position * clip_len + within[None, :]
    half_width = features // 2
    frequency = 0.0625 * jnp.exp(-math.log(1000.0) * jnp.arange(half_width, dtype=jnp.float32) / half_width)
    phases = frame_time.astype(jnp.float32)[:, :, None] * frequency
    return jnp.concatenate([jnp.sin(phases), jnp.cos(phases)], axis=-1)

def recompute(memory_full, frame_rows, bias_rows, offsets, position, norm_gain, w_query, w_key, w_value):
    batch, row_count, features = memory_full.shape
    inv_rms = lax.rsqrt(lax.optimization_barrier(jnp.mean(memory_full * memory_full, axis=-1, keepdims=True)) + NORM_EPSILON)
    unit_rows = memory_full * inv_rms
    normed = (unit_rows * norm_gain).astype(jnp.bfloat16)
    key_input = (frame_rows + encoding(offsets, position, frame_rows.shape[1], features)).astype(jnp.bfloat16)
    query_proj = product('brd,de->bre', normed, w_query).astype(jnp.bfloat16)
    key_proj = product('bld,de->ble', key_input, w_key).astype(jnp.bfloat16)
    value_proj = product('bld,de->ble', key_input, w_value).astype(jnp.bfloat16)
    query_heads = query_proj.reshape(batch, row_count, H, HD)
    key_heads = key_proj.reshape(batch, -1, H, HD)
    value_heads = value_proj.reshape(batch, -1, H, HD)
    scores = product('brhd,blhd->bhrl', query_heads, key_heads) * HD ** (-0.5) + bias_rows[:, :, None, :]
    attn_prob = jax.nn.softmax(scores, axis=-1)
    attn_half = attn_prob.astype(jnp.bfloat16)
    attended = product('bhrl,blhd->brhd', attn_half, value_heads).astype(jnp.bfloat16).reshape(batch, row_count, features)
    return (inv_rms, unit_rows, normed, key_input, query_heads, key_heads, value_heads, attn_prob, attn_half, attended)

def chain_part(grad_in, slot_live, unit_rows, inv_rms, attn_prob, key_heads, value_heads, norm_gain, w_query, w_out):
    batch, row_count, features = grad_in.shape
    out_grad = (slot_live[:, None, None] * grad_in).astype(jnp.bfloat16)
    att_grad = product('bre,de->brd', out_grad, w_out).astype(jnp.bfloat16)
    att_heads = att_grad.reshape(batch, row_count, H, HD)
    prob_grad = product('brhd,blhd->bhrl', att_heads, value_heads)
    inner_sum = lax.optimization_barrier(jnp.sum(attn_prob * prob_grad, axis=-1, keepdims=True))
    score_grad = (attn_prob * (prob_grad - inner_sum) * HD ** (-0.5)).astype(jnp.bfloat16)
    query_grad = product('bhrl,blhd->brhd', score_grad, key_heads).astype(jnp.bfloat16).reshape(batch, row_count, features)
    normed_grad = product('bre,de->brd', query_grad, w_query)
    gain_term = lax.optimization_barrier(jnp.sum(normed_grad * unit_rows, axis=(0, 1)))
    scaled_grad = normed_grad * norm_gain
    passed = grad_in + inv_rms * (scaled_grad - unit_rows * lax.optimization_barrier(jnp.mean(scaled_grad * unit_rows, axis=-1, keepdims=True)))
    return (passed, out_grad, att_heads, score_grad, query_grad, gain_term)

def weight_part(normed, key_input, query_heads, attn_half, attended, out_grad, att_heads, score_grad, query_grad):
    batch, length, features = key_input.shape
    value_grad = product('bhrl,brhd->blhd', attn_half, att_heads).astype(jnp.bfloat16).reshape(batch, length, features)
    key_grad = product('bhrl,brhd->blhd', score_grad, query_heads).astype(jnp.bfloat16).reshape(batch, length, features)
    return (product('brd,bre->de', normed, query_grad), product('bld,ble->de', key_input, key_grad), product('bld,ble->de', key_input, value_grad), product('brd,bre->de', attended, out_grad))

def reference(memory, frames, mem_cot, slot_used, key_bias, start_offset, norm_gain, w_query, w_key, w_value, w_out):
    groups, owners, streams, row_count, features = memory.shape
    batch = groups * streams
    offsets = start_offset.reshape(batch)

    def take(array, owner):
        picked = lax.dynamic_index_in_dim(array, owner, 1, keepdims=False)
        return picked.reshape((batch,) + picked.shape[2:])

    def one_clip(carried, owner):
        incoming, sum_query, sum_key, sum_value, sum_out, sum_gain = carried
        parts = recompute(take(memory, owner).astype(jnp.float32), take(frames, owner), take(key_bias, owner), offsets, owner, norm_gain, w_query, w_key, w_value)
        inv_rms, unit_rows, normed, key_input, query_heads, key_heads, value_heads, attn_prob, attn_half, attended = parts
        grad_in = incoming + take(mem_cot, owner).astype(jnp.float32)
        passed, out_grad, att_heads, score_grad, query_grad, gain_term = chain_part(grad_in, take(slot_used, owner).astype(jnp.float32), unit_rows, inv_rms, attn_prob, key_heads, value_heads, norm_gain, w_query, w_out)
        weight_terms = weight_part(normed, key_input, query_heads, attn_half, attended, out_grad, att_heads, score_grad, query_grad)
        return ((passed, sum_query + weight_terms[0], sum_key + weight_terms[1], sum_value + weight_terms[2], sum_out + weight_terms[3], sum_gain + gain_term), passed)
    zero_square = jnp.zeros((features, features), jnp.float32)
    start = (jnp.zeros((batch, row_count, features), jnp.float32), zero_square, zero_square, zero_square, zero_square, jnp.zeros((features,), jnp.float32))
    owner_order = jnp.arange(owners - 1, -1, -1, dtype=jnp.int32)
    final, stacked = lax.scan(one_clip, start, owner_order)
    grad_memory = jnp.flip(stacked, 0).reshape(owners, groups, streams, row_count, features).transpose(1, 0, 2, 3, 4)
    mean_scale = 1.0 / (groups * owners * streams)
    return (grad_memory, final[1] * mean_scale, final[2] * mean_scale, final[3] * mean_scale, final[4] * mean_scale, final[5] * mean_scale)
```

```python
import functools
import math
import types

import jax
import jax.numpy as jnp
from jax import lax
from jax.experimental import pallas as pl
from jax.experimental.pallas import tpu as pltpu
from jax.sharding import PartitionSpec as P

NORM_EPSILON = 1e-06
MESH = pl.DeviceIdType.MESH
F32 = jnp.float32
BF16 = jnp.bfloat16
NN = (((1,), (0,)), ((), ()))
NT = (((1,), (1,)), ((), ()))
TN = (((0,), (0,)), ((), ()))
CHUNKS = 4


def dot(left, right, form):
    return lax.dot_general(left, right, form, preferred_element_type=F32)


def key_rows(frame_rows, offset, position):
    length, features = frame_rows.shape
    within = jnp.arange(length, dtype=jnp.int32)
    frame_time = (offset + position * length + within).astype(F32)
    half_width = features // 2
    frequency = 0.0625 * jnp.exp(-math.log(1000.0) * jnp.arange(half_width, dtype=F32) / half_width)
    phases = frame_time[:, None] * frequency
    return frame_rows + jnp.concatenate([jnp.sin(phases), jnp.cos(phases)], axis=-1)


def group_member(groups, g):
    me = lax.axis_index("tm")
    return {"video": lax.div(g, 2), "tm": (me // 2) * 2 + lax.rem(g, 2)}


def whole_kernel(
    owners, groups, heads,
    slot_ref, mem_ref, keyin_ref, cot_ref, bias_ref, gain_ref, wq_ref, wk_ref, wv_ref, wo_ref,
    grad_ref, out_ref, gain_out_ref,
    a1_ref, a2_ref, b1_ref, b2_ref, gsum_ref,
    incoming, mine, prob, half, kbd, vbd, qp, att_all, sg_all, og_all, qg_all, unit_ref, inv_ref, wot, wqt,
    chain_send, chain_recv, a_send, a_recv,
    *reduce_scratch,
):
    me = lax.axis_index("tm")
    vid = lax.axis_index("video")
    chips = owners // 2
    bits = chips.bit_length() - 1
    chip, core = me // 2, lax.rem(me, 2)
    peers = [chip + (1 - 2 * lax.rem(lax.div(chip, 2 ** b), 2)) * 2 ** b for b in range(bits)]
    rows, features = mem_ref.shape
    length = keyin_ref.shape[0]
    head = features // heads
    pairs = heads // 2
    pw = 2 * head
    members = 2 * groups
    g_me = vid * 2 + lax.rem(me, 2)
    scale = head ** (-0.5)

    barrier = pltpu.get_barrier_semaphore()
    for off in range(1, members):
        pl.semaphore_signal(barrier, inc=1, device_id=group_member(groups, lax.rem(g_me + off, members)), device_id_type=MESH)

    for peer in peers:
        pl.semaphore_signal(barrier, inc=1, device_id={"tm": peer * 2 + core}, device_id_type=MESH)

    @pl.when(me > 0)
    def _():
        pl.semaphore_signal(barrier, inc=1, device_id={"tm": me - 1}, device_id_type=MESH)

    @pl.when(me < owners - 1)
    def _():
        pl.semaphore_signal(barrier, inc=1, device_id={"tm": me + 1}, device_id_type=MESH)

    ends = jnp.where(me > 0, 1, 0) + jnp.where(me < owners - 1, 1, 0)
    pl.semaphore_wait(barrier, members - 1 + bits + ends)

    def a_copy(which, src, dst, off):
        g = lax.rem(g_me + off, members)
        return pltpu.make_async_remote_copy(
            src_ref=src, dst_ref=dst.at[g_me], send_sem=a_send.at[which, off], recv_sem=a_recv.at[which, g_me],
            device_id=group_member(groups, g), device_id_type=MESH,
        )

    for off in range(1, members):
        a_copy(0, keyin_ref, a1_ref, off).start()
    a1_ref[g_me] = keyin_ref[...]

    mem = mem_ref[...].astype(F32)
    inv = lax.rsqrt(jnp.mean(mem * mem, axis=-1, keepdims=True) + NORM_EPSILON)
    unit = mem * inv
    unit_ref[...] = unit
    inv_ref[...] = jnp.broadcast_to(inv, inv_ref.shape)
    normed = (unit * gain_ref[...]).astype(BF16)
    mine[1] = normed.astype(F32)
    keyin = keyin_ref[...].astype(BF16)
    query = dot(normed, wq_ref[...], NN).astype(BF16)
    qp[...] = query
    kp = dot(keyin, wk_ref[...], NN).astype(BF16)
    vp = dot(keyin, wv_ref[...], NN).astype(BF16)
    low = lax.broadcasted_iota(jnp.int32, (length, pw), 1) < head
    zero = jnp.zeros((length, pw), BF16)
    for p in range(pairs):
        kk = kp[:, p * pw:(p + 1) * pw]
        vv = vp[:, p * pw:(p + 1) * pw]
        kbd[p, :length] = jnp.where(low, kk, zero)
        kbd[p, length:] = jnp.where(low, zero, kk)
        vbd[p, :length] = jnp.where(low, vv, zero)
        vbd[p, length:] = jnp.where(low, zero, vv)
    wot[...] = jnp.transpose(wo_ref[...])
    wqt[...] = jnp.transpose(wq_ref[...])
    scores = [dot(query[:, p * pw:(p + 1) * pw], kbd[p], NT) for p in range(pairs)]
    for p in range(pairs):
        halves = []
        for q in range(2):
            h = 2 * p + q
            s = scores[p][:, q * length:(q + 1) * length] * scale + bias_ref[h:h + 1, :]
            e = jnp.exp(s - jnp.max(s, axis=-1, keepdims=True))
            pr = e / jnp.sum(e, axis=-1, keepdims=True)
            prob[:, h * length:(h + 1) * length] = pr
            halves.append(pr.astype(BF16))
        both = jnp.concatenate(halves, axis=-1)
        half[:, p * 2 * length:(p + 1) * 2 * length] = both
        mine[0, :, p * pw:(p + 1) * pw] = dot(both, vbd[p], NN).astype(BF16).astype(F32)

    for off in range(1, members):
        g = lax.rem(g_me + off, members)
        a_copy(1, mine.at[lax.rem(g, 2)], a2_ref, off).start()
    a2_ref[g_me] = mine[lax.rem(me, 2)]

    live = slot_ref[0].astype(F32)
    step = rows // CHUNKS

    def chain_copy(c):
        return pltpu.make_async_remote_copy(
            src_ref=grad_ref.at[pl.ds(c * step, step)], dst_ref=incoming.at[pl.ds(c * step, step)],
            send_sem=chain_send.at[c], recv_sem=chain_recv.at[c],
            device_id={"tm": jnp.maximum(me - 1, 0)}, device_id_type=MESH,
        )

    @pl.when(me == owners - 1)
    def _():
        incoming[...] = jnp.zeros_like(incoming)

    gain_total = jnp.zeros((1, features), F32)
    for c in range(CHUNKS):
        r = slice(c * step, (c + 1) * step)

        @pl.when(me < owners - 1)
        def _():
            chain_copy(c).wait_recv()

        grad_in = incoming[r, :] + cot_ref[r, :].astype(F32)
        og = (live * grad_in).astype(BF16)
        att = dot(og, wot[...], NN).astype(BF16)
        prob_grads = [dot(att[:, p * pw:(p + 1) * pw], vbd[p], NT) for p in range(pairs)]
        query_grads = []
        score_grads = []
        for p in range(pairs):
            for q in range(2):
                h = 2 * p + q
                pg = prob_grads[p][:, q * length:(q + 1) * length]
                pr = prob[r, h * length:(h + 1) * length]
                inner = jnp.sum(pr * pg, axis=-1, keepdims=True)
                score_grads.append((pr * (pg - inner) * scale).astype(BF16))
            query_grads.append(dot(jnp.concatenate(score_grads[-2:], axis=-1), kbd[p], NN).astype(BF16))
        qg = jnp.concatenate(query_grads, axis=-1)
        ng = dot(qg, wqt[...], NN)
        un = unit_ref[r, :]
        gain_total = gain_total + jnp.sum(ng * un, axis=0, keepdims=True)
        sc = ng * gain_ref[...]
        grad_ref[r, :] = grad_in + inv_ref[r, 0:1] * (sc - un * jnp.mean(sc * un, axis=-1, keepdims=True))

        @pl.when(me > 0)
        def _():
            chain_copy(c).start()

        og_all[r, :] = og
        att_all[r, :] = att
        qg_all[r, :] = qg
        for h in range(heads):
            sg_all[r, h * length:(h + 1) * length] = score_grads[h]

    gsum_ref[...] = gain_total

    width = features // groups
    lowr = lax.broadcasted_iota(jnp.int32, (rows, pw), 1) < head
    zr = jnp.zeros((rows, pw), BF16)

    def put(out, which, p, value):
        for v in range(groups):
            lo, hi = max(p * pw, v * width), min((p + 1) * pw, (v + 1) * width)
            if lo < hi:
                out[which, v, :, lo - v * width:hi - v * width] = value[:, lo - p * pw:hi - p * pw]

    for p in range(pairs):
        for which, (left_ref, right_ref) in enumerate(((sg_all, qp), (half, att_all))):
            right = right_ref[:, p * pw:(p + 1) * pw]
            right = jnp.concatenate([jnp.where(lowr, right, zr), jnp.where(lowr, zr, right)], axis=0)
            base = 2 * p * length
            left = jnp.concatenate([left_ref[:, base:base + length], left_ref[:, base + length:base + 2 * length]], axis=0)
            put(b1_ref, which, p, dot(left, right, TN).astype(BF16).astype(F32))
        put(b2_ref, 0, p, og_all[:, p * pw:(p + 1) * pw].astype(F32))
        put(b2_ref, 1, p, qg_all[:, p * pw:(p + 1) * pw].astype(F32))

    def a_arrive():
        for off in range(1, members):
            g = lax.rem(g_me + members - off, members)
            for which, dst in ((0, a1_ref), (1, a2_ref)):
                a_copy(which, dst.at[g_me], dst, off).wait_send()
                pltpu.make_async_remote_copy(
                    src_ref=dst.at[g], dst_ref=dst.at[g], send_sem=a_send.at[which, off], recv_sem=a_recv.at[which, g],
                    device_id=group_member(groups, g), device_id_type=MESH,
                ).wait_recv()

    reduce_part(
        owners, groups, peers, a_arrive, a1_ref, a2_ref, b1_ref, b2_ref, gsum_ref, out_ref, gain_out_ref, *reduce_scratch
    )

    @pl.when(me > 0)
    def _():
        for c in range(CHUNKS):
            chain_copy(c).wait_send()


def reduce_part(
    owners, groups, peers, a_arrive,
    a1_ref, a2_ref, b1_ref, b2_ref, gsum_ref,
    out_ref, gain_ref,
    s1, s2, t1, t2, acc, final, gslot, gacc, gland, *rest,
):
    me = lax.axis_index("tm")
    vid = lax.axis_index("video")
    members = 2 * groups
    chips = owners // 2
    bits = chips.bit_length() - 1
    lands = rest[:bits]
    b_send, b_recv, r_send, r_recv, q_send, q_recv, f_send, f_recv = rest[bits:]
    chip, core = me // 2, lax.rem(me, 2)
    g_me = vid * 2 + core
    pieces, features, pw = acc.shape
    per = pieces // 2
    block = features // chips
    part = block // 2
    scale = 1.0 / (owners * groups)
    length, rows = a1_ref.shape[1], a2_ref.shape[1]

    def b_copy(which, off):
        g = lax.rem(g_me + off, members)
        v, c = lax.div(g, 2), lax.rem(g, 2)
        src, dst = ((b1_ref.at[c, v], s1), (b2_ref.at[c, v], s2), (gsum_ref, gslot))[which]
        return pltpu.make_async_remote_copy(
            src_ref=src, dst_ref=dst.at[g_me], send_sem=b_send.at[which, off], recv_sem=b_recv.at[which, g_me],
            device_id=group_member(groups, g), device_id_type=MESH,
        )

    def b_arrive(which, off):
        g = lax.rem(g_me + members - off, members)
        dst = (s1, s2, gslot)[which]
        return pltpu.make_async_remote_copy(
            src_ref=dst.at[g], dst_ref=dst.at[g], send_sem=b_send.at[which, off], recv_sem=b_recv.at[which, g],
            device_id=group_member(groups, g), device_id_type=MESH,
        )

    for which in (2, 1, 0):
        for off in range(1, members):
            b_copy(which, off).start()
    s1[g_me] = b1_ref[core, vid]
    s2[g_me] = b2_ref[core, vid]
    gslot[g_me] = gsum_ref[...]
    a_arrive()
    for g in range(members):
        t1[:, g * length:(g + 1) * length] = jnp.transpose(a1_ref[g]).astype(BF16)
    for g in range(0, members, 2):
        both = jnp.concatenate([a2_ref[g], a2_ref[g + 1]], axis=0)
        t2[:, g * rows:(g + 2) * rows] = jnp.transpose(both).astype(BF16)

    order = [int(format(i, "b").zfill(bits)[::-1], 2) if bits else 0 for i in range(chips)]

    def products(which):
        slots, left = ((s2, t2), (s1, t1))[which]
        for off in range(1, members):
            b_arrive(1 - which, off).wait_recv()
        for i in range(per):
            right = slots[:, :, i * pw:(i + 1) * pw].reshape(left.shape[1], pw).astype(BF16)
            value = dot(left[...], right, NN)
            for pos in range(chips):
                k = order[pos]
                acc[which * per + i, pos * block:(pos + 1) * block, :] = value[k * block:(k + 1) * block, :]

    starts = []
    lo = 0
    for s in range(bits):
        span = features >> (s + 1)
        bit = lax.rem(lax.div(chip, 2 ** s), 2)
        starts.append((lo + (1 - bit) * span, lo + bit * span, span, peers[s]))
        lo = lo + bit * span

    def r_copy(p, s):
        give, _, span, peer = starts[s]
        return pltpu.make_async_remote_copy(
            src_ref=acc.at[p, pl.ds(pl.multiple_of(give, 8), span)], dst_ref=lands[s].at[p],
            send_sem=r_send.at[p, s], recv_sem=r_recv.at[p, s],
            device_id={"tm": peer * 2 + core}, device_id_type=MESH,
        )

    def g_copy(s):
        return pltpu.make_async_remote_copy(
            src_ref=gacc.at[s], dst_ref=gland.at[s], send_sem=q_send.at[s], recv_sem=q_recv.at[s],
            device_id={"tm": peers[s] * 2 + core}, device_id_type=MESH,
        )

    def r_finish(p, s):
        _, keep, span, _ = starts[s]
        r_copy(p, s).wait_recv()
        at = pl.ds(pl.multiple_of(keep, 8), span)
        acc[p, at, :] = acc[p, at, :] + lands[s][p]

    def f_copy(p):
        theirs = pl.ds(pl.multiple_of(lo + (1 - core) * part, 8), part)
        return pltpu.make_async_remote_copy(
            src_ref=acc.at[p, theirs], dst_ref=final.at[p], send_sem=f_send.at[p], recv_sem=f_recv.at[p],
            device_id={"tm": chip * 2 + 1 - core}, device_id_type=MESH,
        )

    for wave in range(pieces + bits):
        if wave == 0:
            products(0)
        if wave == per:
            products(1)
        for s in reversed(range(bits + 1)):
            p = wave - s
            if 0 <= p < pieces:
                if s > 0:
                    r_finish(p, s - 1)
                if s < bits:
                    r_copy(p, s).start()
                else:
                    f_copy(p).start()
        if wave == 0:
            for off in range(1, members):
                b_arrive(2, off).wait_recv()
            gacc[0] = jnp.sum(gslot[...], axis=0)
        if 0 < wave <= bits:
            g_copy(wave - 1).wait_recv()
            gacc[wave] = gacc[wave - 1] + gland[wave - 1]
        if wave < bits:
            g_copy(wave).start()

    mine_rows = pl.ds(pl.multiple_of(lo + core * part, 8), part)
    for p in range(pieces):
        which, i = p // per, p % per
        cols = slice(i * pw, (i + 1) * pw)
        out_ref[2 * which + core, :, cols] = acc[p, mine_rows, :] * scale
    for p in range(pieces):
        which, i = p // per, p % per
        cols = slice(i * pw, (i + 1) * pw)
        f_copy(p).wait_recv()
        out_ref[2 * which + 1 - core, :, cols] = final[p] * scale

    gain_ref[...] = gacc[bits] * scale
    for s in range(bits):
        g_copy(s).wait_send()
    for which in range(3):
        for off in range(1, members):
            b_copy(which, off).wait_send()
    for p in range(pieces):
        for s in range(bits):
            r_copy(p, s).wait_send()
        f_copy(p).wait_send()


QUAD = 4


def xor_bits(value, bits):
    high, low = lax.div(value, 2), lax.rem(value, 2)
    if bits & 2:
        high = 1 - high
    if bits & 1:
        low = 1 - low
    return high * 2 + low


def encoded(frames_ref, first_time, put):
    length, features = frames_ref.shape
    half_width = features // 2
    index = lax.broadcasted_iota(jnp.int32, (1, half_width), 1).astype(F32)
    frequency = 0.0625 * jnp.exp(-math.log(1000.0) * index / half_width)
    groups_of = length // 8
    outer = first_time + 8 * lax.broadcasted_iota(jnp.int32, (groups_of, half_width), 0)
    inner = lax.broadcasted_iota(jnp.int32, (8, half_width), 0)
    outer, inner = outer.astype(F32) * frequency, inner.astype(F32) * frequency
    so, co, si, ci = jnp.sin(outer), jnp.cos(outer), jnp.sin(inner), jnp.cos(inner)
    for a in range(groups_of):
        s, c = so[a:a + 1], co[a:a + 1]
        r = slice(a * 8, (a + 1) * 8)
        put(r, slice(0, half_width), frames_ref[r, :half_width] + (s * ci + c * si))
        put(r, slice(half_width, features), frames_ref[r, half_width:] + (c * ci - s * si))


def quad_kernel(owners, groups, heads, names, *refs):
    b = types.SimpleNamespace(**dict(zip(names, refs)))
    me = lax.axis_index("tm")
    vid = lax.axis_index("video")
    planes = owners // QUAD
    plane, q = lax.div(me, QUAD), lax.rem(me, QUAD)
    y = lax.div(q, 2)
    members = groups * QUAD
    mine = vid * QUAD + q
    rows, features = b.mem.shape
    length = b.frames.shape[0]
    head = features // heads
    pairs = heads // 2
    pw = 2 * head
    blk = rows // QUAD
    pieces = pairs // groups
    span = features // planes
    part = features // owners
    scale = head ** (-0.5)
    q1, q2, q3 = xor_bits(q, 1), xor_bits(q, 2), xor_bits(q, 3)
    pending = []

    def dev(v, at, qq):
        return {"video": v, "tm": at * QUAD + qq}

    def member(g):
        return dev(lax.div(g, QUAD), plane, lax.rem(g, QUAD))

    def remote(src, dst, ss, rs, to):
        return pltpu.make_async_remote_copy(
            src_ref=src, dst_ref=dst, send_sem=ss, recv_sem=rs, device_id=to, device_id_type=MESH
        )

    def guarded(cond, act):
        if cond is None:
            act()
        else:
            pl.when(cond)(act)

    def send(cond, *copy):
        guarded(cond, lambda: remote(*copy).start())
        pending.append((cond, copy))

    def arrived(dst, rs):
        remote(dst, dst, b.dummy.at[0], rs, dev(vid, plane, q1)).wait_recv()

    weights = [(b.wq_hbm, b.wq), (b.wk_hbm, b.wk), (b.wv_hbm, b.wv), (b.wo_hbm, b.wo)]

    def load(k):
        return pltpu.make_async_copy(weights[k][0], weights[k][1], b.w_sem.at[k])

    for k in (1, 2, 0, 3):
        load(k).start()

    barrier = pltpu.get_barrier_semaphore()
    for off in range(1, members):
        pl.semaphore_signal(barrier, inc=1, device_id=member(lax.rem(mine + off, members)), device_id_type=MESH)
    for off in range(1, planes):
        pl.semaphore_signal(
            barrier, inc=1, device_id=dev(vid, lax.rem(plane + off, planes), q), device_id_type=MESH
        )

    def put_key(r, cols, value):
        b.kin[vid, q, r, cols] = value

    encoded(b.frames, b.offset[0] + me * length, put_key)
    for h in range(heads):
        b.misc[q, h:h + 1, :] = b.bias[h]
    b.misc[q, heads:heads + 1, :] = jnp.zeros((1, length), F32) + b.slot[0].astype(F32)
    for j in range(QUAD):
        b.pack_out[j, :blk] = b.mem[j * blk:(j + 1) * blk, :].astype(F32)
        b.pack_out[j, blk:] = b.cot[j * blk:(j + 1) * blk, :].astype(F32)
    b.pack[q] = b.pack_out[q]

    pl.semaphore_wait(barrier, members - 1 + planes - 1)

    def send_key(cond, slot, sem, to):
        send(cond, b.kin.at[vid, slot], b.kin.at[vid, slot], b.kin_send.at[sem], b.kin_recv.at[vid, slot], to)

    send_key(None, q, 0, dev(vid, plane, q2))
    send_key(None, q, 1, dev(vid, plane, q1))
    for k, other in ((0, q1), (1, q2), (2, q3)):
        to = dev(vid, plane, other)
        send(None, b.misc.at[q], b.misc.at[q], b.misc_send.at[k], b.misc_recv.at[q], to)
        send(None, b.pack_out.at[other], b.pack.at[q], b.pack_send.at[k], b.pack_recv.at[q], to)
    for off in range(1, groups):
        send_key(y == 0, q, 3 * off, dev(lax.rem(vid + off, groups), plane, q))

    low = lax.broadcasted_iota(jnp.int32, (length, pw), 1) < head
    zero = jnp.zeros((length, pw), BF16)

    def project(slot):
        keyin = b.kin[vid, slot].astype(BF16)
        kp = dot(keyin, b.wk[...], NN).astype(BF16)
        vp = dot(keyin, b.wv[...], NN).astype(BF16)
        for p in range(pairs):
            kk = kp[:, p * pw:(p + 1) * pw]
            vv = vp[:, p * pw:(p + 1) * pw]
            b.kbd[slot, p, :length] = jnp.where(low, kk, zero)
            b.kbd[slot, p, length:] = jnp.where(low, zero, kk)
            b.vbd[slot, p, :length] = jnp.where(low, vv, zero)
            b.vbd[slot, p, length:] = jnp.where(low, zero, vv)

    for k in (1, 2, 0, 3):
        load(k).wait()
    project(q)
    b.wot[...] = jnp.transpose(b.wo[...])
    b.wqt[...] = jnp.transpose(b.wq[...])
    arrived(b.kin.at[vid, q1], b.kin_recv.at[vid, q1])
    project(q1)
    arrived(b.kin.at[vid, q2], b.kin_recv.at[vid, q2])
    send_key(None, q2, 2, dev(vid, plane, q1))
    for off in range(1, groups):
        send_key(y == 0, q2, 3 * off + 1, dev(lax.rem(vid + off, groups), plane, q))
    project(q2)
    arrived(b.kin.at[vid, q3], b.kin_recv.at[vid, q3])
    project(q3)
    for other in (q1, q2, q3):
        arrived(b.misc.at[other], b.misc_recv.at[other])
        arrived(b.pack.at[other], b.pack_recv.at[other])

    gain = jnp.concatenate([b.gain[k:k + 1, :] for k in range(b.gain.shape[0])], axis=-1)
    mem = jnp.concatenate([b.pack[j, :blk] for j in range(QUAD)], axis=0)
    inv = lax.rsqrt(jnp.mean(mem * mem, axis=-1, keepdims=True) + NORM_EPSILON)
    unit = mem * inv
    b.unit[...] = unit
    b.inv[...] = jnp.broadcast_to(inv, b.inv.shape)
    normed = (unit * gain).astype(BF16)
    b.normed[...] = normed.astype(F32)
    query = dot(normed, b.wq[...], NN).astype(BF16)
    for p in range(pairs):
        b.qp[p] = query[:, p * pw:(p + 1) * pw].astype(F32)
    for j in reversed(range(QUAD)):
        r = slice(j * blk, (j + 1) * blk)
        scores = [dot(query[r, p * pw:(p + 1) * pw], b.kbd[j, p], NT) for p in range(pairs)]
        for p in range(pairs):
            halves = []
            for k in range(2):
                h = 2 * p + k
                sc = scores[p][:, k * length:(k + 1) * length] * scale + b.misc[j, h:h + 1, :]
                e = jnp.exp(sc - jnp.max(sc, axis=-1, keepdims=True))
                pr = e / jnp.sum(e, axis=-1, keepdims=True)
                b.prob[r, h * length:(h + 1) * length] = pr
                halves.append(pr.astype(BF16))
            both = jnp.concatenate(halves, axis=-1)
            b.half[p, r, :] = both.astype(F32)
            b.attended[r, p * pw:(p + 1) * pw] = dot(both, b.vbd[j, p], NN).astype(BF16).astype(F32)

    def early_refs(role, v):
        at = pl.ds(v * pieces, pieces)
        return (
            (b.qp.at[at], b.narrow), (b.half.at[at], b.wide), (b.attended, b.early), (b.normed, b.early),
        )[role]

    for role in range(QUAD):
        for off in range(groups):
            v = lax.rem(vid + off, groups)
            src, dst = early_refs(role, v)
            send(
                q != role if off == 0 else None, src, dst.at[mine],
                b.early_send.at[role, off], b.early_recv.at[mine], dev(v, plane, role),
            )

        @pl.when(q == role)
        def _():
            src, dst = early_refs(role, vid)
            dst[mine] = src[...]

    def early_work():
        for role in range(QUAD):
            @pl.when(q == role)
            def _():
                dst = early_refs(role, vid)[1]
                for off in range(1, members):
                    g = lax.rem(mine + off, members)
                    arrived(dst.at[g], b.early_recv.at[g])

        @pl.when(y == 0)
        def _():
            for off in range(1, groups):
                v = lax.rem(vid + off, groups)
                for k, slot in ((0, q), (1, q2)):
                    arrived(b.kin.at[v, slot], b.kin_recv.at[v, slot])
                    forward(off, k, v, slot).start()
            for off in range(1, groups):
                v = lax.rem(vid + off, groups)
                for slot in (q1, q3):
                    arrived(b.kin.at[v, slot], b.kin_recv.at[v, slot])
            for g in range(members):
                b.left[:, g * length:(g + 1) * length] = jnp.transpose(b.kin[g // QUAD, g % QUAD]).astype(BF16)

        @pl.when(y == 1)
        def _():
            for g in range(0, members, 2):
                both = jnp.concatenate([b.early[g], b.early[g + 1]], axis=0)
                b.left[:, g * rows:(g + 2) * rows] = jnp.transpose(both).astype(BF16)

    def forward(off, k, v, slot):
        return remote(
            b.kin.at[v, slot], b.kin.at[v, slot], b.fwd_send.at[off, k], b.kin_recv.at[v, slot],
            dev(vid, plane, q1),
        )

    before = planes // 2

    @pl.when(plane < before)
    def _():
        early_work()

    @pl.when(plane == planes - 1)
    def _():
        b.incoming[...] = jnp.zeros_like(b.incoming)

    @pl.when(plane < planes - 1)
    def _():
        arrived(b.incoming, b.chain_recv.at[0])

    gain_total = jnp.zeros((1, features), F32)
    carried = b.incoming[...]
    for j in reversed(range(QUAD)):
        r = slice(j * blk, (j + 1) * blk)
        grad_in = carried + b.pack[j, blk:]
        live = jnp.concatenate([b.misc[j, heads:heads + 1, :]] * (features // length), axis=-1)
        og = (live * grad_in).astype(BF16)
        att = dot(og, b.wot[...], NN).astype(BF16)
        prob_grads = [dot(att[:, p * pw:(p + 1) * pw], b.vbd[j, p], NT) for p in range(pairs)]
        query_grads = []
        score_grads = []
        for p in range(pairs):
            halves = []
            for k in range(2):
                h = 2 * p + k
                pg = prob_grads[p][:, k * length:(k + 1) * length]
                pr = b.prob[r, h * length:(h + 1) * length]
                inner = jnp.sum(pr * pg, axis=-1, keepdims=True)
                halves.append((pr * (pg - inner) * scale).astype(BF16))
            both = jnp.concatenate(halves, axis=-1)
            score_grads.append(both)
            query_grads.append(dot(both, b.kbd[j, p], NN).astype(BF16))
        qg = jnp.concatenate(query_grads, axis=-1)
        ng = dot(qg, b.wqt[...], NN)
        un = b.unit[r, :]
        sc = ng * gain
        carried = grad_in + b.inv[r, 0:1] * (sc - un * jnp.mean(sc * un, axis=-1, keepdims=True))
        b.passed[j] = carried
        if j == 0:
            send(
                plane > 0, b.passed.at[0], b.incoming, b.chain_send.at[0], b.chain_recv.at[0],
                dev(vid, jnp.maximum(plane - 1, 0), q),
            )
        gain_total = gain_total + jnp.sum(ng * un, axis=0, keepdims=True)
        for p in range(pairs):
            cols = slice(p * pw, (p + 1) * pw)
            b.sg[p, r, :] = score_grads[p].astype(F32)
            b.att[p, r, :] = att[:, cols].astype(F32)
            b.og[p, r, :] = og[:, cols].astype(F32)
            b.qg[p, r, :] = qg[:, cols].astype(F32)

    b.gsum[mine] = gain_total
    for off in range(1, members):
        g = lax.rem(mine + off, members)
        send(None, b.gsum.at[mine], b.gsum.at[mine], b.gsum_send.at[off], b.gsum_recv.at[mine], member(g))

    def late_refs(role, v, i):
        at = v * pieces + i
        return (
            (b.sg.at[at], b.wide), (b.att.at[at], b.narrow), (b.og.at[at], b.narrow), (b.qg.at[at], b.narrow),
        )[role]

    for i in range(pieces):
        for off in reversed(range(groups)):
            v = lax.rem(vid + off, groups)
            for role in range(QUAD):
                src, dst = late_refs(role, v, i)
                send(
                    q != role if off == 0 else None, src, dst.at[mine, i],
                    b.late_send.at[i, role, off], b.late_recv.at[mine, i], dev(v, plane, role),
                )
        for role in range(QUAD):
            @pl.when(q == role)
            def _():
                src, dst = late_refs(role, vid, i)
                dst[mine, i] = src[...]

    for j in range(QUAD):
        send(
            q != j, b.passed.at[j], b.returned.at[q], b.ret_send.at[j], b.ret_recv.at[q], dev(vid, plane, j)
        )

    @pl.when(plane >= before)
    def _():
        early_work()

    lowr = lax.broadcasted_iota(jnp.int32, (rows, pw), 1) < head
    zr = jnp.zeros((rows, pw), BF16)

    def product(i):
        for role in range(QUAD):
            @pl.when(q == role)
            def _():
                dst = late_refs(role, vid, i)[1]
                for off in range(1, members):
                    g = lax.rem(mine + off, members)
                    arrived(dst.at[g, i], b.late_recv.at[g, i])

        @pl.when(y == 0)
        def _():
            for v in range(groups):
                for j in range(QUAD):
                    r = slice(j * blk, (j + 1) * blk)
                    wide = jnp.concatenate([b.wide[v * QUAD + k, i, r, :] for k in range(QUAD)], axis=0).astype(BF16)
                    right = jnp.concatenate([b.narrow[v * QUAD + k, i, r, :] for k in range(QUAD)], axis=0).astype(BF16)
                    wide = jnp.concatenate([wide[:, :length], wide[:, length:]], axis=0)
                    right = jnp.concatenate([jnp.where(lowr, right, zr), jnp.where(lowr, zr, right)], axis=0)
                    at = (v * QUAD + j) * length
                    b.right[at:at + length, :] = dot(wide, right, TN).astype(BF16)
            b.acc[i] = dot(b.left[...], b.right[...], NN)

        @pl.when(y == 1)
        def _():
            right = jnp.concatenate([b.narrow[g, i] for g in range(members)], axis=0).astype(BF16)
            b.acc[i] = dot(b.left[:, :members * rows], right, NN)

    def block(at):
        return pl.ds(pl.multiple_of(at * span, 8), span)

    def flow(i, k, up):
        to = plane + k if up else plane - k
        ok = to < planes if up else to >= 0
        fed = plane > 0 if up else plane < planes - 1
        land, ss, rs = (b.up, b.up_send, b.up_recv) if up else (b.down, b.down_send, b.down_recv)
        to = jnp.clip(to, 0, planes - 1)
        at = block(to)
        step = jnp.clip(plane + 1 if up else plane - 1, 0, planes - 1)

        @pl.when(jnp.logical_and(ok, fed))
        def _():
            arrived(land.at[i, at], rs.at[i, to])
            b.acc[i, at, :] = b.acc[i, at, :] + land[i, at, :]

        return ok, (b.acc.at[i, at], land.at[i, at], ss.at[i, to], rs.at[i, to], dev(vid, step, q))

    def flow_all(i, up):
        for k in reversed(range(1, planes)):
            ok, copy = flow(i, k, up)
            pl.when(ok)(lambda: remote(*copy).start())

    mean = 1.0 / (owners * groups)

    def settle(i):
        at = block(plane)

        @pl.when(plane < planes - 1)
        def _():
            arrived(b.down.at[i, at], b.down_recv.at[i, plane])
            b.acc[i, at, :] = b.acc[i, at, :] + b.down[i, at, :]

        @pl.when(plane > 0)
        def _():
            arrived(b.up.at[i, at], b.up_recv.at[i, plane])
            b.acc[i, at, :] = b.acc[i, at, :] + b.up[i, at, :]

        b.final[i] = b.acc[i, at, :] * mean
        for k, other in ((0, q1), (1, q2), (2, q3)):
            to = dev(vid, plane, other)
            rows_of = pl.ds(pl.multiple_of(other * part, 8), part)
            send(None, b.final.at[i, rows_of], b.fin_land.at[q, i], b.fin_send.at[k, i], b.fin_recv.at[q, i], to)
        b.out[q, :, i * pw:(i + 1) * pw] = b.final[i, pl.ds(pl.multiple_of(q * part, 8), part), :]

    for off in range(1, members):
        g = lax.rem(mine + off, members)
        arrived(b.gsum.at[g], b.gsum_recv.at[g])
    b.gplane[plane] = jnp.sum(b.gsum[...], axis=0)
    for off in range(1, planes):
        to = dev(vid, lax.rem(plane + off, planes), q)
        send(None, b.gplane.at[plane], b.gplane.at[plane], b.gp_send.at[off], b.gp_recv.at[plane], to)

    for i in range(pieces):
        product(i)
        flow_all(i, False)

        @pl.when(plane == 0)
        def _():
            flow_all(i, True)

    for i in range(pieces):
        @pl.when(plane > 0)
        def _():
            flow_all(i, True)

        settle(i)

    b.grad[pl.ds(pl.multiple_of(q * blk, 8), blk), :] = b.passed[q]
    for other in (q1, q2, q3):
        arrived(b.returned.at[other], b.ret_recv.at[other])
        b.grad[pl.ds(pl.multiple_of(other * blk, 8), blk), :] = b.returned[other]
    for off in range(1, planes):
        at = lax.rem(plane + off, planes)
        arrived(b.gplane.at[at], b.gp_recv.at[at])
    total = jnp.sum(b.gplane[...], axis=0) * mean
    for k in range(b.gain_out.shape[0]):
        b.gain_out[k:k + 1, :] = total[:, k * 128:(k + 1) * 128]
    for i in range(pieces):
        for other in (q1, q2, q3):
            arrived(b.fin_land.at[other, i], b.fin_recv.at[other, i])
            b.out[other, :, i * pw:(i + 1) * pw] = b.fin_land[other, i]

    for cond, copy in pending:
        guarded(cond, lambda: remote(*copy).wait_send())

    @pl.when(y == 0)
    def _():
        for off in range(1, groups):
            v = lax.rem(vid + off, groups)
            for k, slot in ((0, q), (1, q2)):
                forward(off, k, v, slot).wait_send()

    for i in range(pieces):
        for up in (False, True):
            for k in range(1, planes):
                to = plane + k if up else plane - k
                ok = to < planes if up else to >= 0
                to = jnp.clip(to, 0, planes - 1)
                land, ss, rs = (b.up, b.up_send, b.up_recv) if up else (b.down, b.down_send, b.down_recv)

                @pl.when(ok)
                def _():
                    remote(
                        b.acc.at[i, block(to)], land.at[i, block(to)], ss.at[i, to], rs.at[i, to],
                        dev(vid, jnp.clip(plane + 1 if up else plane - 1, 0, planes - 1), q),
                    ).wait_send()


def quad_fits(owners, groups, heads, rows, length, features):
    pw = 2 * features // heads
    return (
        owners % QUAD == 0 and rows % (16 * QUAD) == 0 and length % 128 == 0 and pw == 128 and length == pw
        and (heads // 2) % groups == 0 and features % (8 * owners) == 0 and features % 256 == 0
    )


def quad_call(memory, frames, mem_cot, slot_used, key_bias, start_offset, norm_gain, w_query, w_key, w_value, w_out):
    owners = lax.axis_size("tm")
    groups = lax.axis_size("video")
    rows, features = memory.shape[3:]
    length = frames.shape[3]
    heads = key_bias.shape[3]
    planes = owners // QUAD
    members = groups * QUAD
    pairs = heads // 2
    pieces = pairs // groups
    pw = 2 * features // heads
    blk = rows // QUAD
    part = features // owners
    width = features // groups
    vm, sds = pltpu.VMEM, jax.ShapeDtypeStruct
    sem = lambda *shape: pltpu.SemaphoreType.DMA(shape)
    scratch = dict(
        kin=vm((groups, QUAD, length, features), F32), misc=vm((QUAD, 16, length), F32),
        pack_out=vm((QUAD, 2 * blk, features), F32), pack=vm((QUAD, 2 * blk, features), F32),
        wq=vm((features, features), BF16), wk=vm((features, features), BF16),
        wv=vm((features, features), BF16), wo=vm((features, features), BF16),
        wot=vm((features, features), BF16), wqt=vm((features, features), BF16),
        kbd=vm((QUAD, pairs, 2 * length, pw), BF16), vbd=vm((QUAD, pairs, 2 * length, pw), BF16),
        unit=vm((rows, features), F32), inv=vm((rows, 128), F32), prob=vm((rows, heads * length), F32),
        normed=vm((rows, features), F32), attended=vm((rows, features), F32),
        qp=vm((pairs, rows, pw), F32), att=vm((pairs, rows, pw), F32),
        og=vm((pairs, rows, pw), F32), qg=vm((pairs, rows, pw), F32),
        half=vm((pairs, rows, 2 * length), F32), sg=vm((pairs, rows, 2 * length), F32),
        wide=vm((members, pieces, rows, 2 * length), F32), narrow=vm((members, pieces, rows, pw), F32),
        early=vm((members, rows, features), F32), left=vm((features, members * length), BF16),
        right=vm((members * length, pw), BF16), acc=vm((pieces, features, pw), F32),
        up=vm((pieces, features, pw), F32), down=vm((pieces, features, pw), F32),
        final=vm((pieces, features // planes, pw), F32), fin_land=vm((QUAD, pieces, part, pw), F32),
        incoming=vm((blk, features), F32), passed=vm((QUAD, blk, features), F32),
        returned=vm((QUAD, blk, features), F32),
        gsum=vm((members, 1, features), F32), gplane=vm((planes, 1, features), F32),
        dummy=sem(1), w_sem=sem(4), kin_send=sem(3 * groups), kin_recv=sem(groups, QUAD),
        misc_send=sem(3), misc_recv=sem(QUAD), pack_send=sem(3), pack_recv=sem(QUAD),
        early_send=sem(QUAD, groups), early_recv=sem(members), fwd_send=sem(groups, 2),
        chain_send=sem(1), chain_recv=sem(1), gsum_send=sem(members), gsum_recv=sem(members),
        late_send=sem(pieces, QUAD, groups), late_recv=sem(members, pieces),
        ret_send=sem(QUAD), ret_recv=sem(QUAD), gp_send=sem(planes), gp_recv=sem(planes),
        up_send=sem(pieces, planes), up_recv=sem(pieces, planes),
        down_send=sem(pieces, planes), down_recv=sem(pieces, planes),
        fin_send=sem(3, pieces), fin_recv=sem(QUAD, pieces),
    )
    names = ["slot", "offset", "mem", "frames", "cot", "bias", "gain", "wq_hbm", "wk_hbm", "wv_hbm", "wo_hbm"]
    names = names + ["grad", "out", "gain_out"] + list(scratch)
    vmem = pl.BlockSpec(memory_space=pltpu.VMEM)
    smem = pl.BlockSpec(memory_space=pltpu.SMEM)
    hbm = pl.BlockSpec(memory_space=pl.ANY)
    grad, weights, gain = pl.pallas_call(
        functools.partial(quad_kernel, owners, groups, heads, tuple(names)),
        out_shape=(
            sds((rows, features), F32), sds((QUAD, part, width), F32), sds((features // 128, 128), F32),
        ),
        in_specs=[smem, smem] + [vmem] * 5 + [hbm] * 4,
        out_specs=(vmem,) * 3,
        scratch_shapes=list(scratch.values()),
        compiler_params=pltpu.CompilerParams(collective_id=0, has_side_effects=True, vmem_limit_bytes=58 * 1024 * 1024),
        name="quad",
    )(
        slot_used[0, 0], start_offset[0], memory[0, 0, 0], frames[0, 0, 0], mem_cot[0, 0, 0],
        key_bias[0, 0, 0][:, None, :], norm_gain.reshape(features // 128, 128), w_query, w_key, w_value, w_out,
    )
    return (grad[None, None, None], weights[3], weights[0], weights[1], weights[2], gain.reshape(features))


def on_device(
    memory, frames, mem_cot, slot_used, key_bias, start_offset, norm_gain, w_query, w_key, w_value, w_out
):
    owners = lax.axis_size("tm")
    groups = lax.axis_size("video")
    position = lax.axis_index("tm")
    streams, rows, features = memory.shape[2:]
    length = frames.shape[3]
    heads = key_bias.shape[3]
    if quad_fits(owners, groups, heads, rows, length, features):
        return quad_call(
            memory, frames, mem_cot, slot_used, key_bias, start_offset, norm_gain, w_query, w_key, w_value, w_out
        )
    members = 2 * groups
    chips = owners // 2
    bits = chips.bit_length() - 1
    width = features // groups
    keyin = key_rows(frames[0, 0, 0], start_offset[0, 0], position)
    vmem = pl.BlockSpec(memory_space=pltpu.VMEM)
    smem = pl.BlockSpec(memory_space=pltpu.SMEM)
    sds = jax.ShapeDtypeStruct
    pw = 128 if width % 128 == 0 else width
    pieces = 2 * (width // pw)
    dma = pltpu.SemaphoreType.DMA
    grad, weights, gain = pl.pallas_call(
        functools.partial(whole_kernel, owners, groups, heads),
        out_shape=(
            sds((rows, features), F32),
            sds((4, features // owners, width), F32),
            sds((1, features), F32),
        ),
        in_specs=[smem] + [vmem] * 9,
        out_specs=(vmem,) * 3,
        scratch_shapes=[
            pltpu.VMEM((members, length, features), F32),
            pltpu.VMEM((members, rows, features), F32),
            pltpu.VMEM((2, groups, length, width), F32),
            pltpu.VMEM((2, groups, rows, width), F32),
            pltpu.VMEM((1, features), F32),
            pltpu.VMEM((rows, features), F32),
            pltpu.VMEM((2, rows, features), F32),
            pltpu.VMEM((rows, heads * length), F32),
            pltpu.VMEM((rows, heads * length), BF16),
            pltpu.VMEM((heads // 2, 2 * length, 2 * features // heads), BF16),
            pltpu.VMEM((heads // 2, 2 * length, 2 * features // heads), BF16),
            pltpu.VMEM((rows, features), BF16),
            pltpu.VMEM((rows, features), BF16),
            pltpu.VMEM((rows, heads * length), BF16),
            pltpu.VMEM((rows, features), BF16),
            pltpu.VMEM((rows, features), BF16),
            pltpu.VMEM((rows, features), F32),
            pltpu.VMEM((rows, 128), F32),
            pltpu.VMEM((features, features), BF16),
            pltpu.VMEM((features, features), BF16),
            dma((CHUNKS,)), dma((CHUNKS,)), dma((2, members)), dma((2, members)),
            pltpu.VMEM((members, length, width), F32),
            pltpu.VMEM((members, rows, width), F32),
            pltpu.VMEM((features, members * length), BF16),
            pltpu.VMEM((features, members * rows), BF16),
            pltpu.VMEM((pieces, features, pw), F32),
            pltpu.VMEM((pieces, features // owners, pw), F32),
            pltpu.VMEM((members, 1, features), F32),
            pltpu.VMEM((bits + 1, 1, features), F32),
            pltpu.VMEM((max(bits, 1), 1, features), F32),
        ]
        + [pltpu.VMEM((pieces, features >> (s + 1), pw), F32) for s in range(bits)]
        + [
            dma((3, members)), dma((3, members)), dma((pieces, bits)), dma((pieces, bits)),
            dma((bits,)), dma((bits,)), dma((pieces,)), dma((pieces,)),
        ],
        compiler_params=pltpu.CompilerParams(collective_id=0, has_side_effects=True, vmem_limit_bytes=58 * 1024 * 1024),
        name="whole",
    )(
        slot_used[0, 0], memory[0, 0, 0], keyin, mem_cot[0, 0, 0], key_bias[0, 0, 0],
        norm_gain[None, :], w_query, w_key, w_value, w_out,
    )
    return (grad[None, None, None], weights[1], weights[2], weights[3], weights[0], gain[0])


def solution(mesh):
    return jax.shard_map(
        on_device,
        mesh=mesh,
        in_specs=(
            P("video", "tm", None, None, None),
            P("video", "tm", None, None, None),
            P("video", "tm", None, None, None),
            P("video", "tm", None),
            P("video", "tm", None, None, None),
            P("video", None),
            P(),
            P(),
            P(),
            P(),
            P(),
        ),
        out_specs=(
            P("video", "tm", None, None, None),
            P("tm", "video"),
            P("tm", "video"),
            P("tm", "video"),
            P("tm", "video"),
            P(),
        ),
        check_vma=False,
    )
```

```python
import functools
import math
import types

import jax
import jax.numpy as jnp
from jax import lax
from jax.experimental import pallas as pl
from jax.experimental.pallas import tpu as pltpu
from jax.sharding import PartitionSpec as P

NORM_EPSILON = 1e-06
MESH = pl.DeviceIdType.MESH
F32 = jnp.float32
BF16 = jnp.bfloat16
NN = (((1,), (0,)), ((), ()))
NT = (((1,), (1,)), ((), ()))
TN = (((0,), (0,)), ((), ()))
CHUNKS = 4


def dot(left, right, form):
    return lax.dot_general(left, right, form, preferred_element_type=F32)


def key_rows(frame_rows, offset, position):
    length, features = frame_rows.shape
    within = jnp.arange(length, dtype=jnp.int32)
    frame_time = (offset + position * length + within).astype(F32)
    half_width = features // 2
    frequency = 0.0625 * jnp.exp(-math.log(1000.0) * jnp.arange(half_width, dtype=F32) / half_width)
    phases = frame_time[:, None] * frequency
    return frame_rows + jnp.concatenate([jnp.sin(phases), jnp.cos(phases)], axis=-1)


def group_member(groups, g):
    me = lax.axis_index("tm")
    return {"video": lax.div(g, 2), "tm": (me // 2) * 2 + lax.rem(g, 2)}


def whole_kernel(
    owners, groups, heads,
    slot_ref, mem_ref, keyin_ref, cot_ref, bias_ref, gain_ref, wq_ref, wk_ref, wv_ref, wo_ref,
    grad_ref, out_ref, gain_out_ref,
    a1_ref, a2_ref, b1_ref, b2_ref, gsum_ref,
    incoming, mine, prob, half, kbd, vbd, qp, att_all, sg_all, og_all, qg_all, unit_ref, inv_ref, wot, wqt,
    chain_send, chain_recv, a_send, a_recv,
    *reduce_scratch,
):
    me = lax.axis_index("tm")
    vid = lax.axis_index("video")
    chips = owners // 2
    bits = chips.bit_length() - 1
    chip, core = me // 2, lax.rem(me, 2)
    peers = [chip + (1 - 2 * lax.rem(lax.div(chip, 2 ** b), 2)) * 2 ** b for b in range(bits)]
    rows, features = mem_ref.shape
    length = keyin_ref.shape[0]
    head = features // heads
    pairs = heads // 2
    pw = 2 * head
    members = 2 * groups
    g_me = vid * 2 + lax.rem(me, 2)
    scale = head ** (-0.5)

    barrier = pltpu.get_barrier_semaphore()
    for off in range(1, members):
        pl.semaphore_signal(barrier, inc=1, device_id=group_member(groups, lax.rem(g_me + off, members)), device_id_type=MESH)

    for peer in peers:
        pl.semaphore_signal(barrier, inc=1, device_id={"tm": peer * 2 + core}, device_id_type=MESH)

    @pl.when(me > 0)
    def _():
        pl.semaphore_signal(barrier, inc=1, device_id={"tm": me - 1}, device_id_type=MESH)

    @pl.when(me < owners - 1)
    def _():
        pl.semaphore_signal(barrier, inc=1, device_id={"tm": me + 1}, device_id_type=MESH)

    ends = jnp.where(me > 0, 1, 0) + jnp.where(me < owners - 1, 1, 0)
    pl.semaphore_wait(barrier, members - 1 + bits + ends)

    def a_copy(which, src, dst, off):
        g = lax.rem(g_me + off, members)
        return pltpu.make_async_remote_copy(
            src_ref=src, dst_ref=dst.at[g_me], send_sem=a_send.at[which, off], recv_sem=a_recv.at[which, g_me],
            device_id=group_member(groups, g), device_id_type=MESH,
        )

    for off in range(1, members):
        a_copy(0, keyin_ref, a1_ref, off).start()
    a1_ref[g_me] = keyin_ref[...]

    mem = mem_ref[...].astype(F32)
    inv = lax.rsqrt(jnp.mean(mem * mem, axis=-1, keepdims=True) + NORM_EPSILON)
    unit = mem * inv
    unit_ref[...] = unit
    inv_ref[...] = jnp.broadcast_to(inv, inv_ref.shape)
    normed = (unit * gain_ref[...]).astype(BF16)
    mine[1] = normed.astype(F32)
    keyin = keyin_ref[...].astype(BF16)
    query = dot(normed, wq_ref[...], NN).astype(BF16)
    qp[...] = query
    kp = dot(keyin, wk_ref[...], NN).astype(BF16)
    vp = dot(keyin, wv_ref[...], NN).astype(BF16)
    low = lax.broadcasted_iota(jnp.int32, (length, pw), 1) < head
    zero = jnp.zeros((length, pw), BF16)
    for p in range(pairs):
        kk = kp[:, p * pw:(p + 1) * pw]
        vv = vp[:, p * pw:(p + 1) * pw]
        kbd[p, :length] = jnp.where(low, kk, zero)
        kbd[p, length:] = jnp.where(low, zero, kk)
        vbd[p, :length] = jnp.where(low, vv, zero)
        vbd[p, length:] = jnp.where(low, zero, vv)
    wot[...] = jnp.transpose(wo_ref[...])
    wqt[...] = jnp.transpose(wq_ref[...])
    scores = [dot(query[:, p * pw:(p + 1) * pw], kbd[p], NT) for p in range(pairs)]
    for p in range(pairs):
        halves = []
        for q in range(2):
            h = 2 * p + q
            s = scores[p][:, q * length:(q + 1) * length] * scale + bias_ref[h:h + 1, :]
            e = jnp.exp(s - jnp.max(s, axis=-1, keepdims=True))
            pr = e / jnp.sum(e, axis=-1, keepdims=True)
            prob[:, h * length:(h + 1) * length] = pr
            halves.append(pr.astype(BF16))
        both = jnp.concatenate(halves, axis=-1)
        half[:, p * 2 * length:(p + 1) * 2 * length] = both
        mine[0, :, p * pw:(p + 1) * pw] = dot(both, vbd[p], NN).astype(BF16).astype(F32)

    for off in range(1, members):
        g = lax.rem(g_me + off, members)
        a_copy(1, mine.at[lax.rem(g, 2)], a2_ref, off).start()
    a2_ref[g_me] = mine[lax.rem(me, 2)]

    live = slot_ref[0].astype(F32)
    step = rows // CHUNKS

    def chain_copy(c):
        return pltpu.make_async_remote_copy(
            src_ref=grad_ref.at[pl.ds(c * step, step)], dst_ref=incoming.at[pl.ds(c * step, step)],
            send_sem=chain_send.at[c], recv_sem=chain_recv.at[c],
            device_id={"tm": jnp.maximum(me - 1, 0)}, device_id_type=MESH,
        )

    @pl.when(me == owners - 1)
    def _():
        incoming[...] = jnp.zeros_like(incoming)

    gain_total = jnp.zeros((1, features), F32)
    for c in range(CHUNKS):
        r = slice(c * step, (c + 1) * step)

        @pl.when(me < owners - 1)
        def _():
            chain_copy(c).wait_recv()

        grad_in = incoming[r, :] + cot_ref[r, :].astype(F32)
        og = (live * grad_in).astype(BF16)
        att = dot(og, wot[...], NN).astype(BF16)
        prob_grads = [dot(att[:, p * pw:(p + 1) * pw], vbd[p], NT) for p in range(pairs)]
        query_grads = []
        score_grads = []
        for p in range(pairs):
            for q in range(2):
                h = 2 * p + q
                pg = prob_grads[p][:, q * length:(q + 1) * length]
                pr = prob[r, h * length:(h + 1) * length]
                inner = jnp.sum(pr * pg, axis=-1, keepdims=True)
                score_grads.append((pr * (pg - inner) * scale).astype(BF16))
            query_grads.append(dot(jnp.concatenate(score_grads[-2:], axis=-1), kbd[p], NN).astype(BF16))
        qg = jnp.concatenate(query_grads, axis=-1)
        ng = dot(qg, wqt[...], NN)
        un = unit_ref[r, :]
        gain_total = gain_total + jnp.sum(ng * un, axis=0, keepdims=True)
        sc = ng * gain_ref[...]
        grad_ref[r, :] = grad_in + inv_ref[r, 0:1] * (sc - un * jnp.mean(sc * un, axis=-1, keepdims=True))

        @pl.when(me > 0)
        def _():
            chain_copy(c).start()

        og_all[r, :] = og
        att_all[r, :] = att
        qg_all[r, :] = qg
        for h in range(heads):
            sg_all[r, h * length:(h + 1) * length] = score_grads[h]

    gsum_ref[...] = gain_total

    width = features // groups
    lowr = lax.broadcasted_iota(jnp.int32, (rows, pw), 1) < head
    zr = jnp.zeros((rows, pw), BF16)

    def put(out, which, p, value):
        for v in range(groups):
            lo, hi = max(p * pw, v * width), min((p + 1) * pw, (v + 1) * width)
            if lo < hi:
                out[which, v, :, lo - v * width:hi - v * width] = value[:, lo - p * pw:hi - p * pw]

    for p in range(pairs):
        for which, (left_ref, right_ref) in enumerate(((sg_all, qp), (half, att_all))):
            right = right_ref[:, p * pw:(p + 1) * pw]
            right = jnp.concatenate([jnp.where(lowr, right, zr), jnp.where(lowr, zr, right)], axis=0)
            base = 2 * p * length
            left = jnp.concatenate([left_ref[:, base:base + length], left_ref[:, base + length:base + 2 * length]], axis=0)
            put(b1_ref, which, p, dot(left, right, TN).astype(BF16).astype(F32))
        put(b2_ref, 0, p, og_all[:, p * pw:(p + 1) * pw].astype(F32))
        put(b2_ref, 1, p, qg_all[:, p * pw:(p + 1) * pw].astype(F32))

    def a_arrive():
        for off in range(1, members):
            g = lax.rem(g_me + members - off, members)
            for which, dst in ((0, a1_ref), (1, a2_ref)):
                a_copy(which, dst.at[g_me], dst, off).wait_send()
                pltpu.make_async_remote_copy(
                    src_ref=dst.at[g], dst_ref=dst.at[g], send_sem=a_send.at[which, off], recv_sem=a_recv.at[which, g],
                    device_id=group_member(groups, g), device_id_type=MESH,
                ).wait_recv()

    reduce_part(
        owners, groups, peers, a_arrive, a1_ref, a2_ref, b1_ref, b2_ref, gsum_ref, out_ref, gain_out_ref, *reduce_scratch
    )

    @pl.when(me > 0)
    def _():
        for c in range(CHUNKS):
            chain_copy(c).wait_send()


def reduce_part(
    owners, groups, peers, a_arrive,
    a1_ref, a2_ref, b1_ref, b2_ref, gsum_ref,
    out_ref, gain_ref,
    s1, s2, t1, t2, acc, final, gslot, gacc, gland, *rest,
):
    me = lax.axis_index("tm")
    vid = lax.axis_index("video")
    members = 2 * groups
    chips = owners // 2
    bits = chips.bit_length() - 1
    lands = rest[:bits]
    b_send, b_recv, r_send, r_recv, q_send, q_recv, f_send, f_recv = rest[bits:]
    chip, core = me // 2, lax.rem(me, 2)
    g_me = vid * 2 + core
    pieces, features, pw = acc.shape
    per = pieces // 2
    block = features // chips
    part = block // 2
    scale = 1.0 / (owners * groups)
    length, rows = a1_ref.shape[1], a2_ref.shape[1]

    def b_copy(which, off):
        g = lax.rem(g_me + off, members)
        v, c = lax.div(g, 2), lax.rem(g, 2)
        src, dst = ((b1_ref.at[c, v], s1), (b2_ref.at[c, v], s2), (gsum_ref, gslot))[which]
        return pltpu.make_async_remote_copy(
            src_ref=src, dst_ref=dst.at[g_me], send_sem=b_send.at[which, off], recv_sem=b_recv.at[which, g_me],
            device_id=group_member(groups, g), device_id_type=MESH,
        )

    def b_arrive(which, off):
        g = lax.rem(g_me + members - off, members)
        dst = (s1, s2, gslot)[which]
        return pltpu.make_async_remote_copy(
            src_ref=dst.at[g], dst_ref=dst.at[g], send_sem=b_send.at[which, off], recv_sem=b_recv.at[which, g],
            device_id=group_member(groups, g), device_id_type=MESH,
        )

    for which in (2, 1, 0):
        for off in range(1, members):
            b_copy(which, off).start()
    s1[g_me] = b1_ref[core, vid]
    s2[g_me] = b2_ref[core, vid]
    gslot[g_me] = gsum_ref[...]
    a_arrive()
    for g in range(members):
        t1[:, g * length:(g + 1) * length] = jnp.transpose(a1_ref[g]).astype(BF16)
    for g in range(0, members, 2):
        both = jnp.concatenate([a2_ref[g], a2_ref[g + 1]], axis=0)
        t2[:, g * rows:(g + 2) * rows] = jnp.transpose(both).astype(BF16)

    order = [int(format(i, "b").zfill(bits)[::-1], 2) if bits else 0 for i in range(chips)]

    def products(which):
        slots, left = ((s2, t2), (s1, t1))[which]
        for off in range(1, members):
            b_arrive(1 - which, off).wait_recv()
        for i in range(per):
            right = slots[:, :, i * pw:(i + 1) * pw].reshape(left.shape[1], pw).astype(BF16)
            value = dot(left[...], right, NN)
            for pos in range(chips):
                k = order[pos]
                acc[which * per + i, pos * block:(pos + 1) * block, :] = value[k * block:(k + 1) * block, :]

    starts = []
    lo = 0
    for s in range(bits):
        span = features >> (s + 1)
        bit = lax.rem(lax.div(chip, 2 ** s), 2)
        starts.append((lo + (1 - bit) * span, lo + bit * span, span, peers[s]))
        lo = lo + bit * span

    def r_copy(p, s):
        give, _, span, peer = starts[s]
        return pltpu.make_async_remote_copy(
            src_ref=acc.at[p, pl.ds(pl.multiple_of(give, 8), span)], dst_ref=lands[s].at[p],
            send_sem=r_send.at[p, s], recv_sem=r_recv.at[p, s],
            device_id={"tm": peer * 2 + core}, device_id_type=MESH,
        )

    def g_copy(s):
        return pltpu.make_async_remote_copy(
            src_ref=gacc.at[s], dst_ref=gland.at[s], send_sem=q_send.at[s], recv_sem=q_recv.at[s],
            device_id={"tm": peers[s] * 2 + core}, device_id_type=MESH,
        )

    def r_finish(p, s):
        _, keep, span, _ = starts[s]
        r_copy(p, s).wait_recv()
        at = pl.ds(pl.multiple_of(keep, 8), span)
        acc[p, at, :] = acc[p, at, :] + lands[s][p]

    def f_copy(p):
        theirs = pl.ds(pl.multiple_of(lo + (1 - core) * part, 8), part)
        return pltpu.make_async_remote_copy(
            src_ref=acc.at[p, theirs], dst_ref=final.at[p], send_sem=f_send.at[p], recv_sem=f_recv.at[p],
            device_id={"tm": chip * 2 + 1 - core}, device_id_type=MESH,
        )

    for wave in range(pieces + bits):
        if wave == 0:
            products(0)
        if wave == per:
            products(1)
        for s in reversed(range(bits + 1)):
            p = wave - s
            if 0 <= p < pieces:
                if s > 0:
                    r_finish(p, s - 1)
                if s < bits:
                    r_copy(p, s).start()
                else:
                    f_copy(p).start()
        if wave == 0:
            for off in range(1, members):
                b_arrive(2, off).wait_recv()
            gacc[0] = jnp.sum(gslot[...], axis=0)
        if 0 < wave <= bits:
            g_copy(wave - 1).wait_recv()
            gacc[wave] = gacc[wave - 1] + gland[wave - 1]
        if wave < bits:
            g_copy(wave).start()

    mine_rows = pl.ds(pl.multiple_of(lo + core * part, 8), part)
    for p in range(pieces):
        which, i = p // per, p % per
        cols = slice(i * pw, (i + 1) * pw)
        out_ref[2 * which + core, :, cols] = acc[p, mine_rows, :] * scale
    for p in range(pieces):
        which, i = p // per, p % per
        cols = slice(i * pw, (i + 1) * pw)
        f_copy(p).wait_recv()
        out_ref[2 * which + 1 - core, :, cols] = final[p] * scale

    gain_ref[...] = gacc[bits] * scale
    for s in range(bits):
        g_copy(s).wait_send()
    for which in range(3):
        for off in range(1, members):
            b_copy(which, off).wait_send()
    for p in range(pieces):
        for s in range(bits):
            r_copy(p, s).wait_send()
        f_copy(p).wait_send()


QUAD = 4


def xor_bits(value, bits):
    high, low = lax.div(value, 2), lax.rem(value, 2)
    if bits & 2:
        high = 1 - high
    if bits & 1:
        low = 1 - low
    return high * 2 + low


def encoded(frames_ref, first_time, put):
    length, features = frames_ref.shape
    half_width = features // 2
    index = lax.broadcasted_iota(jnp.int32, (1, half_width), 1).astype(F32)
    frequency = 0.0625 * jnp.exp(-math.log(1000.0) * index / half_width)
    groups_of = length // 8
    outer = first_time + 8 * lax.broadcasted_iota(jnp.int32, (groups_of, half_width), 0)
    inner = lax.broadcasted_iota(jnp.int32, (8, half_width), 0)
    outer, inner = outer.astype(F32) * frequency, inner.astype(F32) * frequency
    so, co, si, ci = jnp.sin(outer), jnp.cos(outer), jnp.sin(inner), jnp.cos(inner)
    for a in range(groups_of):
        s, c = so[a:a + 1], co[a:a + 1]
        r = slice(a * 8, (a + 1) * 8)
        put(r, slice(0, half_width), frames_ref[r, :half_width] + (s * ci + c * si))
        put(r, slice(half_width, features), frames_ref[r, half_width:] + (c * ci - s * si))


def quad_kernel(owners, groups, heads, names, *refs):
    b = types.SimpleNamespace(**dict(zip(names, refs)))
    me = lax.axis_index("tm")
    vid = lax.axis_index("video")
    planes = owners // QUAD
    plane, q = lax.div(me, QUAD), lax.rem(me, QUAD)
    y = lax.div(q, 2)
    members = groups * QUAD
    mine = vid * QUAD + q
    rows, features = b.mem.shape
    length = b.frames.shape[0]
    head = features // heads
    pairs = heads // 2
    pw = 2 * head
    blk = rows // QUAD
    pieces = pairs // groups
    span = features // planes
    part = features // owners
    scale = head ** (-0.5)
    q1, q2, q3 = xor_bits(q, 1), xor_bits(q, 2), xor_bits(q, 3)
    core = lax.rem(q, 2)
    last, rest = plane == planes - 1, plane < planes - 1
    last_low = jnp.logical_and(last, y == 0)
    last_high = jnp.logical_and(last, y == 1)
    own_half, other_half = pl.ds(2 * core, 2), pl.ds(2 * (1 - core), 2)
    pending = []

    def dev(v, at, qq):
        return {"video": v, "tm": at * QUAD + qq}

    def member(g):
        return dev(lax.div(g, QUAD), plane, lax.rem(g, QUAD))

    def remote(src, dst, ss, rs, to):
        return pltpu.make_async_remote_copy(
            src_ref=src, dst_ref=dst, send_sem=ss, recv_sem=rs, device_id=to, device_id_type=MESH
        )

    def guarded(cond, act):
        if cond is None:
            act()
        else:
            pl.when(cond)(act)

    def send(cond, *copy):
        guarded(cond, lambda: remote(*copy).start())
        pending.append((cond, copy))

    def arrived(dst, rs):
        remote(dst, dst, b.dummy.at[0], rs, dev(vid, plane, q1)).wait_recv()

    weights = [(b.wq_hbm, b.wq), (b.wk_hbm, b.wk), (b.wv_hbm, b.wv), (b.wo_hbm, b.wo)]

    def load(k):
        return pltpu.make_async_copy(weights[k][0], weights[k][1], b.w_sem.at[k])

    for k in (1, 2, 0, 3):
        load(k).start()

    barrier = pltpu.get_barrier_semaphore()
    for off in range(1, members):
        pl.semaphore_signal(barrier, inc=1, device_id=member(lax.rem(mine + off, members)), device_id_type=MESH)
    for off in range(1, planes):
        pl.semaphore_signal(
            barrier, inc=1, device_id=dev(vid, lax.rem(plane + off, planes), q), device_id_type=MESH
        )

    @pl.when(plane == planes - 2)
    def _():
        pl.semaphore_signal(
            barrier, inc=1, device_id=dev(vid, jnp.minimum(plane + 1, planes - 1), y), device_id_type=MESH
        )

    def put_key(r, cols, value):
        b.kin[vid, q, r, cols] = value

    encoded(b.frames, b.offset[0] + me * length, put_key)
    for h in range(heads):
        b.misc[q, h:h + 1, :] = b.bias[h]
    b.misc[q, heads:heads + 1, :] = jnp.zeros((1, length), F32) + b.slot[0].astype(F32)
    for j in range(QUAD):
        b.pack_out[j, :blk] = b.mem[j * blk:(j + 1) * blk, :].astype(F32)
        b.pack_out[j, blk:] = b.cot[j * blk:(j + 1) * blk, :].astype(F32)

    @pl.when(rest)
    def _():
        b.pack[q] = b.pack_out[q]

    @pl.when(last)
    def _():
        b.pack[own_half] = b.pack_out[own_half]

    pl.semaphore_wait(barrier, members - 1 + planes - 1 + jnp.where(last_low, 2 if planes > 1 else 0, 0))

    def send_key(cond, slot, sem, to):
        send(cond, b.kin.at[vid, slot], b.kin.at[vid, slot], b.kin_send.at[sem], b.kin_recv.at[vid, slot], to)

    send_key(rest, q, 0, dev(vid, plane, q2))
    send_key(None, q, 1, dev(vid, plane, q1))
    for k, other in ((0, q1), (1, q2), (2, q3)):
        to = dev(vid, plane, other)
        send(None if k == 0 else rest, b.misc.at[q], b.misc.at[q], b.misc_send.at[k], b.misc_recv.at[q], to)
        send(rest, b.pack_out.at[other], b.pack.at[q], b.pack_send.at[k], b.pack_recv.at[q], to)
    send(
        last, b.pack_out.at[other_half], b.pack.at[own_half], b.pack_send.at[0], b.pack_recv.at[q],
        dev(vid, plane, q1),
    )
    for off in range(1, groups):
        send_key(y == 0, q, 3 * off, dev(lax.rem(vid + off, groups), plane, q))

    low = lax.broadcasted_iota(jnp.int32, (length, pw), 1) < head
    zero = jnp.zeros((length, pw), BF16)

    def project(slot):
        keyin = b.kin[vid, slot].astype(BF16)
        kp = dot(keyin, b.wk[...], NN).astype(BF16)
        vp = dot(keyin, b.wv[...], NN).astype(BF16)
        for p in range(pairs):
            kk = kp[:, p * pw:(p + 1) * pw]
            vv = vp[:, p * pw:(p + 1) * pw]
            b.kbd[slot, p, :length] = jnp.where(low, kk, zero)
            b.kbd[slot, p, length:] = jnp.where(low, zero, kk)
            b.vbd[slot, p, :length] = jnp.where(low, vv, zero)
            b.vbd[slot, p, length:] = jnp.where(low, zero, vv)

    for k in (1, 2, 0, 3):
        load(k).wait()
    project(q)
    b.wot[...] = jnp.transpose(b.wo[...])
    b.wqt[...] = jnp.transpose(b.wq[...])
    arrived(b.kin.at[vid, q1], b.kin_recv.at[vid, q1])
    project(q1)
    arrived(b.misc.at[q1], b.misc_recv.at[q1])

    def pass_on(cond, low_cond):
        guarded(cond, lambda: arrived(b.kin.at[vid, q2], b.kin_recv.at[vid, q2]))
        send_key(cond, q2, 2, dev(vid, plane, q1))
        for off in range(1, groups):
            send_key(low_cond, q2, 3 * off + 1, dev(lax.rem(vid + off, groups), plane, q))

    pass_on(rest, jnp.logical_and(rest, y == 0))

    @pl.when(rest)
    def _():
        project(q2)
        arrived(b.kin.at[vid, q3], b.kin_recv.at[vid, q3])
        project(q3)
        for other in (q1, q2, q3):
            arrived(b.pack.at[other], b.pack_recv.at[other])
        for other in (q2, q3):
            arrived(b.misc.at[other], b.misc_recv.at[other])

    @pl.when(last)
    def _():
        arrived(b.pack.at[other_half], b.pack_recv.at[q1])

    gain = jnp.concatenate([b.gain[k:k + 1, :] for k in range(b.gain.shape[0])], axis=-1)
    mem = jnp.concatenate([b.pack[j, :blk] for j in range(QUAD)], axis=0)
    inv = lax.rsqrt(jnp.mean(mem * mem, axis=-1, keepdims=True) + NORM_EPSILON)
    unit = mem * inv
    b.unit[...] = unit
    b.inv[...] = jnp.broadcast_to(inv, b.inv.shape)
    normed = (unit * gain).astype(BF16)
    b.normed[...] = normed.astype(F32)
    query = dot(normed, b.wq[...], NN).astype(BF16)
    for p in range(pairs):
        b.qp[p] = query[:, p * pw:(p + 1) * pw].astype(F32)
    def attend(r, slot):
        scores = [dot(query[r, p * pw:(p + 1) * pw], b.kbd[slot, p], NT) for p in range(pairs)]
        for p in range(pairs):
            halves = []
            for k in range(2):
                h = 2 * p + k
                sc = scores[p][:, k * length:(k + 1) * length] * scale + b.misc[slot, h:h + 1, :]
                e = jnp.exp(sc - jnp.max(sc, axis=-1, keepdims=True))
                pr = e / jnp.sum(e, axis=-1, keepdims=True)
                b.prob[r, h * length:(h + 1) * length] = pr
                halves.append(pr.astype(BF16))
            both = jnp.concatenate(halves, axis=-1)
            b.half[p, r, :] = both.astype(F32)
            b.attended[r, p * pw:(p + 1) * pw] = dot(both, b.vbd[slot, p], NN).astype(BF16).astype(F32)

    singles = [(slice(j * blk, (j + 1) * blk), (j,)) for j in reversed(range(QUAD))]
    doubles = [(slice(2 * a * blk, 2 * (a + 1) * blk), (2 * a, 2 * a + 1)) for a in (1, 0)]

    @pl.when(rest)
    def _():
        for r, (j,) in singles:
            attend(r, j)

    @pl.when(last)
    def _():
        for r, (k, _) in doubles:
            attend(r, 2 * y + k // 2)

    def early_refs(role, v):
        at = pl.ds(v * pieces, pieces)
        return (
            (b.qp.at[at], b.narrow), (b.half.at[at], b.wide), (b.attended, b.early), (b.normed, b.early),
        )[role]

    for role in range(QUAD):
        for off in range(groups):
            v = lax.rem(vid + off, groups)
            src, dst = early_refs(role, v)
            send(
                q != role if off == 0 else None, src, dst.at[mine],
                b.early_send.at[role, off], b.early_recv.at[mine], dev(v, plane, role),
            )

        @pl.when(q == role)
        def _():
            src, dst = early_refs(role, vid)
            dst[mine] = src[...]

    def early_work(after):
        for role in range(QUAD):
            @pl.when(q == role)
            def _():
                dst = early_refs(role, vid)[1]
                for off in range(1, members):
                    g = lax.rem(mine + off, members)
                    arrived(dst.at[g], b.early_recv.at[g])

        @pl.when(y == 0)
        def _():
            if after:
                guarded(last, lambda: arrived(b.kin.at[vid, q3], b.kin_recv.at[vid, q3]))
            for off in range(1, groups):
                v = lax.rem(vid + off, groups)
                for k, slot in ((0, q), (1, q2)):
                    arrived(b.kin.at[v, slot], b.kin_recv.at[v, slot])
                    forward(off, k, v, slot).start()
            for off in range(1, groups):
                v = lax.rem(vid + off, groups)
                for slot in (q1, q3):
                    arrived(b.kin.at[v, slot], b.kin_recv.at[v, slot])
            for g in range(members):
                b.left[:, g * length:(g + 1) * length] = jnp.transpose(b.kin[g // QUAD, g % QUAD]).astype(BF16)

        @pl.when(y == 1)
        def _():
            for g in range(0, members, 2):
                both = jnp.concatenate([b.early[g], b.early[g + 1]], axis=0)
                b.left[:, g * rows:(g + 2) * rows] = jnp.transpose(both).astype(BF16)

    def forward(off, k, v, slot):
        return remote(
            b.kin.at[v, slot], b.kin.at[v, slot], b.fwd_send.at[off, k], b.kin_recv.at[v, slot],
            dev(vid, plane, q1),
        )

    before = planes // 2

    @pl.when(plane < before)
    def _():
        early_work(False)

    below = jnp.maximum(plane - 1, 0)
    single_to = (
        jnp.logical_and(rest, plane > 0),
        (b.passed.at[0], b.incoming, b.chain_send.at[0], b.chain_recv.at[0], dev(vid, below, q)),
    )
    across_to = (
        last_high,
        (b.passed.at[pl.ds(0, 2)], b.across, b.chain_send.at[0], b.across_recv.at[0], dev(vid, plane, q2)),
    )
    double_to = [
        (
            jnp.logical_and(last_low, plane > 0),
            (b.passed.at[k], b.incoming, b.chain_send.at[k], b.chain_recv.at[0], dev(vid, below, 2 * core + k)),
        )
        for k in range(2)
    ]

    def step(r, blocks, slot, carried, outgoing):
        grad_in = carried + jnp.concatenate([b.pack[k, blk:] for k in blocks], axis=0)
        live = jnp.concatenate([b.misc[slot, heads:heads + 1, :]] * (features // length), axis=-1)
        og = (live * grad_in).astype(BF16)
        att = dot(og, b.wot[...], NN).astype(BF16)
        prob_grads = [dot(att[:, p * pw:(p + 1) * pw], b.vbd[slot, p], NT) for p in range(pairs)]
        query_grads = []
        score_grads = []
        for p in range(pairs):
            halves = []
            for k in range(2):
                h = 2 * p + k
                pg = prob_grads[p][:, k * length:(k + 1) * length]
                pr = b.prob[r, h * length:(h + 1) * length]
                inner = jnp.sum(pr * pg, axis=-1, keepdims=True)
                halves.append((pr * (pg - inner) * scale).astype(BF16))
            both = jnp.concatenate(halves, axis=-1)
            score_grads.append(both)
            query_grads.append(dot(both, b.kbd[slot, p], NN).astype(BF16))
        qg = jnp.concatenate(query_grads, axis=-1)
        ng = dot(qg, b.wqt[...], NN)
        un = b.unit[r, :]
        sc = ng * gain
        carried = grad_in + b.inv[r, 0:1] * (sc - un * jnp.mean(sc * un, axis=-1, keepdims=True))
        for n, k in enumerate(blocks):
            b.passed[k] = carried[n * blk:(n + 1) * blk]
        for cond, copy in outgoing:
            pl.when(cond)(lambda: remote(*copy).start())
        for p in range(pairs):
            cols = slice(p * pw, (p + 1) * pw)
            b.sg[p, r, :] = score_grads[p].astype(F32)
            b.att[p, r, :] = att[:, cols].astype(F32)
            b.og[p, r, :] = og[:, cols].astype(F32)
            b.qg[p, r, :] = qg[:, cols].astype(F32)
        return carried, jnp.sum(ng * un, axis=0, keepdims=True)

    pending.extend([single_to, across_to] + double_to)

    @pl.when(rest)
    def _():
        arrived(b.incoming, b.chain_recv.at[0])
        gain_total = jnp.zeros((1, features), F32)
        carried = b.incoming[...]
        for r, (j,) in singles:
            carried, gain_part = step(r, (j,), j, carried, [single_to] if j == 0 else [])
            gain_total = gain_total + gain_part
        b.gsum[mine] = gain_total

    @pl.when(last_high)
    def _():
        b.across[...] = jnp.zeros_like(b.across)

    @pl.when(last_low)
    def _():
        arrived(b.across, b.across_recv.at[0])

    @pl.when(last)
    def _():
        gain_total = jnp.zeros((1, features), F32)
        carried = jnp.concatenate([b.across[0], b.across[1]], axis=0)
        for r, blocks in doubles:
            outgoing = [across_to] + double_to if blocks[0] == 0 else []
            carried, gain_part = step(r, blocks, 2 * y + blocks[0] // 2, carried, outgoing)
            gain_total = gain_total + gain_part
        b.gsum[mine] = gain_total

    send_key(last_high, q, 0, dev(vid, plane, q2))
    for off in range(1, members):
        g = lax.rem(mine + off, members)
        send(None, b.gsum.at[mine], b.gsum.at[mine], b.gsum_send.at[off], b.gsum_recv.at[mine], member(g))

    def late_refs(role, v, i):
        at = v * pieces + i
        return (
            (b.sg.at[at], b.wide), (b.att.at[at], b.narrow), (b.og.at[at], b.narrow), (b.qg.at[at], b.narrow),
        )[role]

    for i in range(pieces):
        for off in reversed(range(groups)):
            v = lax.rem(vid + off, groups)
            for role in range(QUAD):
                src, dst = late_refs(role, v, i)
                send(
                    q != role if off == 0 else None, src, dst.at[mine, i],
                    b.late_send.at[i, role, off], b.late_recv.at[mine, i], dev(v, plane, role),
                )
        for role in range(QUAD):
            @pl.when(q == role)
            def _():
                src, dst = late_refs(role, vid, i)
                dst[mine, i] = src[...]

    for j in range(QUAD):
        send(
            jnp.logical_and(rest, q != j), b.passed.at[j], b.returned.at[q], b.ret_send.at[j], b.ret_recv.at[q],
            dev(vid, plane, j),
        )
    send(
        last, b.passed.at[other_half], b.returned.at[own_half], b.ret_send.at[0], b.ret_recv.at[q],
        dev(vid, plane, q1),
    )
    pass_on(last_low, last_low)

    @pl.when(plane >= before)
    def _():
        early_work(True)

    lowr = lax.broadcasted_iota(jnp.int32, (rows, pw), 1) < head
    zr = jnp.zeros((rows, pw), BF16)

    def product(i):
        for role in range(QUAD):
            @pl.when(q == role)
            def _():
                dst = late_refs(role, vid, i)[1]
                for off in range(1, members):
                    g = lax.rem(mine + off, members)
                    arrived(dst.at[g, i], b.late_recv.at[g, i])

        def gather(ref, v, j, paired):
            if paired:
                r = slice(2 * (j % 2) * blk, 2 * (j % 2 + 1) * blk)
                return jnp.concatenate([ref[v * QUAD + 2 * (j // 2) + k, i, r, :] for k in range(2)], axis=0)
            r = slice(j * blk, (j + 1) * blk)
            return jnp.concatenate([ref[v * QUAD + k, i, r, :] for k in range(QUAD)], axis=0)

        def key_rows_of(paired):
            for v in range(groups):
                for j in range(QUAD):
                    wide = gather(b.wide, v, j, paired).astype(BF16)
                    right = gather(b.narrow, v, j, paired).astype(BF16)
                    wide = jnp.concatenate([wide[:, :length], wide[:, length:]], axis=0)
                    right = jnp.concatenate([jnp.where(lowr, right, zr), jnp.where(lowr, zr, right)], axis=0)
                    at = (v * QUAD + j) * length
                    b.right[at:at + length, :] = dot(wide, right, TN).astype(BF16)

        @pl.when(jnp.logical_and(rest, y == 0))
        def _():
            key_rows_of(False)

        @pl.when(last_low)
        def _():
            key_rows_of(True)

        @pl.when(y == 0)
        def _():
            b.acc[i] = dot(b.left[...], b.right[...], NN)

        @pl.when(y == 1)
        def _():
            right = jnp.concatenate([b.narrow[g, i] for g in range(members)], axis=0).astype(BF16)
            b.acc[i] = dot(b.left[:, :members * rows], right, NN)

    def block(at):
        return pl.ds(pl.multiple_of(at * span, 8), span)

    def flow(i, k, up):
        to = plane + k if up else plane - k
        ok = to < planes if up else to >= 0
        fed = plane > 0 if up else plane < planes - 1
        land, ss, rs = (b.up, b.up_send, b.up_recv) if up else (b.down, b.down_send, b.down_recv)
        to = jnp.clip(to, 0, planes - 1)
        at = block(to)
        step = jnp.clip(plane + 1 if up else plane - 1, 0, planes - 1)

        @pl.when(jnp.logical_and(ok, fed))
        def _():
            arrived(land.at[i, at], rs.at[i, to])
            b.acc[i, at, :] = b.acc[i, at, :] + land[i, at, :]

        return ok, (b.acc.at[i, at], land.at[i, at], ss.at[i, to], rs.at[i, to], dev(vid, step, q))

    def flow_all(i, up, near=1):
        for k in reversed(range(near, planes)):
            ok, copy = flow(i, k, up)
            pl.when(ok)(lambda: remote(*copy).start())

    mean = 1.0 / (owners * groups)

    def settle(i):
        at = block(plane)

        @pl.when(plane < planes - 1)
        def _():
            arrived(b.down.at[i, at], b.down_recv.at[i, plane])
            b.acc[i, at, :] = b.acc[i, at, :] + b.down[i, at, :]

        @pl.when(plane > 0)
        def _():
            arrived(b.up.at[i, at], b.up_recv.at[i, plane])
            b.acc[i, at, :] = b.acc[i, at, :] + b.up[i, at, :]

        b.final[i] = b.acc[i, at, :] * mean
        for k, other in ((0, q1), (1, q2), (2, q3)):
            to = dev(vid, plane, other)
            rows_of = pl.ds(pl.multiple_of(other * part, 8), part)
            send(None, b.final.at[i, rows_of], b.fin_land.at[q, i], b.fin_send.at[k, i], b.fin_recv.at[q, i], to)
        b.out[q, :, i * pw:(i + 1) * pw] = b.final[i, pl.ds(pl.multiple_of(q * part, 8), part), :]

    for off in range(1, members):
        g = lax.rem(mine + off, members)
        arrived(b.gsum.at[g], b.gsum_recv.at[g])
    b.gplane[plane] = jnp.sum(b.gsum[...], axis=0)
    for off in range(1, planes):
        to = dev(vid, lax.rem(plane + off, planes), q)
        send(None, b.gplane.at[plane], b.gplane.at[plane], b.gp_send.at[off], b.gp_recv.at[plane], to)

    for i in range(pieces):
        product(i)
        flow_all(i, False)

        @pl.when(plane == 0)
        def _():
            flow_all(i, True, 2)

    @pl.when(plane == 0)
    def _():
        for i in range(pieces):
            for ok, copy in [flow(i, 1, True)] if planes > 1 else []:
                pl.when(ok)(lambda: remote(*copy).start())

    @pl.when(plane > 0)
    def _():
        for i in range(pieces):
            flow_all(i, True)

    for i in range(pieces):
        settle(i)

    def block_rows(at):
        return pl.ds(pl.multiple_of(at * blk, 8), blk)

    @pl.when(rest)
    def _():
        b.grad[block_rows(q), :] = b.passed[q]
        for other in (q1, q2, q3):
            arrived(b.returned.at[other], b.ret_recv.at[other])
            b.grad[block_rows(other), :] = b.returned[other]

    @pl.when(last)
    def _():
        arrived(b.returned.at[other_half], b.ret_recv.at[q1])
        for k in range(2):
            mine_at, other_at = 2 * core + k, 2 * (1 - core) + k
            b.grad[block_rows(mine_at), :] = b.passed[mine_at]
            b.grad[block_rows(other_at), :] = b.returned[other_at]
    for off in range(1, planes):
        at = lax.rem(plane + off, planes)
        arrived(b.gplane.at[at], b.gp_recv.at[at])
    total = jnp.sum(b.gplane[...], axis=0) * mean
    for k in range(b.gain_out.shape[0]):
        b.gain_out[k:k + 1, :] = total[:, k * 128:(k + 1) * 128]
    for i in range(pieces):
        for other in (q1, q2, q3):
            arrived(b.fin_land.at[other, i], b.fin_recv.at[other, i])
            b.out[other, :, i * pw:(i + 1) * pw] = b.fin_land[other, i]

    for cond, copy in pending:
        guarded(cond, lambda: remote(*copy).wait_send())

    @pl.when(y == 0)
    def _():
        for off in range(1, groups):
            v = lax.rem(vid + off, groups)
            for k, slot in ((0, q), (1, q2)):
                forward(off, k, v, slot).wait_send()

    for i in range(pieces):
        for up in (False, True):
            for k in range(1, planes):
                to = plane + k if up else plane - k
                ok = to < planes if up else to >= 0
                to = jnp.clip(to, 0, planes - 1)
                land, ss, rs = (b.up, b.up_send, b.up_recv) if up else (b.down, b.down_send, b.down_recv)

                @pl.when(ok)
                def _():
                    remote(
                        b.acc.at[i, block(to)], land.at[i, block(to)], ss.at[i, to], rs.at[i, to],
                        dev(vid, jnp.clip(plane + 1 if up else plane - 1, 0, planes - 1), q),
                    ).wait_send()


def hand_over(grad, weights, gain, grad_out, query_out, key_out, value_out, out_out, gain_out):
    grad_out[...] = grad[...]
    for k, ref in enumerate((key_out, value_out, out_out, query_out)):
        ref[...] = weights[k]
    gain_out[...] = gain[...]


def quad_fits(owners, groups, heads, rows, length, features):
    pw = 2 * features // heads
    return (
        owners % QUAD == 0 and rows % (16 * QUAD) == 0 and length % 128 == 0 and pw == 128 and length == pw
        and (heads // 2) % groups == 0 and features % (8 * owners) == 0 and features % 256 == 0
    )


def quad_call(memory, frames, mem_cot, slot_used, key_bias, start_offset, norm_gain, w_query, w_key, w_value, w_out):
    owners = lax.axis_size("tm")
    groups = lax.axis_size("video")
    rows, features = memory.shape[3:]
    length = frames.shape[3]
    heads = key_bias.shape[3]
    planes = owners // QUAD
    members = groups * QUAD
    pairs = heads // 2
    pieces = pairs // groups
    pw = 2 * features // heads
    blk = rows // QUAD
    part = features // owners
    width = features // groups
    vm, sds = pltpu.VMEM, jax.ShapeDtypeStruct
    sem = lambda *shape: pltpu.SemaphoreType.DMA(shape)
    scratch = dict(
        kin=vm((groups, QUAD, length, features), F32), misc=vm((QUAD, 16, length), F32),
        pack_out=vm((QUAD, 2 * blk, features), F32), pack=vm((QUAD, 2 * blk, features), F32),
        wq=vm((features, features), BF16), wk=vm((features, features), BF16),
        wv=vm((features, features), BF16), wo=vm((features, features), BF16),
        wot=vm((features, features), BF16), wqt=vm((features, features), BF16),
        kbd=vm((QUAD, pairs, 2 * length, pw), BF16), vbd=vm((QUAD, pairs, 2 * length, pw), BF16),
        unit=vm((rows, features), F32), inv=vm((rows, 128), F32), prob=vm((rows, heads * length), F32),
        normed=vm((rows, features), F32), attended=vm((rows, features), F32),
        qp=vm((pairs, rows, pw), F32), att=vm((pairs, rows, pw), F32),
        og=vm((pairs, rows, pw), F32), qg=vm((pairs, rows, pw), F32),
        half=vm((pairs, rows, 2 * length), F32), sg=vm((pairs, rows, 2 * length), F32),
        wide=vm((members, pieces, rows, 2 * length), F32), narrow=vm((members, pieces, rows, pw), F32),
        early=vm((members, rows, features), F32), left=vm((features, members * length), BF16),
        right=vm((members * length, pw), BF16), acc=vm((pieces, features, pw), F32),
        up=vm((pieces, features, pw), F32), down=vm((pieces, features, pw), F32),
        final=vm((pieces, features // planes, pw), F32), fin_land=vm((QUAD, pieces, part, pw), F32),
        incoming=vm((blk, features), F32), across=vm((2, blk, features), F32), passed=vm((QUAD, blk, features), F32),
        returned=vm((QUAD, blk, features), F32),
        gsum=vm((members, 1, features), F32), gplane=vm((planes, 1, features), F32),
        dummy=sem(1), w_sem=sem(4), kin_send=sem(3 * groups), kin_recv=sem(groups, QUAD),
        misc_send=sem(3), misc_recv=sem(QUAD), pack_send=sem(3), pack_recv=sem(QUAD),
        early_send=sem(QUAD, groups), early_recv=sem(members), fwd_send=sem(groups, 2),
        chain_send=sem(2), chain_recv=sem(1), across_recv=sem(1), gsum_send=sem(members), gsum_recv=sem(members),
        late_send=sem(pieces, QUAD, groups), late_recv=sem(members, pieces),
        ret_send=sem(QUAD), ret_recv=sem(QUAD), gp_send=sem(planes), gp_recv=sem(planes),
        up_send=sem(pieces, planes), up_recv=sem(pieces, planes),
        down_send=sem(pieces, planes), down_recv=sem(pieces, planes),
        fin_send=sem(3, pieces), fin_recv=sem(QUAD, pieces),
    )
    names = ["slot", "offset", "mem", "frames", "cot", "bias", "gain", "wq_hbm", "wk_hbm", "wv_hbm", "wo_hbm"]
    names = names + ["grad", "out", "gain_out"] + list(scratch)
    vmem = pl.BlockSpec(memory_space=pltpu.VMEM)
    smem = pl.BlockSpec(memory_space=pltpu.SMEM)
    hbm = pl.BlockSpec(memory_space=pl.ANY)
    grad, weights, gain = pl.pallas_call(
        functools.partial(quad_kernel, owners, groups, heads, tuple(names)),
        out_shape=(
            sds((rows, features), F32), sds((QUAD, part, width), F32), sds((features // 128, 128), F32),
        ),
        in_specs=[smem, smem] + [vmem] * 5 + [hbm] * 4,
        out_specs=(vmem,) * 3,
        scratch_shapes=list(scratch.values()),
        compiler_params=pltpu.CompilerParams(collective_id=0, has_side_effects=True, vmem_limit_bytes=58 * 1024 * 1024),
        name="quad",
    )(
        slot_used[0, 0], start_offset[0], memory[0, 0, 0], frames[0, 0, 0], mem_cot[0, 0, 0],
        key_bias[0, 0, 0][:, None, :], norm_gain.reshape(features // 128, 128), w_query, w_key, w_value, w_out,
    )
    matrix = sds((part, width), F32)
    grad, query, key, value, out, gain = pl.pallas_call(
        hand_over,
        out_shape=(sds((rows, features), F32), matrix, matrix, matrix, matrix, sds((features // 128, 128), F32)),
        in_specs=[vmem] * 3,
        out_specs=(vmem,) * 6,
        name="hand_over",
    )(grad, weights, gain)
    return (grad[None, None, None], query, key, value, out, gain.reshape(features))


def on_device(
    memory, frames, mem_cot, slot_used, key_bias, start_offset, norm_gain, w_query, w_key, w_value, w_out
):
    owners = lax.axis_size("tm")
    groups = lax.axis_size("video")
    position = lax.axis_index("tm")
    streams, rows, features = memory.shape[2:]
    length = frames.shape[3]
    heads = key_bias.shape[3]
    if quad_fits(owners, groups, heads, rows, length, features):
        return quad_call(
            memory, frames, mem_cot, slot_used, key_bias, start_offset, norm_gain, w_query, w_key, w_value, w_out
        )
    members = 2 * groups
    chips = owners // 2
    bits = chips.bit_length() - 1
    width = features // groups
    keyin = key_rows(frames[0, 0, 0], start_offset[0, 0], position)
    vmem = pl.BlockSpec(memory_space=pltpu.VMEM)
    smem = pl.BlockSpec(memory_space=pltpu.SMEM)
    sds = jax.ShapeDtypeStruct
    pw = 128 if width % 128 == 0 else width
    pieces = 2 * (width // pw)
    dma = pltpu.SemaphoreType.DMA
    grad, weights, gain = pl.pallas_call(
        functools.partial(whole_kernel, owners, groups, heads),
        out_shape=(
            sds((rows, features), F32),
            sds((4, features // owners, width), F32),
            sds((1, features), F32),
        ),
        in_specs=[smem] + [vmem] * 9,
        out_specs=(vmem,) * 3,
        scratch_shapes=[
            pltpu.VMEM((members, length, features), F32),
            pltpu.VMEM((members, rows, features), F32),
            pltpu.VMEM((2, groups, length, width), F32),
            pltpu.VMEM((2, groups, rows, width), F32),
            pltpu.VMEM((1, features), F32),
            pltpu.VMEM((rows, features), F32),
            pltpu.VMEM((2, rows, features), F32),
            pltpu.VMEM((rows, heads * length), F32),
            pltpu.VMEM((rows, heads * length), BF16),
            pltpu.VMEM((heads // 2, 2 * length, 2 * features // heads), BF16),
            pltpu.VMEM((heads // 2, 2 * length, 2 * features // heads), BF16),
            pltpu.VMEM((rows, features), BF16),
            pltpu.VMEM((rows, features), BF16),
            pltpu.VMEM((rows, heads * length), BF16),
            pltpu.VMEM((rows, features), BF16),
            pltpu.VMEM((rows, features), BF16),
            pltpu.VMEM((rows, features), F32),
            pltpu.VMEM((rows, 128), F32),
            pltpu.VMEM((features, features), BF16),
            pltpu.VMEM((features, features), BF16),
            dma((CHUNKS,)), dma((CHUNKS,)), dma((2, members)), dma((2, members)),
            pltpu.VMEM((members, length, width), F32),
            pltpu.VMEM((members, rows, width), F32),
            pltpu.VMEM((features, members * length), BF16),
            pltpu.VMEM((features, members * rows), BF16),
            pltpu.VMEM((pieces, features, pw), F32),
            pltpu.VMEM((pieces, features // owners, pw), F32),
            pltpu.VMEM((members, 1, features), F32),
            pltpu.VMEM((bits + 1, 1, features), F32),
            pltpu.VMEM((max(bits, 1), 1, features), F32),
        ]
        + [pltpu.VMEM((pieces, features >> (s + 1), pw), F32) for s in range(bits)]
        + [
            dma((3, members)), dma((3, members)), dma((pieces, bits)), dma((pieces, bits)),
            dma((bits,)), dma((bits,)), dma((pieces,)), dma((pieces,)),
        ],
        compiler_params=pltpu.CompilerParams(collective_id=0, has_side_effects=True, vmem_limit_bytes=58 * 1024 * 1024),
        name="whole",
    )(
        slot_used[0, 0], memory[0, 0, 0], keyin, mem_cot[0, 0, 0], key_bias[0, 0, 0],
        norm_gain[None, :], w_query, w_key, w_value, w_out,
    )
    return (grad[None, None, None], weights[1], weights[2], weights[3], weights[0], gain[0])


def solution(mesh):
    return jax.shard_map(
        on_device,
        mesh=mesh,
        in_specs=(
            P("video", "tm", None, None, None),
            P("video", "tm", None, None, None),
            P("video", "tm", None, None, None),
            P("video", "tm", None),
            P("video", "tm", None, None, None),
            P("video", None),
            P(),
            P(),
            P(),
            P(),
            P(),
        ),
        out_specs=(
            P("video", "tm", None, None, None),
            P("tm", "video"),
            P("tm", "video"),
            P("tm", "video"),
            P("tm", "video"),
            P(),
        ),
        check_vma=False,
    )
```

```python
import functools
import math
import types

import jax
import jax.numpy as jnp
from jax import lax
from jax.experimental import pallas as pl
from jax.experimental.pallas import tpu as pltpu
from jax.sharding import PartitionSpec as P

NORM_EPSILON = 1e-06
MESH = pl.DeviceIdType.MESH
F32 = jnp.float32
BF16 = jnp.bfloat16
NN = (((1,), (0,)), ((), ()))
NT = (((1,), (1,)), ((), ()))
TN = (((0,), (0,)), ((), ()))
CHUNKS = 4


def dot(left, right, form):
    return lax.dot_general(left, right, form, preferred_element_type=F32)


def key_rows(frame_rows, offset, position):
    length, features = frame_rows.shape
    within = jnp.arange(length, dtype=jnp.int32)
    frame_time = (offset + position * length + within).astype(F32)
    half_width = features // 2
    frequency = 0.0625 * jnp.exp(-math.log(1000.0) * jnp.arange(half_width, dtype=F32) / half_width)
    phases = frame_time[:, None] * frequency
    return frame_rows + jnp.concatenate([jnp.sin(phases), jnp.cos(phases)], axis=-1)


def group_member(groups, g):
    me = lax.axis_index("tm")
    return {"video": lax.div(g, 2), "tm": (me // 2) * 2 + lax.rem(g, 2)}


def whole_kernel(
    owners, groups, heads,
    slot_ref, mem_ref, keyin_ref, cot_ref, bias_ref, gain_ref, wq_ref, wk_ref, wv_ref, wo_ref,
    grad_ref, out_ref, gain_out_ref,
    a1_ref, a2_ref, b1_ref, b2_ref, gsum_ref,
    incoming, mine, prob, half, kbd, vbd, qp, att_all, sg_all, og_all, qg_all, unit_ref, inv_ref, wot, wqt,
    chain_send, chain_recv, a_send, a_recv,
    *reduce_scratch,
):
    me = lax.axis_index("tm")
    vid = lax.axis_index("video")
    chips = owners // 2
    bits = chips.bit_length() - 1
    chip, core = me // 2, lax.rem(me, 2)
    peers = [chip + (1 - 2 * lax.rem(lax.div(chip, 2 ** b), 2)) * 2 ** b for b in range(bits)]
    rows, features = mem_ref.shape
    length = keyin_ref.shape[0]
    head = features // heads
    pairs = heads // 2
    pw = 2 * head
    members = 2 * groups
    g_me = vid * 2 + lax.rem(me, 2)
    scale = head ** (-0.5)

    barrier = pltpu.get_barrier_semaphore()
    for off in range(1, members):
        pl.semaphore_signal(barrier, inc=1, device_id=group_member(groups, lax.rem(g_me + off, members)), device_id_type=MESH)

    for peer in peers:
        pl.semaphore_signal(barrier, inc=1, device_id={"tm": peer * 2 + core}, device_id_type=MESH)

    @pl.when(me > 0)
    def _():
        pl.semaphore_signal(barrier, inc=1, device_id={"tm": me - 1}, device_id_type=MESH)

    @pl.when(me < owners - 1)
    def _():
        pl.semaphore_signal(barrier, inc=1, device_id={"tm": me + 1}, device_id_type=MESH)

    ends = jnp.where(me > 0, 1, 0) + jnp.where(me < owners - 1, 1, 0)
    pl.semaphore_wait(barrier, members - 1 + bits + ends)

    def a_copy(which, src, dst, off):
        g = lax.rem(g_me + off, members)
        return pltpu.make_async_remote_copy(
            src_ref=src, dst_ref=dst.at[g_me], send_sem=a_send.at[which, off], recv_sem=a_recv.at[which, g_me],
            device_id=group_member(groups, g), device_id_type=MESH,
        )

    for off in range(1, members):
        a_copy(0, keyin_ref, a1_ref, off).start()
    a1_ref[g_me] = keyin_ref[...]

    mem = mem_ref[...].astype(F32)
    inv = lax.rsqrt(jnp.mean(mem * mem, axis=-1, keepdims=True) + NORM_EPSILON)
    unit = mem * inv
    unit_ref[...] = unit
    inv_ref[...] = jnp.broadcast_to(inv, inv_ref.shape)
    normed = (unit * gain_ref[...]).astype(BF16)
    mine[1] = normed.astype(F32)
    keyin = keyin_ref[...].astype(BF16)
    query = dot(normed, wq_ref[...], NN).astype(BF16)
    qp[...] = query
    kp = dot(keyin, wk_ref[...], NN).astype(BF16)
    vp = dot(keyin, wv_ref[...], NN).astype(BF16)
    low = lax.broadcasted_iota(jnp.int32, (length, pw), 1) < head
    zero = jnp.zeros((length, pw), BF16)
    for p in range(pairs):
        kk = kp[:, p * pw:(p + 1) * pw]
        vv = vp[:, p * pw:(p + 1) * pw]
        kbd[p, :length] = jnp.where(low, kk, zero)
        kbd[p, length:] = jnp.where(low, zero, kk)
        vbd[p, :length] = jnp.where(low, vv, zero)
        vbd[p, length:] = jnp.where(low, zero, vv)
    wot[...] = jnp.transpose(wo_ref[...])
    wqt[...] = jnp.transpose(wq_ref[...])
    scores = [dot(query[:, p * pw:(p + 1) * pw], kbd[p], NT) for p in range(pairs)]
    for p in range(pairs):
        halves = []
        for q in range(2):
            h = 2 * p + q
            s = scores[p][:, q * length:(q + 1) * length] * scale + bias_ref[h:h + 1, :]
            e = jnp.exp(s - jnp.max(s, axis=-1, keepdims=True))
            pr = e / jnp.sum(e, axis=-1, keepdims=True)
            prob[:, h * length:(h + 1) * length] = pr
            halves.append(pr.astype(BF16))
        both = jnp.concatenate(halves, axis=-1)
        half[:, p * 2 * length:(p + 1) * 2 * length] = both
        mine[0, :, p * pw:(p + 1) * pw] = dot(both, vbd[p], NN).astype(BF16).astype(F32)

    for off in range(1, members):
        g = lax.rem(g_me + off, members)
        a_copy(1, mine.at[lax.rem(g, 2)], a2_ref, off).start()
    a2_ref[g_me] = mine[lax.rem(me, 2)]

    live = slot_ref[0].astype(F32)
    step = rows // CHUNKS

    def chain_copy(c):
        return pltpu.make_async_remote_copy(
            src_ref=grad_ref.at[pl.ds(c * step, step)], dst_ref=incoming.at[pl.ds(c * step, step)],
            send_sem=chain_send.at[c], recv_sem=chain_recv.at[c],
            device_id={"tm": jnp.maximum(me - 1, 0)}, device_id_type=MESH,
        )

    @pl.when(me == owners - 1)
    def _():
        incoming[...] = jnp.zeros_like(incoming)

    gain_total = jnp.zeros((1, features), F32)
    for c in range(CHUNKS):
        r = slice(c * step, (c + 1) * step)

        @pl.when(me < owners - 1)
        def _():
            chain_copy(c).wait_recv()

        grad_in = incoming[r, :] + cot_ref[r, :].astype(F32)
        og = (live * grad_in).astype(BF16)
        att = dot(og, wot[...], NN).astype(BF16)
        prob_grads = [dot(att[:, p * pw:(p + 1) * pw], vbd[p], NT) for p in range(pairs)]
        query_grads = []
        score_grads = []
        for p in range(pairs):
            for q in range(2):
                h = 2 * p + q
                pg = prob_grads[p][:, q * length:(q + 1) * length]
                pr = prob[r, h * length:(h + 1) * length]
                inner = jnp.sum(pr * pg, axis=-1, keepdims=True)
                score_grads.append((pr * (pg - inner) * scale).astype(BF16))
            query_grads.append(dot(jnp.concatenate(score_grads[-2:], axis=-1), kbd[p], NN).astype(BF16))
        qg = jnp.concatenate(query_grads, axis=-1)
        ng = dot(qg, wqt[...], NN)
        un = unit_ref[r, :]
        gain_total = gain_total + jnp.sum(ng * un, axis=0, keepdims=True)
        sc = ng * gain_ref[...]
        grad_ref[r, :] = grad_in + inv_ref[r, 0:1] * (sc - un * jnp.mean(sc * un, axis=-1, keepdims=True))

        @pl.when(me > 0)
        def _():
            chain_copy(c).start()

        og_all[r, :] = og
        att_all[r, :] = att
        qg_all[r, :] = qg
        for h in range(heads):
            sg_all[r, h * length:(h + 1) * length] = score_grads[h]

    gsum_ref[...] = gain_total

    width = features // groups
    lowr = lax.broadcasted_iota(jnp.int32, (rows, pw), 1) < head
    zr = jnp.zeros((rows, pw), BF16)

    def put(out, which, p, value):
        for v in range(groups):
            lo, hi = max(p * pw, v * width), min((p + 1) * pw, (v + 1) * width)
            if lo < hi:
                out[which, v, :, lo - v * width:hi - v * width] = value[:, lo - p * pw:hi - p * pw]

    for p in range(pairs):
        for which, (left_ref, right_ref) in enumerate(((sg_all, qp), (half, att_all))):
            right = right_ref[:, p * pw:(p + 1) * pw]
            right = jnp.concatenate([jnp.where(lowr, right, zr), jnp.where(lowr, zr, right)], axis=0)
            base = 2 * p * length
            left = jnp.concatenate([left_ref[:, base:base + length], left_ref[:, base + length:base + 2 * length]], axis=0)
            put(b1_ref, which, p, dot(left, right, TN).astype(BF16).astype(F32))
        put(b2_ref, 0, p, og_all[:, p * pw:(p + 1) * pw].astype(F32))
        put(b2_ref, 1, p, qg_all[:, p * pw:(p + 1) * pw].astype(F32))

    def a_arrive():
        for off in range(1, members):
            g = lax.rem(g_me + members - off, members)
            for which, dst in ((0, a1_ref), (1, a2_ref)):
                a_copy(which, dst.at[g_me], dst, off).wait_send()
                pltpu.make_async_remote_copy(
                    src_ref=dst.at[g], dst_ref=dst.at[g], send_sem=a_send.at[which, off], recv_sem=a_recv.at[which, g],
                    device_id=group_member(groups, g), device_id_type=MESH,
                ).wait_recv()

    reduce_part(
        owners, groups, peers, a_arrive, a1_ref, a2_ref, b1_ref, b2_ref, gsum_ref, out_ref, gain_out_ref, *reduce_scratch
    )

    @pl.when(me > 0)
    def _():
        for c in range(CHUNKS):
            chain_copy(c).wait_send()


def reduce_part(
    owners, groups, peers, a_arrive,
    a1_ref, a2_ref, b1_ref, b2_ref, gsum_ref,
    out_ref, gain_ref,
    s1, s2, t1, t2, acc, final, gslot, gacc, gland, *rest,
):
    me = lax.axis_index("tm")
    vid = lax.axis_index("video")
    members = 2 * groups
    chips = owners // 2
    bits = chips.bit_length() - 1
    lands = rest[:bits]
    b_send, b_recv, r_send, r_recv, q_send, q_recv, f_send, f_recv = rest[bits:]
    chip, core = me // 2, lax.rem(me, 2)
    g_me = vid * 2 + core
    pieces, features, pw = acc.shape
    per = pieces // 2
    block = features // chips
    part = block // 2
    scale = 1.0 / (owners * groups)
    length, rows = a1_ref.shape[1], a2_ref.shape[1]

    def b_copy(which, off):
        g = lax.rem(g_me + off, members)
        v, c = lax.div(g, 2), lax.rem(g, 2)
        src, dst = ((b1_ref.at[c, v], s1), (b2_ref.at[c, v], s2), (gsum_ref, gslot))[which]
        return pltpu.make_async_remote_copy(
            src_ref=src, dst_ref=dst.at[g_me], send_sem=b_send.at[which, off], recv_sem=b_recv.at[which, g_me],
            device_id=group_member(groups, g), device_id_type=MESH,
        )

    def b_arrive(which, off):
        g = lax.rem(g_me + members - off, members)
        dst = (s1, s2, gslot)[which]
        return pltpu.make_async_remote_copy(
            src_ref=dst.at[g], dst_ref=dst.at[g], send_sem=b_send.at[which, off], recv_sem=b_recv.at[which, g],
            device_id=group_member(groups, g), device_id_type=MESH,
        )

    for which in (2, 1, 0):
        for off in range(1, members):
            b_copy(which, off).start()
    s1[g_me] = b1_ref[core, vid]
    s2[g_me] = b2_ref[core, vid]
    gslot[g_me] = gsum_ref[...]
    a_arrive()
    for g in range(members):
        t1[:, g * length:(g + 1) * length] = jnp.transpose(a1_ref[g]).astype(BF16)
    for g in range(0, members, 2):
        both = jnp.concatenate([a2_ref[g], a2_ref[g + 1]], axis=0)
        t2[:, g * rows:(g + 2) * rows] = jnp.transpose(both).astype(BF16)

    order = [int(format(i, "b").zfill(bits)[::-1], 2) if bits else 0 for i in range(chips)]

    def products(which):
        slots, left = ((s2, t2), (s1, t1))[which]
        for off in range(1, members):
            b_arrive(1 - which, off).wait_recv()
        for i in range(per):
            right = slots[:, :, i * pw:(i + 1) * pw].reshape(left.shape[1], pw).astype(BF16)
            value = dot(left[...], right, NN)
            for pos in range(chips):
                k = order[pos]
                acc[which * per + i, pos * block:(pos + 1) * block, :] = value[k * block:(k + 1) * block, :]

    starts = []
    lo = 0
    for s in range(bits):
        span = features >> (s + 1)
        bit = lax.rem(lax.div(chip, 2 ** s), 2)
        starts.append((lo + (1 - bit) * span, lo + bit * span, span, peers[s]))
        lo = lo + bit * span

    def r_copy(p, s):
        give, _, span, peer = starts[s]
        return pltpu.make_async_remote_copy(
            src_ref=acc.at[p, pl.ds(pl.multiple_of(give, 8), span)], dst_ref=lands[s].at[p],
            send_sem=r_send.at[p, s], recv_sem=r_recv.at[p, s],
            device_id={"tm": peer * 2 + core}, device_id_type=MESH,
        )

    def g_copy(s):
        return pltpu.make_async_remote_copy(
            src_ref=gacc.at[s], dst_ref=gland.at[s], send_sem=q_send.at[s], recv_sem=q_recv.at[s],
            device_id={"tm": peers[s] * 2 + core}, device_id_type=MESH,
        )

    def r_finish(p, s):
        _, keep, span, _ = starts[s]
        r_copy(p, s).wait_recv()
        at = pl.ds(pl.multiple_of(keep, 8), span)
        acc[p, at, :] = acc[p, at, :] + lands[s][p]

    def f_copy(p):
        theirs = pl.ds(pl.multiple_of(lo + (1 - core) * part, 8), part)
        return pltpu.make_async_remote_copy(
            src_ref=acc.at[p, theirs], dst_ref=final.at[p], send_sem=f_send.at[p], recv_sem=f_recv.at[p],
            device_id={"tm": chip * 2 + 1 - core}, device_id_type=MESH,
        )

    for wave in range(pieces + bits):
        if wave == 0:
            products(0)
        if wave == per:
            products(1)
        for s in reversed(range(bits + 1)):
            p = wave - s
            if 0 <= p < pieces:
                if s > 0:
                    r_finish(p, s - 1)
                if s < bits:
                    r_copy(p, s).start()
                else:
                    f_copy(p).start()
        if wave == 0:
            for off in range(1, members):
                b_arrive(2, off).wait_recv()
            gacc[0] = jnp.sum(gslot[...], axis=0)
        if 0 < wave <= bits:
            g_copy(wave - 1).wait_recv()
            gacc[wave] = gacc[wave - 1] + gland[wave - 1]
        if wave < bits:
            g_copy(wave).start()

    mine_rows = pl.ds(pl.multiple_of(lo + core * part, 8), part)
    for p in range(pieces):
        which, i = p // per, p % per
        cols = slice(i * pw, (i + 1) * pw)
        out_ref[2 * which + core, :, cols] = acc[p, mine_rows, :] * scale
    for p in range(pieces):
        which, i = p // per, p % per
        cols = slice(i * pw, (i + 1) * pw)
        f_copy(p).wait_recv()
        out_ref[2 * which + 1 - core, :, cols] = final[p] * scale

    gain_ref[...] = gacc[bits] * scale
    for s in range(bits):
        g_copy(s).wait_send()
    for which in range(3):
        for off in range(1, members):
            b_copy(which, off).wait_send()
    for p in range(pieces):
        for s in range(bits):
            r_copy(p, s).wait_send()
        f_copy(p).wait_send()


QUAD = 4


def xor_bits(value, bits):
    high, low = lax.div(value, 2), lax.rem(value, 2)
    if bits & 2:
        high = 1 - high
    if bits & 1:
        low = 1 - low
    return high * 2 + low


def encoded(frames_ref, first_time, put):
    length, features = frames_ref.shape
    half_width = features // 2
    index = lax.broadcasted_iota(jnp.int32, (1, half_width), 1).astype(F32)
    frequency = 0.0625 * jnp.exp(-math.log(1000.0) * index / half_width)
    groups_of = length // 8
    outer = first_time + 8 * lax.broadcasted_iota(jnp.int32, (groups_of, half_width), 0)
    inner = lax.broadcasted_iota(jnp.int32, (8, half_width), 0)
    outer, inner = outer.astype(F32) * frequency, inner.astype(F32) * frequency
    so, co, si, ci = jnp.sin(outer), jnp.cos(outer), jnp.sin(inner), jnp.cos(inner)
    for a in range(groups_of):
        s, c = so[a:a + 1], co[a:a + 1]
        r = slice(a * 8, (a + 1) * 8)
        put(r, slice(0, half_width), frames_ref[r, :half_width] + (s * ci + c * si))
        put(r, slice(half_width, features), frames_ref[r, half_width:] + (c * ci - s * si))


def quad_kernel(owners, groups, heads, names, *refs):
    b = types.SimpleNamespace(**dict(zip(names, refs)))
    me = lax.axis_index("tm")
    vid = lax.axis_index("video")
    planes = owners // QUAD
    plane, q = lax.div(me, QUAD), lax.rem(me, QUAD)
    y = lax.div(q, 2)
    members = groups * QUAD
    mine = vid * QUAD + q
    rows, features = b.mem.shape
    length = b.frames.shape[0]
    head = features // heads
    pairs = heads // 2
    pw = 2 * head
    blk = rows // QUAD
    pieces = pairs // groups
    span = features // planes
    part = features // owners
    scale = head ** (-0.5)
    q1, q2, q3 = xor_bits(q, 1), xor_bits(q, 2), xor_bits(q, 3)
    core = lax.rem(q, 2)
    last, rest = plane == planes - 1, plane < planes - 1
    last_low = jnp.logical_and(last, y == 0)
    last_high = jnp.logical_and(last, y == 1)
    own_half, other_half = pl.ds(2 * core, 2), pl.ds(2 * (1 - core), 2)
    pending = []

    def dev(v, at, qq):
        return {"video": v, "tm": at * QUAD + qq}

    def member(g):
        return dev(lax.div(g, QUAD), plane, lax.rem(g, QUAD))

    def remote(src, dst, ss, rs, to):
        return pltpu.make_async_remote_copy(
            src_ref=src, dst_ref=dst, send_sem=ss, recv_sem=rs, device_id=to, device_id_type=MESH
        )

    def guarded(cond, act):
        if cond is None:
            act()
        else:
            pl.when(cond)(act)

    def send(cond, *copy):
        guarded(cond, lambda: remote(*copy).start())
        pending.append((cond, copy))

    def arrived(dst, rs):
        remote(dst, dst, b.dummy.at[0], rs, dev(vid, plane, q1)).wait_recv()

    weights = [(b.wq_hbm, b.wq), (b.wk_hbm, b.wk), (b.wv_hbm, b.wv), (b.wo_hbm, b.wo)]

    def load(k):
        return pltpu.make_async_copy(weights[k][0], weights[k][1], b.w_sem.at[k])

    for k in (1, 2, 0, 3):
        load(k).start()

    barrier = pltpu.get_barrier_semaphore()
    for off in range(1, members):
        pl.semaphore_signal(barrier, inc=1, device_id=member(lax.rem(mine + off, members)), device_id_type=MESH)
    for off in range(1, planes):
        pl.semaphore_signal(
            barrier, inc=1, device_id=dev(vid, lax.rem(plane + off, planes), q), device_id_type=MESH
        )

    @pl.when(plane == planes - 2)
    def _():
        pl.semaphore_signal(
            barrier, inc=1, device_id=dev(vid, jnp.minimum(plane + 1, planes - 1), y), device_id_type=MESH
        )

    def put_key(r, cols, value):
        b.kin[vid, q, r, cols] = value

    encoded(b.frames, b.offset[0] + me * length, put_key)
    for h in range(heads):
        b.misc[vid, q, h:h + 1, :] = b.bias[h]
    b.misc[vid, q, heads:heads + 1, :] = jnp.zeros((1, length), F32) + b.slot[0].astype(F32)
    for j in range(QUAD):
        b.pack_out[j, :blk] = b.mem[j * blk:(j + 1) * blk, :].astype(F32)
        b.pack_out[j, blk:] = b.cot[j * blk:(j + 1) * blk, :].astype(F32)

    @pl.when(rest)
    def _():
        b.pack[q] = b.pack_out[q]

    @pl.when(last)
    def _():
        b.pack[own_half] = b.pack_out[own_half]

    pl.semaphore_wait(barrier, members - 1 + planes - 1 + jnp.where(last_low, 2 if planes > 1 else 0, 0))

    def send_key(cond, slot, sem, to):
        send(cond, b.kin.at[vid, slot], b.kin.at[vid, slot], b.kin_send.at[sem], b.kin_recv.at[vid, slot], to)

    def send_misc(cond, sem, to):
        send(cond, b.misc.at[vid, q], b.misc.at[vid, q], b.misc_send.at[sem], b.misc_recv.at[vid, q], to)

    send_key(rest, q, 0, dev(vid, plane, q2))
    send_key(None, q, 1, dev(vid, plane, q1))
    for k, other in ((0, q1), (1, q2), (2, q3)):
        to = dev(vid, plane, other)
        send_misc(None, k, to)
        send(rest, b.pack_out.at[other], b.pack.at[q], b.pack_send.at[k], b.pack_recv.at[q], to)
    send(
        last, b.pack_out.at[other_half], b.pack.at[own_half], b.pack_send.at[0], b.pack_recv.at[q],
        dev(vid, plane, q1),
    )
    for off in range(1, groups):
        send_key(y == 0, q, 3 * off, dev(lax.rem(vid + off, groups), plane, q))
        send_misc(None, 2 + off, dev(lax.rem(vid + off, groups), plane, core))

    low = lax.broadcasted_iota(jnp.int32, (length, pw), 1) < head
    zero = jnp.zeros((length, pw), BF16)

    def project(slot):
        keyin = b.kin[vid, slot].astype(BF16)
        kp = dot(keyin, b.wk[...], NN).astype(BF16)
        vp = dot(keyin, b.wv[...], NN).astype(BF16)
        for p in range(pairs):
            kk = kp[:, p * pw:(p + 1) * pw]
            vv = vp[:, p * pw:(p + 1) * pw]
            b.kbd[slot, p, :length] = jnp.where(low, kk, zero)
            b.kbd[slot, p, length:] = jnp.where(low, zero, kk)
            b.vbd[slot, p, :length] = jnp.where(low, vv, zero)
            b.vbd[slot, p, length:] = jnp.where(low, zero, vv)

    for k in (1, 2, 0, 3):
        load(k).wait()
    project(q)
    b.wot[...] = jnp.transpose(b.wo[...])
    b.wqt[...] = jnp.transpose(b.wq[...])
    arrived(b.kin.at[vid, q1], b.kin_recv.at[vid, q1])
    project(q1)
    for other in (q1, q2, q3):
        arrived(b.misc.at[vid, other], b.misc_recv.at[vid, other])

    def pass_on(cond):
        guarded(cond, lambda: arrived(b.kin.at[vid, q2], b.kin_recv.at[vid, q2]))
        send_key(cond, q2, 2, dev(vid, plane, q1))

    def cross(cond):
        for off in range(1, groups):
            send_key(cond, q, 3 * off + 1, dev(lax.rem(vid + off, groups), plane, core))

    pass_on(rest)

    @pl.when(rest)
    def _():
        project(q2)
        arrived(b.kin.at[vid, q3], b.kin_recv.at[vid, q3])
        project(q3)
        for other in (q1, q2, q3):
            arrived(b.pack.at[other], b.pack_recv.at[other])

    @pl.when(last)
    def _():
        arrived(b.pack.at[other_half], b.pack_recv.at[q1])

    cross(jnp.logical_and(rest, y == 1))

    gain = jnp.concatenate([b.gain[k:k + 1, :] for k in range(b.gain.shape[0])], axis=-1)
    mem = jnp.concatenate([b.pack[j, :blk] for j in range(QUAD)], axis=0)
    inv = lax.rsqrt(jnp.mean(mem * mem, axis=-1, keepdims=True) + NORM_EPSILON)
    unit = mem * inv
    b.unit[...] = unit
    b.inv[...] = jnp.broadcast_to(inv, b.inv.shape)
    normed = (unit * gain).astype(BF16)
    b.normed[...] = normed.astype(F32)
    query = dot(normed, b.wq[...], NN).astype(BF16)
    for p in range(pairs):
        b.qp[p] = query[:, p * pw:(p + 1) * pw].astype(F32)
    def attend(r, slot):
        scores = [dot(query[r, p * pw:(p + 1) * pw], b.kbd[slot, p], NT) for p in range(pairs)]
        for p in range(pairs):
            halves = []
            for k in range(2):
                h = 2 * p + k
                sc = scores[p][:, k * length:(k + 1) * length] * scale + b.misc[vid, slot, h:h + 1, :]
                e = jnp.exp(sc - jnp.max(sc, axis=-1, keepdims=True))
                pr = e / jnp.sum(e, axis=-1, keepdims=True)
                b.prob[r, h * length:(h + 1) * length] = pr
                halves.append(pr.astype(BF16))
            both = jnp.concatenate(halves, axis=-1)
            b.attended[r, p * pw:(p + 1) * pw] = dot(both, b.vbd[slot, p], NN).astype(BF16).astype(F32)

    singles = [(slice(j * blk, (j + 1) * blk), (j,)) for j in reversed(range(QUAD))]
    doubles = [(slice(2 * a * blk, 2 * (a + 1) * blk), (2 * a, 2 * a + 1)) for a in (1, 0)]

    @pl.when(rest)
    def _():
        for r, (j,) in singles:
            attend(r, j)

    @pl.when(last)
    def _():
        for r, (k, _) in doubles:
            attend(r, 2 * y + k // 2)

    def qp_of(v):
        return b.qp.at[pl.ds(v * pieces, pieces)]

    for off in range(groups):
        v = lax.rem(vid + off, groups)
        send(
            y != 0 if off == 0 else None, qp_of(v), b.query.at[mine], b.early_send.at[0, off],
            b.early_recv.at[mine], dev(v, plane, core),
        )
        for role, src in ((2, b.attended), (3, b.normed)):
            send(
                q != role if off == 0 else None, src, b.early.at[mine], b.early_send.at[role, off],
                b.early_recv.at[mine], dev(v, plane, role),
            )

    @pl.when(y == 0)
    def _():
        b.query[mine] = qp_of(vid)[...]

    for role, src in ((2, b.attended), (3, b.normed)):
        @pl.when(q == role)
        def _():
            b.early[mine] = src[...]

    def same_core(side):
        return [
            (off, e, lax.rem(vid + off, groups) * QUAD + 2 * e + side) for off in range(groups) for e in range(2)
        ]

    def share(ref, index, recv, ss, stage):
        for off, e, g in same_core(core):
            at = ref.at[(g, *index)]
            copy = remote(at, at, ss.at[(off, e, *index)], recv.at[(g, *index)], dev(vid, plane, q1))
            if stage == 0 and (off, e) != (0, 0):
                arrived(at, recv.at[(g, *index)])
            if stage == 0:
                copy.start()
            if stage == 2:
                copy.wait_send()
        if stage == 1:
            for off, e, g in same_core(1 - core):
                arrived(ref.at[(g, *index)], recv.at[(g, *index)])

    def forward(off, k, v, slot):
        at, to = b.kin.at[v, slot], dev(vid, plane, q1)
        small = b.misc.at[v, slot]
        return (
            remote(at, at, b.fwd_send.at[off, k], b.kin_recv.at[v, slot], to),
            remote(small, small, b.fwdm_send.at[off, k], b.misc_recv.at[v, slot], to),
        )

    def gather(ref, v, i, j):
        parts = []
        for k in range(QUAD):
            g = v * QUAD + jnp.where(last, 2 * (j // 2) + k // 2, k)
            at = jnp.where(last, (2 * (j % 2) + k % 2) * blk, j * blk)
            parts.append(ref[g, i, pl.ds(pl.multiple_of(at, blk), blk), :])
        return jnp.concatenate(parts, axis=0).astype(BF16)

    half_cols = pl.ds(pl.multiple_of(vid * pieces * pw, 128), pieces * pw)

    def apart(value, p, out, g):
        vv = value[:, p * pw:(p + 1) * pw]
        out[g, p, :length] = jnp.where(low, vv, zero)
        out[g, p, length:] = jnp.where(low, zero, vv)

    def prepare(v):
        @pl.loop(0, QUAD)
        def _(j):
            g = v * QUAD + j
            keyin = b.kin[v, j]
            b.left[:, pl.ds(pl.multiple_of(g * length, 128), length)] = jnp.transpose(keyin).astype(BF16)
            keyin = keyin.astype(BF16)
            kp = dot(keyin, b.wk[:, half_cols], NN).astype(BF16)
            for p in range(pieces):
                apart(kp, p, b.khalf, g)

            @pl.when(q == 0)
            def _():
                vp = dot(keyin, b.wv[:, half_cols], NN).astype(BF16)
                for p in range(pieces):
                    apart(vp, p, b.vhalf, g)

    @pl.when(jnp.logical_and(y == 0, plane < planes // 2))
    def _():
        prepare(vid)

    def early_low():
        guarded(last, lambda: arrived(b.kin.at[vid, q3], b.kin_recv.at[vid, q3]))
        for off in range(1, groups):
            v = lax.rem(vid + off, groups)
            for k, slot in ((0, q), (1, q2)):
                arrived(b.kin.at[v, slot], b.kin_recv.at[v, slot])
                arrived(b.misc.at[v, slot], b.misc_recv.at[v, slot])
                for copy in forward(off, k, v, slot):
                    copy.start()
        share(b.query, (), b.early_recv, b.query_send, 0)

        @pl.when(plane >= planes // 2)
        def _():
            prepare(vid)

        for off in range(1, groups):
            v = lax.rem(vid + off, groups)
            for slot in (q1, q3):
                arrived(b.kin.at[v, slot], b.kin_recv.at[v, slot])
                arrived(b.misc.at[v, slot], b.misc_recv.at[v, slot])
            prepare(v)
        share(b.query, (), b.early_recv, b.query_send, 1)

        @pl.loop(0, pieces)
        def _(i):
            clips = [(v, j) for v in range(groups) for j in range(QUAD)]
            found = []
            for v, j in clips:
                scores = dot(gather(b.query, v, i, j), b.khalf[v * QUAD + j, i], NT)
                for k in range(2):
                    h = 2 * (vid * pieces + i) + k
                    sc = scores[:, k * length:(k + 1) * length] * scale + b.misc[v, j, pl.ds(h, 1), :]
                    e = jnp.exp(sc - jnp.max(sc, axis=-1, keepdims=True))
                    found.append(e / jnp.sum(e, axis=-1, keepdims=True))
            for n, (v, j) in enumerate(clips):
                for k in range(2):
                    b.wide[v * QUAD + j, i, :, k * length:(k + 1) * length] = found[2 * n + k]

    def early_high():
        for off in range(1, members):
            g = lax.rem(mine + off, members)
            arrived(b.early.at[g], b.early_recv.at[g])
        for g in range(0, members, 2):
            both = jnp.concatenate([b.early[g], b.early[g + 1]], axis=0)
            b.left[:, g * rows:(g + 2) * rows] = jnp.transpose(both).astype(BF16)

    below = jnp.maximum(plane - 1, 0)
    single_to = (
        jnp.logical_and(rest, plane > 0),
        (b.passed.at[0], b.incoming, b.chain_send.at[0], b.chain_recv.at[0], dev(vid, below, q)),
    )
    across_to = (
        last_high,
        (b.passed.at[pl.ds(0, 2)], b.across, b.chain_send.at[0], b.across_recv.at[0], dev(vid, plane, q2)),
    )
    double_to = [
        (
            jnp.logical_and(last_low, plane > 0),
            (b.passed.at[k], b.incoming, b.chain_send.at[k], b.chain_recv.at[0], dev(vid, below, 2 * core + k)),
        )
        for k in range(2)
    ]

    def step(r, blocks, slot, carried, outgoing):
        grad_in = carried + jnp.concatenate([b.pack[k, blk:] for k in blocks], axis=0)
        live = jnp.concatenate([b.misc[vid, slot, heads:heads + 1, :]] * (features // length), axis=-1)
        og = (live * grad_in).astype(BF16)
        att = dot(og, b.wot[...], NN).astype(BF16)
        prob_grads = [dot(att[:, p * pw:(p + 1) * pw], b.vbd[slot, p], NT) for p in range(pairs)]
        query_grads = []
        for p in range(pairs):
            halves = []
            for k in range(2):
                h = 2 * p + k
                pg = prob_grads[p][:, k * length:(k + 1) * length]
                pr = b.prob[r, h * length:(h + 1) * length]
                inner = jnp.sum(pr * pg, axis=-1, keepdims=True)
                halves.append((pr * (pg - inner) * scale).astype(BF16))
            both = jnp.concatenate(halves, axis=-1)
            query_grads.append(dot(both, b.kbd[slot, p], NN).astype(BF16))
        qg = jnp.concatenate(query_grads, axis=-1)
        ng = dot(qg, b.wqt[...], NN)
        un = b.unit[r, :]
        sc = ng * gain
        carried = grad_in + b.inv[r, 0:1] * (sc - un * jnp.mean(sc * un, axis=-1, keepdims=True))
        for n, k in enumerate(blocks):
            b.passed[k] = carried[n * blk:(n + 1) * blk]
        for cond, copy in outgoing:
            pl.when(cond)(lambda: remote(*copy).start())
        for p in range(pairs):
            cols = slice(p * pw, (p + 1) * pw)
            b.att[p, r, :] = att[:, cols].astype(F32)
            b.og[p, r, :] = og[:, cols].astype(F32)
            b.qg[p, r, :] = qg[:, cols].astype(F32)
        return carried, jnp.sum(ng * un, axis=0, keepdims=True)

    pending.extend([single_to, across_to] + double_to)

    @pl.when(rest)
    def _():
        arrived(b.incoming, b.chain_recv.at[0])
        gain_total = jnp.zeros((1, features), F32)
        carried = b.incoming[...]
        for r, (j,) in singles:
            carried, gain_part = step(r, (j,), j, carried, [single_to] if j == 0 else [])
            gain_total = gain_total + gain_part
        b.gsum[mine] = gain_total

    @pl.when(last_high)
    def _():
        b.across[...] = jnp.zeros_like(b.across)

    @pl.when(last_low)
    def _():
        arrived(b.across, b.across_recv.at[0])

    @pl.when(last)
    def _():
        gain_total = jnp.zeros((1, features), F32)
        carried = jnp.concatenate([b.across[0], b.across[1]], axis=0)
        for r, blocks in doubles:
            outgoing = [across_to] + double_to if blocks[0] == 0 else []
            carried, gain_part = step(r, blocks, 2 * y + blocks[0] // 2, carried, outgoing)
            gain_total = gain_total + gain_part
        b.gsum[mine] = gain_total

    send_key(last_high, q, 0, dev(vid, plane, q2))
    for off in range(1, members):
        g = lax.rem(mine + off, members)
        send(None, b.gsum.at[mine], b.gsum.at[mine], b.gsum_send.at[off], b.gsum_recv.at[mine], member(g))

    for i in range(pieces):
        for off in reversed(range(groups)):
            v = lax.rem(vid + off, groups)
            for role, cond, src in ((0, y != 0, b.att), (2, q != 2, b.og), (3, q != 3, b.qg)):
                send(
                    cond if off == 0 else None, src.at[v * pieces + i], b.narrow.at[mine, i],
                    b.late_send.at[i, role, off], b.late_recv.at[mine, i],
                    dev(v, plane, core if role == 0 else role),
                )
        for cond, src in ((y == 0, b.att), (q == 2, b.og), (q == 3, b.qg)):
            @pl.when(cond)
            def _():
                b.narrow[mine, i] = src[vid * pieces + i]

    for j in range(QUAD):
        send(
            jnp.logical_and(rest, q != j), b.passed.at[j], b.returned.at[q], b.ret_send.at[j], b.ret_recv.at[q],
            dev(vid, plane, j),
        )
    send(
        last, b.passed.at[other_half], b.returned.at[own_half], b.ret_send.at[0], b.ret_recv.at[q],
        dev(vid, plane, q1),
    )
    pass_on(last_low)
    for off in range(1, groups):
        send_key(last_low, q2, 3 * off + 2, dev(lax.rem(vid + off, groups), plane, q))

    @pl.when(y == 0)
    def _():
        early_low()

    @pl.when(y == 1)
    def _():
        early_high()

    lowr = lax.broadcasted_iota(jnp.int32, (rows, pw), 1) < head
    zr = jnp.zeros((rows, pw), BF16)

    def product(i):
        @pl.when(y == 0)
        def _():
            share(b.narrow, (i,), b.late_recv, b.att_send, 1)

        @pl.when(y == 1)
        def _():
            for off in range(1, members):
                g = lax.rem(mine + off, members)
                arrived(b.narrow.at[g, i], b.late_recv.at[g, i])

        def token_grads(role):
            found = []
            for v in range(groups):
                for j in range(QUAD):
                    g = v * QUAD + j
                    right = att = gather(b.narrow, v, i, j)
                    halves = []
                    if role == 0:
                        right = gather(b.query, v, i, j)
                        prob_grad = dot(att, b.vhalf[g, i], NT)
                    for k in range(2):
                        cols = slice(k * length, (k + 1) * length)
                        pr = b.wide[g, i, :, cols]
                        if role == 0:
                            pg = prob_grad[:, cols]
                            pr = pr * (pg - jnp.sum(pr * pg, axis=-1, keepdims=True)) * scale
                        halves.append(pr.astype(BF16))
                    stacked = jnp.concatenate(halves, axis=0)
                    right = jnp.concatenate([jnp.where(lowr, right, zr), jnp.where(lowr, zr, right)], axis=0)
                    found.append(dot(stacked, right, TN).astype(BF16))
            b.right[...] = jnp.concatenate(found, axis=0)

        for role in range(2):
            pl.when(q == role)(functools.partial(token_grads, role))

        @pl.when(jnp.logical_and(y == 0, i + 1 < pieces))
        def _():
            share(b.narrow, (i + 1,), b.late_recv, b.att_send, 0)

        @pl.when(y == 0)
        def _():
            b.acc[i] = dot(b.left[...], b.right[...], NN)

        @pl.when(y == 1)
        def _():
            right = jnp.concatenate([b.narrow[g, i] for g in range(members)], axis=0).astype(BF16)
            b.acc[i] = dot(b.left[:, :members * rows], right, NN)

    def block(at):
        return pl.ds(pl.multiple_of(at * span, 8), span)

    def flow(i, k, up):
        to = plane + k if up else plane - k
        ok = to < planes if up else to >= 0
        fed = plane > 0 if up else plane < planes - 1
        land, ss, rs = (b.up, b.up_send, b.up_recv) if up else (b.down, b.down_send, b.down_recv)
        to = jnp.clip(to, 0, planes - 1)
        at = block(to)
        step = jnp.clip(plane + 1 if up else plane - 1, 0, planes - 1)

        @pl.when(jnp.logical_and(ok, fed))
        def _():
            arrived(land.at[i, at], rs.at[i, to])
            b.acc[i, at, :] = b.acc[i, at, :] + land[i, at, :]

        return ok, (b.acc.at[i, at], land.at[i, at], ss.at[i, to], rs.at[i, to], dev(vid, step, q))

    def flow_all(i, up, near=1):
        for k in reversed(range(near, planes)):
            ok, copy = flow(i, k, up)
            pl.when(ok)(lambda: remote(*copy).start())

    mean = 1.0 / (owners * groups)

    def settle(i):
        at = block(plane)

        @pl.when(plane < planes - 1)
        def _():
            arrived(b.down.at[i, at], b.down_recv.at[i, plane])
            b.acc[i, at, :] = b.acc[i, at, :] + b.down[i, at, :]

        @pl.when(plane > 0)
        def _():
            arrived(b.up.at[i, at], b.up_recv.at[i, plane])
            b.acc[i, at, :] = b.acc[i, at, :] + b.up[i, at, :]

        b.final[i] = b.acc[i, at, :] * mean
        for k, other in ((0, q1), (1, q2), (2, q3)):
            to = dev(vid, plane, other)
            rows_of = pl.ds(pl.multiple_of(other * part, 8), part)
            send(None, b.final.at[i, rows_of], b.fin_land.at[q, i], b.fin_send.at[k, i], b.fin_recv.at[q, i], to)
        b.out[q, :, i * pw:(i + 1) * pw] = b.final[i, pl.ds(pl.multiple_of(q * part, 8), part), :]

    for off in range(1, members):
        g = lax.rem(mine + off, members)
        arrived(b.gsum.at[g], b.gsum_recv.at[g])
    b.gplane[plane] = jnp.sum(b.gsum[...], axis=0)
    for off in range(1, planes):
        to = dev(vid, lax.rem(plane + off, planes), q)
        send(None, b.gplane.at[plane], b.gplane.at[plane], b.gp_send.at[off], b.gp_recv.at[plane], to)

    @pl.when(y == 0)
    def _():
        share(b.narrow, (0,), b.late_recv, b.att_send, 0)

    @pl.loop(0, pieces)
    def _(i):
        product(i)
        pl.when(last)(lambda: flow_all(i, False))
        pl.when(plane == 0)(lambda: flow_all(i, True, 2))

    @pl.when(jnp.logical_and(plane == 0, planes > 1))
    def _():
        for i in range(pieces):
            remote(*flow(i, 1, True)[1]).start()

    @pl.when(jnp.logical_and(plane > 0, rest))
    def _():
        @pl.loop(0, pieces)
        def _(i):
            flow_all(i, False)
            flow_all(i, True)

    for i in range(pieces):
        settle(i)

    def block_rows(at):
        return pl.ds(pl.multiple_of(at * blk, 8), blk)

    @pl.when(rest)
    def _():
        b.grad[block_rows(q), :] = b.passed[q]
        for other in (q1, q2, q3):
            arrived(b.returned.at[other], b.ret_recv.at[other])
            b.grad[block_rows(other), :] = b.returned[other]

    @pl.when(last)
    def _():
        arrived(b.returned.at[other_half], b.ret_recv.at[q1])
        for k in range(2):
            mine_at, other_at = 2 * core + k, 2 * (1 - core) + k
            b.grad[block_rows(mine_at), :] = b.passed[mine_at]
            b.grad[block_rows(other_at), :] = b.returned[other_at]
    for off in range(1, planes):
        at = lax.rem(plane + off, planes)
        arrived(b.gplane.at[at], b.gp_recv.at[at])
    total = jnp.sum(b.gplane[...], axis=0) * mean
    for k in range(b.gain_out.shape[0]):
        b.gain_out[k:k + 1, :] = total[:, k * 128:(k + 1) * 128]
    for i in range(pieces):
        for other in (q1, q2, q3):
            arrived(b.fin_land.at[other, i], b.fin_recv.at[other, i])
            b.out[other, :, i * pw:(i + 1) * pw] = b.fin_land[other, i]

    for cond, copy in pending:
        guarded(cond, lambda: remote(*copy).wait_send())

    @pl.when(y == 0)
    def _():
        for off in range(1, groups):
            v = lax.rem(vid + off, groups)
            for k, slot in ((0, q), (1, q2)):
                for copy in forward(off, k, v, slot):
                    copy.wait_send()
        share(b.query, (), b.early_recv, b.query_send, 2)
        for i in range(pieces):
            share(b.narrow, (i,), b.late_recv, b.att_send, 2)

    for i in range(pieces):
        for up in (False, True):
            for k in range(1, planes):
                to = plane + k if up else plane - k
                ok = to < planes if up else to >= 0
                to = jnp.clip(to, 0, planes - 1)
                land, ss, rs = (b.up, b.up_send, b.up_recv) if up else (b.down, b.down_send, b.down_recv)

                @pl.when(ok)
                def _():
                    remote(
                        b.acc.at[i, block(to)], land.at[i, block(to)], ss.at[i, to], rs.at[i, to],
                        dev(vid, jnp.clip(plane + 1 if up else plane - 1, 0, planes - 1), q),
                    ).wait_send()


def hand_over(grad, weights, gain, grad_out, query_out, key_out, value_out, out_out, gain_out):
    grad_out[...] = grad[...]
    for k, ref in enumerate((key_out, value_out, out_out, query_out)):
        ref[...] = weights[k]
    gain_out[...] = gain[...]


def quad_fits(owners, groups, heads, rows, length, features):
    pw = 2 * features // heads
    return (
        owners % QUAD == 0 and rows % (16 * QUAD) == 0 and length % 128 == 0 and pw == 128 and length == pw
        and (heads // 2) % groups == 0 and features % (8 * owners) == 0 and features % 256 == 0
    )


def quad_call(memory, frames, mem_cot, slot_used, key_bias, start_offset, norm_gain, w_query, w_key, w_value, w_out):
    owners = lax.axis_size("tm")
    groups = lax.axis_size("video")
    rows, features = memory.shape[3:]
    length = frames.shape[3]
    heads = key_bias.shape[3]
    planes = owners // QUAD
    members = groups * QUAD
    pairs = heads // 2
    pieces = pairs // groups
    pw = 2 * features // heads
    blk = rows // QUAD
    part = features // owners
    width = features // groups
    vm, sds = pltpu.VMEM, jax.ShapeDtypeStruct
    sem = lambda *shape: pltpu.SemaphoreType.DMA(shape)
    scratch = dict(
        kin=vm((groups, QUAD, length, features), F32), misc=vm((groups, QUAD, 16, length), F32),
        pack_out=vm((QUAD, 2 * blk, features), F32), pack=vm((QUAD, 2 * blk, features), F32),
        wq=vm((features, features), BF16), wk=vm((features, features), BF16),
        wv=vm((features, features), BF16), wo=vm((features, features), BF16),
        wot=vm((features, features), BF16), wqt=vm((features, features), BF16),
        kbd=vm((QUAD, pairs, 2 * length, pw), BF16), vbd=vm((QUAD, pairs, 2 * length, pw), BF16),
        unit=vm((rows, features), F32), inv=vm((rows, 128), F32), prob=vm((rows, heads * length), F32),
        normed=vm((rows, features), F32), attended=vm((rows, features), F32),
        qp=vm((pairs, rows, pw), F32), att=vm((pairs, rows, pw), F32),
        og=vm((pairs, rows, pw), F32), qg=vm((pairs, rows, pw), F32),
        query=vm((members, pieces, rows, pw), F32), khalf=vm((members, pieces, 2 * length, pw), BF16),
        vhalf=vm((members, pieces, 2 * length, pw), BF16),
        wide=vm((members, pieces, rows, 2 * length), F32), narrow=vm((members, pieces, rows, pw), F32),
        early=vm((members, rows, features), F32), left=vm((features, members * length), BF16),
        right=vm((members * length, pw), BF16), acc=vm((pieces, features, pw), F32),
        up=vm((pieces, features, pw), F32), down=vm((pieces, features, pw), F32),
        final=vm((pieces, features // planes, pw), F32), fin_land=vm((QUAD, pieces, part, pw), F32),
        incoming=vm((blk, features), F32), across=vm((2, blk, features), F32), passed=vm((QUAD, blk, features), F32),
        returned=vm((QUAD, blk, features), F32),
        gsum=vm((members, 1, features), F32), gplane=vm((planes, 1, features), F32),
        dummy=sem(1), w_sem=sem(4), kin_send=sem(3 * groups), kin_recv=sem(groups, QUAD),
        misc_send=sem(2 + groups), misc_recv=sem(groups, QUAD), pack_send=sem(3), pack_recv=sem(QUAD),
        early_send=sem(QUAD, groups), early_recv=sem(members), fwd_send=sem(groups, 2), fwdm_send=sem(groups, 2), query_send=sem(groups, 2), att_send=sem(groups, 2, pieces),
        chain_send=sem(2), chain_recv=sem(1), across_recv=sem(1), gsum_send=sem(members), gsum_recv=sem(members),
        late_send=sem(pieces, QUAD, groups), late_recv=sem(members, pieces),
        ret_send=sem(QUAD), ret_recv=sem(QUAD), gp_send=sem(planes), gp_recv=sem(planes),
        up_send=sem(pieces, planes), up_recv=sem(pieces, planes),
        down_send=sem(pieces, planes), down_recv=sem(pieces, planes),
        fin_send=sem(3, pieces), fin_recv=sem(QUAD, pieces),
    )
    names = ["slot", "offset", "mem", "frames", "cot", "bias", "gain", "wq_hbm", "wk_hbm", "wv_hbm", "wo_hbm"]
    names = names + ["grad", "out", "gain_out"] + list(scratch)
    vmem = pl.BlockSpec(memory_space=pltpu.VMEM)
    smem = pl.BlockSpec(memory_space=pltpu.SMEM)
    hbm = pl.BlockSpec(memory_space=pl.ANY)
    grad, weights, gain = pl.pallas_call(
        functools.partial(quad_kernel, owners, groups, heads, tuple(names)),
        out_shape=(
            sds((rows, features), F32), sds((QUAD, part, width), F32), sds((features // 128, 128), F32),
        ),
        in_specs=[smem, smem] + [vmem] * 5 + [hbm] * 4,
        out_specs=(vmem,) * 3,
        scratch_shapes=list(scratch.values()),
        compiler_params=pltpu.CompilerParams(collective_id=0, has_side_effects=True, vmem_limit_bytes=58 * 1024 * 1024),
        name="quad",
    )(
        slot_used[0, 0], start_offset[0], memory[0, 0, 0], frames[0, 0, 0], mem_cot[0, 0, 0],
        key_bias[0, 0, 0][:, None, :], norm_gain.reshape(features // 128, 128), w_query, w_key, w_value, w_out,
    )
    matrix = sds((part, width), F32)
    grad, query, key, value, out, gain = pl.pallas_call(
        hand_over,
        out_shape=(sds((rows, features), F32), matrix, matrix, matrix, matrix, sds((features // 128, 128), F32)),
        in_specs=[vmem] * 3,
        out_specs=(vmem,) * 6,
        name="hand_over",
    )(grad, weights, gain)
    return (grad[None, None, None], query, key, value, out, gain.reshape(features))


def on_device(
    memory, frames, mem_cot, slot_used, key_bias, start_offset, norm_gain, w_query, w_key, w_value, w_out
):
    owners = lax.axis_size("tm")
    groups = lax.axis_size("video")
    position = lax.axis_index("tm")
    streams, rows, features = memory.shape[2:]
    length = frames.shape[3]
    heads = key_bias.shape[3]
    if quad_fits(owners, groups, heads, rows, length, features):
        return quad_call(
            memory, frames, mem_cot, slot_used, key_bias, start_offset, norm_gain, w_query, w_key, w_value, w_out
        )
    members = 2 * groups
    chips = owners // 2
    bits = chips.bit_length() - 1
    width = features // groups
    keyin = key_rows(frames[0, 0, 0], start_offset[0, 0], position)
    vmem = pl.BlockSpec(memory_space=pltpu.VMEM)
    smem = pl.BlockSpec(memory_space=pltpu.SMEM)
    sds = jax.ShapeDtypeStruct
    pw = 128 if width % 128 == 0 else width
    pieces = 2 * (width // pw)
    dma = pltpu.SemaphoreType.DMA
    grad, weights, gain = pl.pallas_call(
        functools.partial(whole_kernel, owners, groups, heads),
        out_shape=(
            sds((rows, features), F32),
            sds((4, features // owners, width), F32),
            sds((1, features), F32),
        ),
        in_specs=[smem] + [vmem] * 9,
        out_specs=(vmem,) * 3,
        scratch_shapes=[
            pltpu.VMEM((members, length, features), F32),
            pltpu.VMEM((members, rows, features), F32),
            pltpu.VMEM((2, groups, length, width), F32),
            pltpu.VMEM((2, groups, rows, width), F32),
            pltpu.VMEM((1, features), F32),
            pltpu.VMEM((rows, features), F32),
            pltpu.VMEM((2, rows, features), F32),
            pltpu.VMEM((rows, heads * length), F32),
            pltpu.VMEM((rows, heads * length), BF16),
            pltpu.VMEM((heads // 2, 2 * length, 2 * features // heads), BF16),
            pltpu.VMEM((heads // 2, 2 * length, 2 * features // heads), BF16),
            pltpu.VMEM((rows, features), BF16),
            pltpu.VMEM((rows, features), BF16),
            pltpu.VMEM((rows, heads * length), BF16),
            pltpu.VMEM((rows, features), BF16),
            pltpu.VMEM((rows, features), BF16),
            pltpu.VMEM((rows, features), F32),
            pltpu.VMEM((rows, 128), F32),
            pltpu.VMEM((features, features), BF16),
            pltpu.VMEM((features, features), BF16),
            dma((CHUNKS,)), dma((CHUNKS,)), dma((2, members)), dma((2, members)),
            pltpu.VMEM((members, length, width), F32),
            pltpu.VMEM((members, rows, width), F32),
            pltpu.VMEM((features, members * length), BF16),
            pltpu.VMEM((features, members * rows), BF16),
            pltpu.VMEM((pieces, features, pw), F32),
            pltpu.VMEM((pieces, features // owners, pw), F32),
            pltpu.VMEM((members, 1, features), F32),
            pltpu.VMEM((bits + 1, 1, features), F32),
            pltpu.VMEM((max(bits, 1), 1, features), F32),
        ]
        + [pltpu.VMEM((pieces, features >> (s + 1), pw), F32) for s in range(bits)]
        + [
            dma((3, members)), dma((3, members)), dma((pieces, bits)), dma((pieces, bits)),
            dma((bits,)), dma((bits,)), dma((pieces,)), dma((pieces,)),
        ],
        compiler_params=pltpu.CompilerParams(collective_id=0, has_side_effects=True, vmem_limit_bytes=58 * 1024 * 1024),
        name="whole",
    )(
        slot_used[0, 0], memory[0, 0, 0], keyin, mem_cot[0, 0, 0], key_bias[0, 0, 0],
        norm_gain[None, :], w_query, w_key, w_value, w_out,
    )
    return (grad[None, None, None], weights[1], weights[2], weights[3], weights[0], gain[0])


def solution(mesh):
    return jax.shard_map(
        on_device,
        mesh=mesh,
        in_specs=(
            P("video", "tm", None, None, None),
            P("video", "tm", None, None, None),
            P("video", "tm", None, None, None),
            P("video", "tm", None),
            P("video", "tm", None, None, None),
            P("video", None),
            P(),
            P(),
            P(),
            P(),
            P(),
        ),
        out_specs=(
            P("video", "tm", None, None, None),
            P("tm", "video"),
            P("tm", "video"),
            P("tm", "video"),
            P("tm", "video"),
            P(),
        ),
        check_vma=False,
    )
```

```python
import functools
import math
import types

import jax
import jax.numpy as jnp
from jax import lax
from jax.experimental import pallas as pl
from jax.experimental.pallas import tpu as pltpu
from jax.sharding import PartitionSpec as P

NORM_EPSILON = 1e-06
MESH = pl.DeviceIdType.MESH
F32 = jnp.float32
BF16 = jnp.bfloat16
NN = (((1,), (0,)), ((), ()))
NT = (((1,), (1,)), ((), ()))
TN = (((0,), (0,)), ((), ()))
CHUNKS = 4


def dot(left, right, form):
    return lax.dot_general(left, right, form, preferred_element_type=F32)


def key_rows(frame_rows, offset, position):
    length, features = frame_rows.shape
    within = jnp.arange(length, dtype=jnp.int32)
    frame_time = (offset + position * length + within).astype(F32)
    half_width = features // 2
    frequency = 0.0625 * jnp.exp(-math.log(1000.0) * jnp.arange(half_width, dtype=F32) / half_width)
    phases = frame_time[:, None] * frequency
    return frame_rows + jnp.concatenate([jnp.sin(phases), jnp.cos(phases)], axis=-1)


def group_member(groups, g):
    me = lax.axis_index("tm")
    return {"video": lax.div(g, 2), "tm": (me // 2) * 2 + lax.rem(g, 2)}


def whole_kernel(
    owners, groups, heads,
    slot_ref, mem_ref, keyin_ref, cot_ref, bias_ref, gain_ref, wq_ref, wk_ref, wv_ref, wo_ref,
    grad_ref, out_ref, gain_out_ref,
    a1_ref, a2_ref, b1_ref, b2_ref, gsum_ref,
    incoming, mine, prob, half, kbd, vbd, qp, att_all, sg_all, og_all, qg_all, unit_ref, inv_ref, wot, wqt,
    chain_send, chain_recv, a_send, a_recv,
    *reduce_scratch,
):
    me = lax.axis_index("tm")
    vid = lax.axis_index("video")
    chips = owners // 2
    bits = chips.bit_length() - 1
    chip, core = me // 2, lax.rem(me, 2)
    peers = [chip + (1 - 2 * lax.rem(lax.div(chip, 2 ** b), 2)) * 2 ** b for b in range(bits)]
    rows, features = mem_ref.shape
    length = keyin_ref.shape[0]
    head = features // heads
    pairs = heads // 2
    pw = 2 * head
    members = 2 * groups
    g_me = vid * 2 + lax.rem(me, 2)
    scale = head ** (-0.5)

    barrier = pltpu.get_barrier_semaphore()
    for off in range(1, members):
        pl.semaphore_signal(barrier, inc=1, device_id=group_member(groups, lax.rem(g_me + off, members)), device_id_type=MESH)

    for peer in peers:
        pl.semaphore_signal(barrier, inc=1, device_id={"tm": peer * 2 + core}, device_id_type=MESH)

    @pl.when(me > 0)
    def _():
        pl.semaphore_signal(barrier, inc=1, device_id={"tm": me - 1}, device_id_type=MESH)

    @pl.when(me < owners - 1)
    def _():
        pl.semaphore_signal(barrier, inc=1, device_id={"tm": me + 1}, device_id_type=MESH)

    ends = jnp.where(me > 0, 1, 0) + jnp.where(me < owners - 1, 1, 0)
    pl.semaphore_wait(barrier, members - 1 + bits + ends)

    def a_copy(which, src, dst, off):
        g = lax.rem(g_me + off, members)
        return pltpu.make_async_remote_copy(
            src_ref=src, dst_ref=dst.at[g_me], send_sem=a_send.at[which, off], recv_sem=a_recv.at[which, g_me],
            device_id=group_member(groups, g), device_id_type=MESH,
        )

    for off in range(1, members):
        a_copy(0, keyin_ref, a1_ref, off).start()
    a1_ref[g_me] = keyin_ref[...]

    mem = mem_ref[...].astype(F32)
    inv = lax.rsqrt(jnp.mean(mem * mem, axis=-1, keepdims=True) + NORM_EPSILON)
    unit = mem * inv
    unit_ref[...] = unit
    inv_ref[...] = jnp.broadcast_to(inv, inv_ref.shape)
    normed = (unit * gain_ref[...]).astype(BF16)
    mine[1] = normed.astype(F32)
    keyin = keyin_ref[...].astype(BF16)
    query = dot(normed, wq_ref[...], NN).astype(BF16)
    qp[...] = query
    kp = dot(keyin, wk_ref[...], NN).astype(BF16)
    vp = dot(keyin, wv_ref[...], NN).astype(BF16)
    low = lax.broadcasted_iota(jnp.int32, (length, pw), 1) < head
    zero = jnp.zeros((length, pw), BF16)
    for p in range(pairs):
        kk = kp[:, p * pw:(p + 1) * pw]
        vv = vp[:, p * pw:(p + 1) * pw]
        kbd[p, :length] = jnp.where(low, kk, zero)
        kbd[p, length:] = jnp.where(low, zero, kk)
        vbd[p, :length] = jnp.where(low, vv, zero)
        vbd[p, length:] = jnp.where(low, zero, vv)
    wot[...] = jnp.transpose(wo_ref[...])
    wqt[...] = jnp.transpose(wq_ref[...])
    scores = [dot(query[:, p * pw:(p + 1) * pw], kbd[p], NT) for p in range(pairs)]
    for p in range(pairs):
        halves = []
        for q in range(2):
            h = 2 * p + q
            s = scores[p][:, q * length:(q + 1) * length] * scale + bias_ref[h:h + 1, :]
            e = jnp.exp(s - jnp.max(s, axis=-1, keepdims=True))
            pr = e / jnp.sum(e, axis=-1, keepdims=True)
            prob[:, h * length:(h + 1) * length] = pr
            halves.append(pr.astype(BF16))
        both = jnp.concatenate(halves, axis=-1)
        half[:, p * 2 * length:(p + 1) * 2 * length] = both
        mine[0, :, p * pw:(p + 1) * pw] = dot(both, vbd[p], NN).astype(BF16).astype(F32)

    for off in range(1, members):
        g = lax.rem(g_me + off, members)
        a_copy(1, mine.at[lax.rem(g, 2)], a2_ref, off).start()
    a2_ref[g_me] = mine[lax.rem(me, 2)]

    live = slot_ref[0].astype(F32)
    step = rows // CHUNKS

    def chain_copy(c):
        return pltpu.make_async_remote_copy(
            src_ref=grad_ref.at[pl.ds(c * step, step)], dst_ref=incoming.at[pl.ds(c * step, step)],
            send_sem=chain_send.at[c], recv_sem=chain_recv.at[c],
            device_id={"tm": jnp.maximum(me - 1, 0)}, device_id_type=MESH,
        )

    @pl.when(me == owners - 1)
    def _():
        incoming[...] = jnp.zeros_like(incoming)

    gain_total = jnp.zeros((1, features), F32)
    for c in range(CHUNKS):
        r = slice(c * step, (c + 1) * step)

        @pl.when(me < owners - 1)
        def _():
            chain_copy(c).wait_recv()

        grad_in = incoming[r, :] + cot_ref[r, :].astype(F32)
        og = (live * grad_in).astype(BF16)
        att = dot(og, wot[...], NN).astype(BF16)
        prob_grads = [dot(att[:, p * pw:(p + 1) * pw], vbd[p], NT) for p in range(pairs)]
        query_grads = []
        score_grads = []
        for p in range(pairs):
            for q in range(2):
                h = 2 * p + q
                pg = prob_grads[p][:, q * length:(q + 1) * length]
                pr = prob[r, h * length:(h + 1) * length]
                inner = jnp.sum(pr * pg, axis=-1, keepdims=True)
                score_grads.append((pr * (pg - inner) * scale).astype(BF16))
            query_grads.append(dot(jnp.concatenate(score_grads[-2:], axis=-1), kbd[p], NN).astype(BF16))
        qg = jnp.concatenate(query_grads, axis=-1)
        ng = dot(qg, wqt[...], NN)
        un = unit_ref[r, :]
        gain_total = gain_total + jnp.sum(ng * un, axis=0, keepdims=True)
        sc = ng * gain_ref[...]
        grad_ref[r, :] = grad_in + inv_ref[r, 0:1] * (sc - un * jnp.mean(sc * un, axis=-1, keepdims=True))

        @pl.when(me > 0)
        def _():
            chain_copy(c).start()

        og_all[r, :] = og
        att_all[r, :] = att
        qg_all[r, :] = qg
        for h in range(heads):
            sg_all[r, h * length:(h + 1) * length] = score_grads[h]

    gsum_ref[...] = gain_total

    width = features // groups
    lowr = lax.broadcasted_iota(jnp.int32, (rows, pw), 1) < head
    zr = jnp.zeros((rows, pw), BF16)

    def put(out, which, p, value):
        for v in range(groups):
            lo, hi = max(p * pw, v * width), min((p + 1) * pw, (v + 1) * width)
            if lo < hi:
                out[which, v, :, lo - v * width:hi - v * width] = value[:, lo - p * pw:hi - p * pw]

    for p in range(pairs):
        for which, (left_ref, right_ref) in enumerate(((sg_all, qp), (half, att_all))):
            right = right_ref[:, p * pw:(p + 1) * pw]
            right = jnp.concatenate([jnp.where(lowr, right, zr), jnp.where(lowr, zr, right)], axis=0)
            base = 2 * p * length
            left = jnp.concatenate([left_ref[:, base:base + length], left_ref[:, base + length:base + 2 * length]], axis=0)
            put(b1_ref, which, p, dot(left, right, TN).astype(BF16).astype(F32))
        put(b2_ref, 0, p, og_all[:, p * pw:(p + 1) * pw].astype(F32))
        put(b2_ref, 1, p, qg_all[:, p * pw:(p + 1) * pw].astype(F32))

    def a_arrive():
        for off in range(1, members):
            g = lax.rem(g_me + members - off, members)
            for which, dst in ((0, a1_ref), (1, a2_ref)):
                a_copy(which, dst.at[g_me], dst, off).wait_send()
                pltpu.make_async_remote_copy(
                    src_ref=dst.at[g], dst_ref=dst.at[g], send_sem=a_send.at[which, off], recv_sem=a_recv.at[which, g],
                    device_id=group_member(groups, g), device_id_type=MESH,
                ).wait_recv()

    reduce_part(
        owners, groups, peers, a_arrive, a1_ref, a2_ref, b1_ref, b2_ref, gsum_ref, out_ref, gain_out_ref, *reduce_scratch
    )

    @pl.when(me > 0)
    def _():
        for c in range(CHUNKS):
            chain_copy(c).wait_send()


def reduce_part(
    owners, groups, peers, a_arrive,
    a1_ref, a2_ref, b1_ref, b2_ref, gsum_ref,
    out_ref, gain_ref,
    s1, s2, t1, t2, acc, final, gslot, gacc, gland, *rest,
):
    me = lax.axis_index("tm")
    vid = lax.axis_index("video")
    members = 2 * groups
    chips = owners // 2
    bits = chips.bit_length() - 1
    lands = rest[:bits]
    b_send, b_recv, r_send, r_recv, q_send, q_recv, f_send, f_recv = rest[bits:]
    chip, core = me // 2, lax.rem(me, 2)
    g_me = vid * 2 + core
    pieces, features, pw = acc.shape
    per = pieces // 2
    block = features // chips
    part = block // 2
    scale = 1.0 / (owners * groups)
    length, rows = a1_ref.shape[1], a2_ref.shape[1]

    def b_copy(which, off):
        g = lax.rem(g_me + off, members)
        v, c = lax.div(g, 2), lax.rem(g, 2)
        src, dst = ((b1_ref.at[c, v], s1), (b2_ref.at[c, v], s2), (gsum_ref, gslot))[which]
        return pltpu.make_async_remote_copy(
            src_ref=src, dst_ref=dst.at[g_me], send_sem=b_send.at[which, off], recv_sem=b_recv.at[which, g_me],
            device_id=group_member(groups, g), device_id_type=MESH,
        )

    def b_arrive(which, off):
        g = lax.rem(g_me + members - off, members)
        dst = (s1, s2, gslot)[which]
        return pltpu.make_async_remote_copy(
            src_ref=dst.at[g], dst_ref=dst.at[g], send_sem=b_send.at[which, off], recv_sem=b_recv.at[which, g],
            device_id=group_member(groups, g), device_id_type=MESH,
        )

    for which in (2, 1, 0):
        for off in range(1, members):
            b_copy(which, off).start()
    s1[g_me] = b1_ref[core, vid]
    s2[g_me] = b2_ref[core, vid]
    gslot[g_me] = gsum_ref[...]
    a_arrive()
    for g in range(members):
        t1[:, g * length:(g + 1) * length] = jnp.transpose(a1_ref[g]).astype(BF16)
    for g in range(0, members, 2):
        both = jnp.concatenate([a2_ref[g], a2_ref[g + 1]], axis=0)
        t2[:, g * rows:(g + 2) * rows] = jnp.transpose(both).astype(BF16)

    order = [int(format(i, "b").zfill(bits)[::-1], 2) if bits else 0 for i in range(chips)]

    def products(which):
        slots, left = ((s2, t2), (s1, t1))[which]
        for off in range(1, members):
            b_arrive(1 - which, off).wait_recv()
        for i in range(per):
            right = slots[:, :, i * pw:(i + 1) * pw].reshape(left.shape[1], pw).astype(BF16)
            value = dot(left[...], right, NN)
            for pos in range(chips):
                k = order[pos]
                acc[which * per + i, pos * block:(pos + 1) * block, :] = value[k * block:(k + 1) * block, :]

    starts = []
    lo = 0
    for s in range(bits):
        span = features >> (s + 1)
        bit = lax.rem(lax.div(chip, 2 ** s), 2)
        starts.append((lo + (1 - bit) * span, lo + bit * span, span, peers[s]))
        lo = lo + bit * span

    def r_copy(p, s):
        give, _, span, peer = starts[s]
        return pltpu.make_async_remote_copy(
            src_ref=acc.at[p, pl.ds(pl.multiple_of(give, 8), span)], dst_ref=lands[s].at[p],
            send_sem=r_send.at[p, s], recv_sem=r_recv.at[p, s],
            device_id={"tm": peer * 2 + core}, device_id_type=MESH,
        )

    def g_copy(s):
        return pltpu.make_async_remote_copy(
            src_ref=gacc.at[s], dst_ref=gland.at[s], send_sem=q_send.at[s], recv_sem=q_recv.at[s],
            device_id={"tm": peers[s] * 2 + core}, device_id_type=MESH,
        )

    def r_finish(p, s):
        _, keep, span, _ = starts[s]
        r_copy(p, s).wait_recv()
        at = pl.ds(pl.multiple_of(keep, 8), span)
        acc[p, at, :] = acc[p, at, :] + lands[s][p]

    def f_copy(p):
        theirs = pl.ds(pl.multiple_of(lo + (1 - core) * part, 8), part)
        return pltpu.make_async_remote_copy(
            src_ref=acc.at[p, theirs], dst_ref=final.at[p], send_sem=f_send.at[p], recv_sem=f_recv.at[p],
            device_id={"tm": chip * 2 + 1 - core}, device_id_type=MESH,
        )

    for wave in range(pieces + bits):
        if wave == 0:
            products(0)
        if wave == per:
            products(1)
        for s in reversed(range(bits + 1)):
            p = wave - s
            if 0 <= p < pieces:
                if s > 0:
                    r_finish(p, s - 1)
                if s < bits:
                    r_copy(p, s).start()
                else:
                    f_copy(p).start()
        if wave == 0:
            for off in range(1, members):
                b_arrive(2, off).wait_recv()
            gacc[0] = jnp.sum(gslot[...], axis=0)
        if 0 < wave <= bits:
            g_copy(wave - 1).wait_recv()
            gacc[wave] = gacc[wave - 1] + gland[wave - 1]
        if wave < bits:
            g_copy(wave).start()

    mine_rows = pl.ds(pl.multiple_of(lo + core * part, 8), part)
    for p in range(pieces):
        which, i = p // per, p % per
        cols = slice(i * pw, (i + 1) * pw)
        out_ref[2 * which + core, :, cols] = acc[p, mine_rows, :] * scale
    for p in range(pieces):
        which, i = p // per, p % per
        cols = slice(i * pw, (i + 1) * pw)
        f_copy(p).wait_recv()
        out_ref[2 * which + 1 - core, :, cols] = final[p] * scale

    gain_ref[...] = gacc[bits] * scale
    for s in range(bits):
        g_copy(s).wait_send()
    for which in range(3):
        for off in range(1, members):
            b_copy(which, off).wait_send()
    for p in range(pieces):
        for s in range(bits):
            r_copy(p, s).wait_send()
        f_copy(p).wait_send()


QUAD = 4


def xor_bits(value, bits):
    high, low = lax.div(value, 2), lax.rem(value, 2)
    if bits & 2:
        high = 1 - high
    if bits & 1:
        low = 1 - low
    return high * 2 + low


def encoded(frames_ref, first_time, put):
    length, features = frames_ref.shape
    half_width = features // 2
    index = lax.broadcasted_iota(jnp.int32, (1, half_width), 1).astype(F32)
    frequency = 0.0625 * jnp.exp(-math.log(1000.0) * index / half_width)
    groups_of = length // 8
    outer = first_time + 8 * lax.broadcasted_iota(jnp.int32, (groups_of, half_width), 0)
    inner = lax.broadcasted_iota(jnp.int32, (8, half_width), 0)
    outer, inner = outer.astype(F32) * frequency, inner.astype(F32) * frequency
    so, co, si, ci = jnp.sin(outer), jnp.cos(outer), jnp.sin(inner), jnp.cos(inner)
    for a in range(groups_of):
        s, c = so[a:a + 1], co[a:a + 1]
        r = slice(a * 8, (a + 1) * 8)
        put(r, slice(0, half_width), frames_ref[r, :half_width] + (s * ci + c * si))
        put(r, slice(half_width, features), frames_ref[r, half_width:] + (c * ci - s * si))


def quad_kernel(owners, groups, heads, names, *refs):
    b = types.SimpleNamespace(**dict(zip(names, refs)))
    me = lax.axis_index("tm")
    vid = lax.axis_index("video")
    planes = owners // QUAD
    plane, q = lax.div(me, QUAD), lax.rem(me, QUAD)
    y = lax.div(q, 2)
    members = groups * QUAD
    mine = vid * QUAD + q
    rows, features = b.mem.shape
    length = b.frames.shape[0]
    head = features // heads
    pairs = heads // 2
    pw = 2 * head
    blk = rows // QUAD
    pieces = pairs // groups
    span = features // planes
    part = features // owners
    scale = head ** (-0.5)
    q1, q2, q3 = xor_bits(q, 1), xor_bits(q, 2), xor_bits(q, 3)
    core = lax.rem(q, 2)
    last, rest = plane == planes - 1, plane < planes - 1
    last_low = jnp.logical_and(last, y == 0)
    last_high = jnp.logical_and(last, y == 1)
    own_half, other_half = pl.ds(2 * core, 2), pl.ds(2 * (1 - core), 2)
    pending = []

    def dev(v, at, qq):
        return {"video": v, "tm": at * QUAD + qq}

    def member(g):
        return dev(lax.div(g, QUAD), plane, lax.rem(g, QUAD))

    def remote(src, dst, ss, rs, to):
        return pltpu.make_async_remote_copy(
            src_ref=src, dst_ref=dst, send_sem=ss, recv_sem=rs, device_id=to, device_id_type=MESH
        )

    def guarded(cond, act):
        if cond is None:
            act()
        else:
            pl.when(cond)(act)

    def send(cond, *copy):
        guarded(cond, lambda: remote(*copy).start())
        pending.append((cond, copy))

    def arrived(dst, rs):
        remote(dst, dst, b.dummy.at[0], rs, dev(vid, plane, q1)).wait_recv()

    weights = [(b.wq_hbm, b.wq), (b.wk_hbm, b.wk), (b.wv_hbm, b.wv), (b.wo_hbm, b.wo)]

    def load(k):
        return pltpu.make_async_copy(weights[k][0], weights[k][1], b.w_sem.at[k])

    for k in (1, 2, 0, 3):
        load(k).start()

    barrier = pltpu.get_barrier_semaphore()
    for off in range(1, members):
        pl.semaphore_signal(barrier, inc=1, device_id=member(lax.rem(mine + off, members)), device_id_type=MESH)
    for off in range(1, planes):
        pl.semaphore_signal(
            barrier, inc=1, device_id=dev(vid, lax.rem(plane + off, planes), q), device_id_type=MESH
        )

    @pl.when(plane == planes - 2)
    def _():
        pl.semaphore_signal(
            barrier, inc=1, device_id=dev(vid, jnp.minimum(plane + 1, planes - 1), y), device_id_type=MESH
        )

    def put_key(r, cols, value):
        b.kin[vid, q, r, cols] = value

    encoded(b.frames, b.offset[0] + me * length, put_key)
    for h in range(heads):
        b.misc[vid, q, h:h + 1, :] = b.bias[h]
    b.misc[vid, q, heads:heads + 1, :] = jnp.zeros((1, length), F32) + b.slot[0].astype(F32)
    for j in range(QUAD):
        b.pack_out[j, :blk] = b.mem[j * blk:(j + 1) * blk, :].astype(F32)
        b.pack_out[j, blk:] = b.cot[j * blk:(j + 1) * blk, :].astype(F32)

    @pl.when(rest)
    def _():
        b.pack[q] = b.pack_out[q]

    @pl.when(last)
    def _():
        b.pack[own_half] = b.pack_out[own_half]

    pl.semaphore_wait(barrier, members - 1 + planes - 1 + jnp.where(last_low, 2 if planes > 1 else 0, 0))

    def send_key(cond, slot, sem, to):
        send(cond, b.kin.at[vid, slot], b.kin.at[vid, slot], b.kin_send.at[sem], b.kin_recv.at[vid, slot], to)

    def send_misc(cond, sem, to):
        send(cond, b.misc.at[vid, q], b.misc.at[vid, q], b.misc_send.at[sem], b.misc_recv.at[vid, q], to)

    send_key(rest, q, 0, dev(vid, plane, q2))
    send_key(None, q, 1, dev(vid, plane, q1))
    for k, other in ((0, q1), (1, q2), (2, q3)):
        to = dev(vid, plane, other)
        send_misc(None, k, to)
        send(rest, b.pack_out.at[other], b.pack.at[q], b.pack_send.at[k], b.pack_recv.at[q], to)
    send(
        last, b.pack_out.at[other_half], b.pack.at[own_half], b.pack_send.at[0], b.pack_recv.at[q],
        dev(vid, plane, q1),
    )
    for off in range(1, groups):
        send_key(y == 0, q, 3 * off, dev(lax.rem(vid + off, groups), plane, q))
        send_misc(None, 2 + off, dev(lax.rem(vid + off, groups), plane, core))

    low = lax.broadcasted_iota(jnp.int32, (length, pw), 1) < head
    zero = jnp.zeros((length, pw), BF16)

    def project(slot):
        keyin = b.kin[vid, slot].astype(BF16)
        kp = dot(keyin, b.wk[...], NN).astype(BF16)
        vp = dot(keyin, b.wv[...], NN).astype(BF16)
        for p in range(pairs):
            kk = kp[:, p * pw:(p + 1) * pw]
            vv = vp[:, p * pw:(p + 1) * pw]
            b.kbd[slot, p, :length] = jnp.where(low, kk, zero)
            b.kbd[slot, p, length:] = jnp.where(low, zero, kk)
            b.vbd[slot, p, :length] = jnp.where(low, vv, zero)
            b.vbd[slot, p, length:] = jnp.where(low, zero, vv)

    for k in (1, 2, 0, 3):
        load(k).wait()
    project(q)
    b.wot[...] = jnp.transpose(b.wo[...])
    b.wqt[...] = jnp.transpose(b.wq[...])
    arrived(b.kin.at[vid, q1], b.kin_recv.at[vid, q1])
    project(q1)
    for other in (q1, q2, q3):
        arrived(b.misc.at[vid, other], b.misc_recv.at[vid, other])

    def pass_on(cond):
        guarded(cond, lambda: arrived(b.kin.at[vid, q2], b.kin_recv.at[vid, q2]))
        send_key(cond, q2, 2, dev(vid, plane, q1))

    def cross(cond):
        for off in range(1, groups):
            send_key(cond, q, 3 * off + 1, dev(lax.rem(vid + off, groups), plane, core))

    pass_on(rest)

    @pl.when(rest)
    def _():
        project(q2)
        arrived(b.kin.at[vid, q3], b.kin_recv.at[vid, q3])
        project(q3)
        for other in (q1, q2, q3):
            arrived(b.pack.at[other], b.pack_recv.at[other])

    @pl.when(last)
    def _():
        arrived(b.pack.at[other_half], b.pack_recv.at[q1])

    cross(jnp.logical_and(rest, y == 1))

    gain = jnp.concatenate([b.gain[k:k + 1, :] for k in range(b.gain.shape[0])], axis=-1)
    mem = jnp.concatenate([b.pack[j, :blk] for j in range(QUAD)], axis=0)
    inv = lax.rsqrt(jnp.mean(mem * mem, axis=-1, keepdims=True) + NORM_EPSILON)
    unit = mem * inv
    b.unit[...] = unit
    b.inv[...] = jnp.broadcast_to(inv, b.inv.shape)
    normed = (unit * gain).astype(BF16)
    b.normed[...] = normed.astype(F32)
    query = dot(normed, b.wq[...], NN).astype(BF16)
    for p in range(pairs):
        b.qp[p] = query[:, p * pw:(p + 1) * pw].astype(F32)
    def attend(r, slot):
        scores = [dot(query[r, p * pw:(p + 1) * pw], b.kbd[slot, p], NT) for p in range(pairs)]
        for p in range(pairs):
            halves = []
            for k in range(2):
                h = 2 * p + k
                sc = scores[p][:, k * length:(k + 1) * length] * scale + b.misc[vid, slot, h:h + 1, :]
                e = jnp.exp(sc - jnp.max(sc, axis=-1, keepdims=True))
                pr = e / jnp.sum(e, axis=-1, keepdims=True)
                b.prob[r, h * length:(h + 1) * length] = pr
                halves.append(pr.astype(BF16))
            both = jnp.concatenate(halves, axis=-1)
            b.attended[r, p * pw:(p + 1) * pw] = dot(both, b.vbd[slot, p], NN).astype(BF16).astype(F32)

    singles = [(slice(j * blk, (j + 1) * blk), (j,)) for j in reversed(range(QUAD))]
    doubles = [(slice(2 * a * blk, 2 * (a + 1) * blk), (2 * a, 2 * a + 1)) for a in (1, 0)]

    @pl.when(rest)
    def _():
        for r, (j,) in singles:
            attend(r, j)

    @pl.when(last)
    def _():
        for r, (k, _) in doubles:
            attend(r, 2 * y + k // 2)

    def qp_of(v):
        return b.qp.at[pl.ds(v * pieces, pieces)]

    for off in range(groups):
        v = lax.rem(vid + off, groups)
        send(
            y != 0 if off == 0 else None, qp_of(v), b.query.at[mine], b.early_send.at[0, off],
            b.early_recv.at[mine], dev(v, plane, core),
        )
    for off in range(groups):
        v = lax.rem(vid + off, groups)
        for role, src in ((2, b.attended), (3, b.normed)):
            send(
                q != role if off == 0 else None, src, b.early.at[mine], b.early_send.at[role, off],
                b.early_recv.at[mine], dev(v, plane, role),
            )

    @pl.when(y == 0)
    def _():
        b.query[mine] = qp_of(vid)[...]

    for role, src in ((2, b.attended), (3, b.normed)):
        @pl.when(q == role)
        def _():
            b.early[mine] = src[...]

    def same_core(side):
        return [
            (off, e, lax.rem(vid + off, groups) * QUAD + 2 * e + side) for off in range(groups) for e in range(2)
        ]

    def share(ref, index, recv, ss, stage):
        for off, e, g in same_core(core):
            at = ref.at[(g, *index)]
            copy = remote(at, at, ss.at[(off, e, *index)], recv.at[(g, *index)], dev(vid, plane, q1))
            if stage == 0 and (off, e) != (0, 0):
                arrived(at, recv.at[(g, *index)])
            if stage == 0:
                copy.start()
            if stage == 2:
                copy.wait_send()
        if stage == 1:
            for off, e, g in same_core(1 - core):
                arrived(ref.at[(g, *index)], recv.at[(g, *index)])

    def forward(off, k, v, slot):
        at, to = b.kin.at[v, slot], dev(vid, plane, q1)
        small = b.misc.at[v, slot]
        return (
            remote(at, at, b.fwd_send.at[off, k], b.kin_recv.at[v, slot], to),
            remote(small, small, b.fwdm_send.at[off, k], b.misc_recv.at[v, slot], to),
        )

    def gather(ref, v, i, j):
        parts = []
        for k in range(QUAD):
            g = v * QUAD + jnp.where(last, 2 * (j // 2) + k // 2, k)
            at = jnp.where(last, (2 * (j % 2) + k % 2) * blk, j * blk)
            parts.append(ref[g, i, pl.ds(pl.multiple_of(at, blk), blk), :])
        return jnp.concatenate(parts, axis=0).astype(BF16)

    half_cols = pl.ds(pl.multiple_of(vid * pieces * pw, 128), pieces * pw)

    def apart(value, p, out, g):
        vv = value[:, p * pw:(p + 1) * pw]
        out[g, p, :length] = jnp.where(low, vv, zero)
        out[g, p, length:] = jnp.where(low, zero, vv)

    def prepare(v):
        @pl.loop(0, QUAD // 2)
        def _(n):
            pair = [v * QUAD + 2 * n + k for k in range(2)]
            keyin = jnp.concatenate([b.kin[v, 2 * n + k].astype(BF16) for k in range(2)], axis=0)
            at = pl.ds(pl.multiple_of(pair[0] * length, 128), 2 * length)
            b.left[:, at] = jnp.transpose(keyin)

            def halves_of(weight, out):
                value = dot(keyin, weight[:, half_cols], NN).astype(BF16)
                for k in range(2):
                    for p in range(pieces):
                        apart(value[k * length:(k + 1) * length], p, out, pair[k])

            halves_of(b.wk, b.khalf)
            pl.when(q == 0)(lambda: halves_of(b.wv, b.vhalf))

    @pl.when(jnp.logical_and(y == 0, plane < planes // 2))
    def _():
        prepare(vid)

    def early_low():
        guarded(last, lambda: arrived(b.kin.at[vid, q3], b.kin_recv.at[vid, q3]))
        for off in range(1, groups):
            v = lax.rem(vid + off, groups)
            for k, slot in ((0, q), (1, q2)):
                arrived(b.kin.at[v, slot], b.kin_recv.at[v, slot])
                arrived(b.misc.at[v, slot], b.misc_recv.at[v, slot])
                for copy in forward(off, k, v, slot):
                    copy.start()
        share(b.query, (), b.early_recv, b.query_send, 0)

        @pl.when(plane >= planes // 2)
        def _():
            prepare(vid)

        for off in range(1, groups):
            v = lax.rem(vid + off, groups)
            for slot in (q1, q3):
                arrived(b.kin.at[v, slot], b.kin_recv.at[v, slot])
                arrived(b.misc.at[v, slot], b.misc_recv.at[v, slot])
            prepare(v)
        share(b.query, (), b.early_recv, b.query_send, 1)

        @pl.loop(0, pieces)
        def _(i):
            clips = [(v, j) for v in range(groups) for j in range(QUAD)]
            found = []
            for v, j in clips:
                scores = dot(gather(b.query, v, i, j), b.khalf[v * QUAD + j, i], NT)
                for k in range(2):
                    h = 2 * (vid * pieces + i) + k
                    sc = scores[:, k * length:(k + 1) * length] * scale + b.misc[v, j, pl.ds(h, 1), :]
                    e = jnp.exp(sc - jnp.max(sc, axis=-1, keepdims=True))
                    found.append(e / jnp.sum(e, axis=-1, keepdims=True))
            for n, (v, j) in enumerate(clips):
                for k in range(2):
                    b.wide[v * QUAD + j, i, :, k * length:(k + 1) * length] = found[2 * n + k]

    def early_high():
        for off in range(1, members):
            g = lax.rem(mine + off, members)
            arrived(b.early.at[g], b.early_recv.at[g])
        for g in range(0, members, 2):
            both = jnp.concatenate([b.early[g], b.early[g + 1]], axis=0)
            b.left[:, g * rows:(g + 2) * rows] = jnp.transpose(both.astype(BF16))

    below = jnp.maximum(plane - 1, 0)
    single_to = (
        jnp.logical_and(rest, plane > 0),
        (b.passed.at[0], b.incoming, b.chain_send.at[0], b.chain_recv.at[0], dev(vid, below, q)),
    )
    across_to = (
        last_high,
        (b.passed.at[pl.ds(0, 2)], b.across, b.chain_send.at[0], b.across_recv.at[0], dev(vid, plane, q2)),
    )
    double_to = [
        (
            jnp.logical_and(last_low, plane > 0),
            (b.passed.at[k], b.incoming, b.chain_send.at[k], b.chain_recv.at[0], dev(vid, below, 2 * core + k)),
        )
        for k in range(2)
    ]

    def step(r, blocks, slot, carried, outgoing):
        grad_in = carried + jnp.concatenate([b.pack[k, blk:] for k in blocks], axis=0)
        live = jnp.concatenate([b.misc[vid, slot, heads:heads + 1, :]] * (features // length), axis=-1)
        og = (live * grad_in).astype(BF16)
        att = dot(og, b.wot[...], NN).astype(BF16)
        prob_grads = [dot(att[:, p * pw:(p + 1) * pw], b.vbd[slot, p], NT) for p in range(pairs)]
        query_grads = []
        for p in range(pairs):
            halves = []
            for k in range(2):
                h = 2 * p + k
                pg = prob_grads[p][:, k * length:(k + 1) * length]
                pr = b.prob[r, h * length:(h + 1) * length]
                inner = jnp.sum(pr * pg, axis=-1, keepdims=True)
                halves.append((pr * (pg - inner) * scale).astype(BF16))
            both = jnp.concatenate(halves, axis=-1)
            query_grads.append(dot(both, b.kbd[slot, p], NN).astype(BF16))
        qg = jnp.concatenate(query_grads, axis=-1)
        ng = dot(qg, b.wqt[...], NN)
        un = b.unit[r, :]
        sc = ng * gain
        carried = grad_in + b.inv[r, 0:1] * (sc - un * jnp.mean(sc * un, axis=-1, keepdims=True))
        for n, k in enumerate(blocks):
            b.passed[k] = carried[n * blk:(n + 1) * blk]
        for cond, copy in outgoing:
            pl.when(cond)(lambda: remote(*copy).start())
        for p in range(pairs):
            cols = slice(p * pw, (p + 1) * pw)
            b.att[p, r, :] = att[:, cols].astype(F32)
            b.og[p, r, :] = og[:, cols].astype(F32)
            b.qg[p, r, :] = qg[:, cols].astype(F32)
        return carried, jnp.sum(ng * un, axis=0, keepdims=True)

    pending.extend([single_to, across_to] + double_to)

    @pl.when(rest)
    def _():
        arrived(b.incoming, b.chain_recv.at[0])
        gain_total = jnp.zeros((1, features), F32)
        carried = b.incoming[...]
        for r, (j,) in singles:
            carried, gain_part = step(r, (j,), j, carried, [single_to] if j == 0 else [])
            gain_total = gain_total + gain_part
        b.gsum[mine] = gain_total

    @pl.when(last_high)
    def _():
        b.across[...] = jnp.zeros_like(b.across)

    @pl.when(last_low)
    def _():
        arrived(b.across, b.across_recv.at[0])

    @pl.when(last)
    def _():
        gain_total = jnp.zeros((1, features), F32)
        carried = jnp.concatenate([b.across[0], b.across[1]], axis=0)
        for r, blocks in doubles:
            outgoing = [across_to] + double_to if blocks[0] == 0 else []
            carried, gain_part = step(r, blocks, 2 * y + blocks[0] // 2, carried, outgoing)
            gain_total = gain_total + gain_part
        b.gsum[mine] = gain_total

    send_key(last_high, q, 0, dev(vid, plane, q2))
    cross(last_high)
    for off in range(1, members):
        g = lax.rem(mine + off, members)
        send(None, b.gsum.at[mine], b.gsum.at[mine], b.gsum_send.at[off], b.gsum_recv.at[mine], member(g))

    rounds = [(i, ((0, y != 0, b.att),)) for i in range(pieces)]
    rounds = rounds + [(i, ((2, q != 2, b.og), (3, q != 3, b.qg))) for i in range(pieces)]
    for i, sent in rounds:
        for off in reversed(range(groups)):
            v = lax.rem(vid + off, groups)
            for role, cond, src in sent:
                send(
                    cond if off == 0 else None, src.at[v * pieces + i], b.narrow.at[mine, i],
                    b.late_send.at[i, role, off], b.late_recv.at[mine, i],
                    dev(v, plane, core if role == 0 else role),
                )
    for cond, src in ((y == 0, b.att), (q == 2, b.og), (q == 3, b.qg)):
        @pl.when(cond)
        def _():
            b.narrow[mine] = src[pl.ds(vid * pieces, pieces)]

    for j in range(QUAD):
        send(
            jnp.logical_and(rest, q != j), b.passed.at[j], b.returned.at[q], b.ret_send.at[j], b.ret_recv.at[q],
            dev(vid, plane, j),
        )
    send(
        last, b.passed.at[other_half], b.returned.at[own_half], b.ret_send.at[0], b.ret_recv.at[q],
        dev(vid, plane, q1),
    )
    pass_on(last_low)

    @pl.when(y == 0)
    def _():
        early_low()

    @pl.when(y == 1)
    def _():
        early_high()

    lowr = lax.broadcasted_iota(jnp.int32, (rows, pw), 1) < head
    zr = jnp.zeros((rows, pw), BF16)

    def product(i):
        @pl.when(y == 0)
        def _():
            share(b.narrow, (i,), b.late_recv, b.att_send, 1)

        @pl.when(y == 1)
        def _():
            for off in range(1, members):
                g = lax.rem(mine + off, members)
                arrived(b.narrow.at[g, i], b.late_recv.at[g, i])

        def token_grads(role):
            found = []
            for v in range(groups):
                for j in range(QUAD):
                    g = v * QUAD + j
                    right = att = gather(b.narrow, v, i, j)
                    halves = []
                    if role == 0:
                        right = gather(b.query, v, i, j)
                        prob_grad = dot(att, b.vhalf[g, i], NT)
                    for k in range(2):
                        cols = slice(k * length, (k + 1) * length)
                        pr = b.wide[g, i, :, cols]
                        if role == 0:
                            pg = prob_grad[:, cols]
                            pr = pr * (pg - jnp.sum(pr * pg, axis=-1, keepdims=True)) * scale
                        halves.append(pr.astype(BF16))
                    stacked = jnp.concatenate(halves, axis=0)
                    right = jnp.concatenate([jnp.where(lowr, right, zr), jnp.where(lowr, zr, right)], axis=0)
                    found.append(dot(stacked, right, TN).astype(BF16))
            b.right[...] = jnp.concatenate(found, axis=0)

        for role in range(2):
            pl.when(q == role)(functools.partial(token_grads, role))

        @pl.when(jnp.logical_and(y == 0, i + 1 < pieces))
        def _():
            share(b.narrow, (i + 1,), b.late_recv, b.att_send, 0)

        @pl.when(y == 0)
        def _():
            b.acc[i] = dot(b.left[...], b.right[...], NN)

        @pl.when(y == 1)
        def _():
            right = jnp.concatenate([b.narrow[g, i] for g in range(members)], axis=0).astype(BF16)
            b.acc[i] = dot(b.left[:, :members * rows], right, NN)

    def block(at):
        return pl.ds(pl.multiple_of(at * span, 8), span)

    def flow(i, k, up):
        to = plane + k if up else plane - k
        ok = to < planes if up else to >= 0
        fed = plane > 0 if up else plane < planes - 1
        land, ss, rs = (b.up, b.up_send, b.up_recv) if up else (b.down, b.down_send, b.down_recv)
        to = jnp.clip(to, 0, planes - 1)
        at = block(to)
        step = jnp.clip(plane + 1 if up else plane - 1, 0, planes - 1)

        @pl.when(jnp.logical_and(ok, fed))
        def _():
            arrived(land.at[i, at], rs.at[i, to])
            b.acc[i, at, :] = b.acc[i, at, :] + land[i, at, :]

        return ok, (b.acc.at[i, at], land.at[i, at], ss.at[i, to], rs.at[i, to], dev(vid, step, q))

    def flow_all(i, up, near=1):
        for k in reversed(range(near, planes)):
            ok, copy = flow(i, k, up)
            pl.when(ok)(lambda: remote(*copy).start())

    mean = 1.0 / (owners * groups)

    def settle(i):
        at = block(plane)

        @pl.when(plane < planes - 1)
        def _():
            arrived(b.down.at[i, at], b.down_recv.at[i, plane])
            b.acc[i, at, :] = b.acc[i, at, :] + b.down[i, at, :]

        @pl.when(plane > 0)
        def _():
            arrived(b.up.at[i, at], b.up_recv.at[i, plane])
            b.acc[i, at, :] = b.acc[i, at, :] + b.up[i, at, :]

        b.final[i] = b.acc[i, at, :] * mean
        for k, other in ((0, q1), (1, q2), (2, q3)):
            to = dev(vid, plane, other)
            rows_of = pl.ds(pl.multiple_of(other * part, 8), part)
            send(None, b.final.at[i, rows_of], b.fin_land.at[q, i], b.fin_send.at[k, i], b.fin_recv.at[q, i], to)
        b.out[q, :, i * pw:(i + 1) * pw] = b.final[i, pl.ds(pl.multiple_of(q * part, 8), part), :]

    for off in range(1, members):
        g = lax.rem(mine + off, members)
        arrived(b.gsum.at[g], b.gsum_recv.at[g])
    b.gplane[plane] = jnp.sum(b.gsum[...], axis=0)
    for off in range(1, planes):
        to = dev(vid, lax.rem(plane + off, planes), q)
        send(None, b.gplane.at[plane], b.gplane.at[plane], b.gp_send.at[off], b.gp_recv.at[plane], to)

    @pl.when(y == 0)
    def _():
        share(b.narrow, (0,), b.late_recv, b.att_send, 0)

    @pl.loop(0, pieces)
    def _(i):
        product(i)
        pl.when(last)(lambda: flow_all(i, False, 2))
        pl.when(plane == 0)(lambda: flow_all(i, True, 2))

    @pl.when(jnp.logical_and(plane == 0, planes > 1))
    def _():
        for i in range(pieces):
            remote(*flow(i, 1, True)[1]).start()

    @pl.when(jnp.logical_and(last, planes > 1))
    def _():
        for i in range(pieces):
            remote(*flow(i, 1, False)[1]).start()

    @pl.when(jnp.logical_and(plane > 0, rest))
    def _():
        @pl.loop(0, pieces)
        def _(i):
            flow_all(i, False, 2)
            flow_all(i, True, 2)

        @pl.loop(0, pieces)
        def _(i):
            for up in (False, True):
                ok, copy = flow(i, 1, up)
                pl.when(ok)(lambda: remote(*copy).start())

    for i in range(pieces):
        settle(i)

    def block_rows(at):
        return pl.ds(pl.multiple_of(at * blk, 8), blk)

    @pl.when(rest)
    def _():
        b.grad[block_rows(q), :] = b.passed[q]
        for other in (q1, q2, q3):
            arrived(b.returned.at[other], b.ret_recv.at[other])
            b.grad[block_rows(other), :] = b.returned[other]

    @pl.when(last)
    def _():
        arrived(b.returned.at[other_half], b.ret_recv.at[q1])
        for k in range(2):
            mine_at, other_at = 2 * core + k, 2 * (1 - core) + k
            b.grad[block_rows(mine_at), :] = b.passed[mine_at]
            b.grad[block_rows(other_at), :] = b.returned[other_at]
    for off in range(1, planes):
        at = lax.rem(plane + off, planes)
        arrived(b.gplane.at[at], b.gp_recv.at[at])
    total = jnp.sum(b.gplane[...], axis=0) * mean
    for k in range(b.gain_out.shape[0]):
        b.gain_out[k:k + 1, :] = total[:, k * 128:(k + 1) * 128]
    for i in range(pieces):
        for other in (q1, q2, q3):
            arrived(b.fin_land.at[other, i], b.fin_recv.at[other, i])
            b.out[other, :, i * pw:(i + 1) * pw] = b.fin_land[other, i]

    for cond, copy in pending:
        guarded(cond, lambda: remote(*copy).wait_send())

    @pl.when(y == 0)
    def _():
        for off in range(1, groups):
            v = lax.rem(vid + off, groups)
            for k, slot in ((0, q), (1, q2)):
                for copy in forward(off, k, v, slot):
                    copy.wait_send()
        share(b.query, (), b.early_recv, b.query_send, 2)
        for i in range(pieces):
            share(b.narrow, (i,), b.late_recv, b.att_send, 2)

    for i in range(pieces):
        for up in (False, True):
            for k in range(1, planes):
                to = plane + k if up else plane - k
                ok = to < planes if up else to >= 0
                to = jnp.clip(to, 0, planes - 1)
                land, ss, rs = (b.up, b.up_send, b.up_recv) if up else (b.down, b.down_send, b.down_recv)

                @pl.when(ok)
                def _():
                    remote(
                        b.acc.at[i, block(to)], land.at[i, block(to)], ss.at[i, to], rs.at[i, to],
                        dev(vid, jnp.clip(plane + 1 if up else plane - 1, 0, planes - 1), q),
                    ).wait_send()


def hand_over(grad, weights, gain, grad_out, query_out, key_out, value_out, out_out, gain_out):
    grad_out[...] = grad[...]
    for k, ref in enumerate((key_out, value_out, out_out, query_out)):
        ref[...] = weights[k]
    gain_out[...] = gain[...]


def quad_fits(owners, groups, heads, rows, length, features):
    pw = 2 * features // heads
    return (
        owners % QUAD == 0 and rows % (16 * QUAD) == 0 and length % 128 == 0 and pw == 128 and length == pw
        and (heads // 2) % groups == 0 and features % (8 * owners) == 0 and features % 256 == 0
    )


def quad_call(memory, frames, mem_cot, slot_used, key_bias, start_offset, norm_gain, w_query, w_key, w_value, w_out):
    owners = lax.axis_size("tm")
    groups = lax.axis_size("video")
    rows, features = memory.shape[3:]
    length = frames.shape[3]
    heads = key_bias.shape[3]
    planes = owners // QUAD
    members = groups * QUAD
    pairs = heads // 2
    pieces = pairs // groups
    pw = 2 * features // heads
    blk = rows // QUAD
    part = features // owners
    width = features // groups
    vm, sds = pltpu.VMEM, jax.ShapeDtypeStruct
    sem = lambda *shape: pltpu.SemaphoreType.DMA(shape)
    scratch = dict(
        kin=vm((groups, QUAD, length, features), F32), misc=vm((groups, QUAD, 16, length), F32),
        pack_out=vm((QUAD, 2 * blk, features), F32), pack=vm((QUAD, 2 * blk, features), F32),
        wq=vm((features, features), BF16), wk=vm((features, features), BF16),
        wv=vm((features, features), BF16), wo=vm((features, features), BF16),
        wot=vm((features, features), BF16), wqt=vm((features, features), BF16),
        kbd=vm((QUAD, pairs, 2 * length, pw), BF16), vbd=vm((QUAD, pairs, 2 * length, pw), BF16),
        unit=vm((rows, features), F32), inv=vm((rows, 128), F32), prob=vm((rows, heads * length), F32),
        normed=vm((rows, features), F32), attended=vm((rows, features), F32),
        qp=vm((pairs, rows, pw), F32), att=vm((pairs, rows, pw), F32),
        og=vm((pairs, rows, pw), F32), qg=vm((pairs, rows, pw), F32),
        query=vm((members, pieces, rows, pw), F32), khalf=vm((members, pieces, 2 * length, pw), BF16),
        vhalf=vm((members, pieces, 2 * length, pw), BF16),
        wide=vm((members, pieces, rows, 2 * length), F32), narrow=vm((members, pieces, rows, pw), F32),
        early=vm((members, rows, features), F32), left=vm((features, members * length), BF16),
        right=vm((members * length, pw), BF16), acc=vm((pieces, features, pw), F32),
        up=vm((pieces, features, pw), F32), down=vm((pieces, features, pw), F32),
        final=vm((pieces, features // planes, pw), F32), fin_land=vm((QUAD, pieces, part, pw), F32),
        incoming=vm((blk, features), F32), across=vm((2, blk, features), F32), passed=vm((QUAD, blk, features), F32),
        returned=vm((QUAD, blk, features), F32),
        gsum=vm((members, 1, features), F32), gplane=vm((planes, 1, features), F32),
        dummy=sem(1), w_sem=sem(4), kin_send=sem(3 * groups), kin_recv=sem(groups, QUAD),
        misc_send=sem(2 + groups), misc_recv=sem(groups, QUAD), pack_send=sem(3), pack_recv=sem(QUAD),
        early_send=sem(QUAD, groups), early_recv=sem(members), fwd_send=sem(groups, 2), fwdm_send=sem(groups, 2), query_send=sem(groups, 2), att_send=sem(groups, 2, pieces),
        chain_send=sem(2), chain_recv=sem(1), across_recv=sem(1), gsum_send=sem(members), gsum_recv=sem(members),
        late_send=sem(pieces, QUAD, groups), late_recv=sem(members, pieces),
        ret_send=sem(QUAD), ret_recv=sem(QUAD), gp_send=sem(planes), gp_recv=sem(planes),
        up_send=sem(pieces, planes), up_recv=sem(pieces, planes),
        down_send=sem(pieces, planes), down_recv=sem(pieces, planes),
        fin_send=sem(3, pieces), fin_recv=sem(QUAD, pieces),
    )
    names = ["slot", "offset", "mem", "frames", "cot", "bias", "gain", "wq_hbm", "wk_hbm", "wv_hbm", "wo_hbm"]
    names = names + ["grad", "out", "gain_out"] + list(scratch)
    vmem = pl.BlockSpec(memory_space=pltpu.VMEM)
    smem = pl.BlockSpec(memory_space=pltpu.SMEM)
    hbm = pl.BlockSpec(memory_space=pl.ANY)
    grad, weights, gain = pl.pallas_call(
        functools.partial(quad_kernel, owners, groups, heads, tuple(names)),
        out_shape=(
            sds((rows, features), F32), sds((QUAD, part, width), F32), sds((features // 128, 128), F32),
        ),
        in_specs=[smem, smem] + [vmem] * 5 + [hbm] * 4,
        out_specs=(vmem,) * 3,
        scratch_shapes=list(scratch.values()),
        compiler_params=pltpu.CompilerParams(collective_id=0, has_side_effects=True, vmem_limit_bytes=58 * 1024 * 1024),
        name="quad",
    )(
        slot_used[0, 0], start_offset[0], memory[0, 0, 0], frames[0, 0, 0], mem_cot[0, 0, 0],
        key_bias[0, 0, 0][:, None, :], norm_gain.reshape(features // 128, 128), w_query, w_key, w_value, w_out,
    )
    matrix = sds((part, width), F32)
    grad, query, key, value, out, gain = pl.pallas_call(
        hand_over,
        out_shape=(sds((rows, features), F32), matrix, matrix, matrix, matrix, sds((features // 128, 128), F32)),
        in_specs=[vmem] * 3,
        out_specs=(vmem,) * 6,
        name="hand_over",
    )(grad, weights, gain)
    return (grad[None, None, None], query, key, value, out, gain.reshape(features))


def on_device(
    memory, frames, mem_cot, slot_used, key_bias, start_offset, norm_gain, w_query, w_key, w_value, w_out
):
    owners = lax.axis_size("tm")
    groups = lax.axis_size("video")
    position = lax.axis_index("tm")
    streams, rows, features = memory.shape[2:]
    length = frames.shape[3]
    heads = key_bias.shape[3]
    if quad_fits(owners, groups, heads, rows, length, features):
        return quad_call(
            memory, frames, mem_cot, slot_used, key_bias, start_offset, norm_gain, w_query, w_key, w_value, w_out
        )
    members = 2 * groups
    chips = owners // 2
    bits = chips.bit_length() - 1
    width = features // groups
    keyin = key_rows(frames[0, 0, 0], start_offset[0, 0], position)
    vmem = pl.BlockSpec(memory_space=pltpu.VMEM)
    smem = pl.BlockSpec(memory_space=pltpu.SMEM)
    sds = jax.ShapeDtypeStruct
    pw = 128 if width % 128 == 0 else width
    pieces = 2 * (width // pw)
    dma = pltpu.SemaphoreType.DMA
    grad, weights, gain = pl.pallas_call(
        functools.partial(whole_kernel, owners, groups, heads),
        out_shape=(
            sds((rows, features), F32),
            sds((4, features // owners, width), F32),
            sds((1, features), F32),
        ),
        in_specs=[smem] + [vmem] * 9,
        out_specs=(vmem,) * 3,
        scratch_shapes=[
            pltpu.VMEM((members, length, features), F32),
            pltpu.VMEM((members, rows, features), F32),
            pltpu.VMEM((2, groups, length, width), F32),
            pltpu.VMEM((2, groups, rows, width), F32),
            pltpu.VMEM((1, features), F32),
            pltpu.VMEM((rows, features), F32),
            pltpu.VMEM((2, rows, features), F32),
            pltpu.VMEM((rows, heads * length), F32),
            pltpu.VMEM((rows, heads * length), BF16),
            pltpu.VMEM((heads // 2, 2 * length, 2 * features // heads), BF16),
            pltpu.VMEM((heads // 2, 2 * length, 2 * features // heads), BF16),
            pltpu.VMEM((rows, features), BF16),
            pltpu.VMEM((rows, features), BF16),
            pltpu.VMEM((rows, heads * length), BF16),
            pltpu.VMEM((rows, features), BF16),
            pltpu.VMEM((rows, features), BF16),
            pltpu.VMEM((rows, features), F32),
            pltpu.VMEM((rows, 128), F32),
            pltpu.VMEM((features, features), BF16),
            pltpu.VMEM((features, features), BF16),
            dma((CHUNKS,)), dma((CHUNKS,)), dma((2, members)), dma((2, members)),
            pltpu.VMEM((members, length, width), F32),
            pltpu.VMEM((members, rows, width), F32),
            pltpu.VMEM((features, members * length), BF16),
            pltpu.VMEM((features, members * rows), BF16),
            pltpu.VMEM((pieces, features, pw), F32),
            pltpu.VMEM((pieces, features // owners, pw), F32),
            pltpu.VMEM((members, 1, features), F32),
            pltpu.VMEM((bits + 1, 1, features), F32),
            pltpu.VMEM((max(bits, 1), 1, features), F32),
        ]
        + [pltpu.VMEM((pieces, features >> (s + 1), pw), F32) for s in range(bits)]
        + [
            dma((3, members)), dma((3, members)), dma((pieces, bits)), dma((pieces, bits)),
            dma((bits,)), dma((bits,)), dma((pieces,)), dma((pieces,)),
        ],
        compiler_params=pltpu.CompilerParams(collective_id=0, has_side_effects=True, vmem_limit_bytes=58 * 1024 * 1024),
        name="whole",
    )(
        slot_used[0, 0], memory[0, 0, 0], keyin, mem_cot[0, 0, 0], key_bias[0, 0, 0],
        norm_gain[None, :], w_query, w_key, w_value, w_out,
    )
    return (grad[None, None, None], weights[1], weights[2], weights[3], weights[0], gain[0])


def solution(mesh):
    return jax.shard_map(
        on_device,
        mesh=mesh,
        in_specs=(
            P("video", "tm", None, None, None),
            P("video", "tm", None, None, None),
            P("video", "tm", None, None, None),
            P("video", "tm", None),
            P("video", "tm", None, None, None),
            P("video", None),
            P(),
            P(),
            P(),
            P(),
            P(),
        ),
        out_specs=(
            P("video", "tm", None, None, None),
            P("tm", "video"),
            P("tm", "video"),
            P("tm", "video"),
            P("tm", "video"),
            P(),
        ),
        check_vma=False,
    )
```

```python
import functools
import math
import types

import jax
import jax.numpy as jnp
from jax import lax
from jax.experimental import pallas as pl
from jax.experimental.pallas import tpu as pltpu
from jax.sharding import PartitionSpec as P

NORM_EPSILON = 1e-06
MESH = pl.DeviceIdType.MESH
F32 = jnp.float32
BF16 = jnp.bfloat16
NN = (((1,), (0,)), ((), ()))
NT = (((1,), (1,)), ((), ()))
TN = (((0,), (0,)), ((), ()))
CHUNKS = 4


def dot(left, right, form):
    return lax.dot_general(left, right, form, preferred_element_type=F32)


def key_rows(frame_rows, offset, position):
    length, features = frame_rows.shape
    within = jnp.arange(length, dtype=jnp.int32)
    frame_time = (offset + position * length + within).astype(F32)
    half_width = features // 2
    frequency = 0.0625 * jnp.exp(-math.log(1000.0) * jnp.arange(half_width, dtype=F32) / half_width)
    phases = frame_time[:, None] * frequency
    return frame_rows + jnp.concatenate([jnp.sin(phases), jnp.cos(phases)], axis=-1)


def group_member(groups, g):
    me = lax.axis_index("tm")
    return {"video": lax.div(g, 2), "tm": (me // 2) * 2 + lax.rem(g, 2)}


def whole_kernel(
    owners, groups, heads,
    slot_ref, mem_ref, keyin_ref, cot_ref, bias_ref, gain_ref, wq_ref, wk_ref, wv_ref, wo_ref,
    grad_ref, out_ref, gain_out_ref,
    a1_ref, a2_ref, b1_ref, b2_ref, gsum_ref,
    incoming, mine, prob, half, kbd, vbd, qp, att_all, sg_all, og_all, qg_all, unit_ref, inv_ref, wot, wqt,
    chain_send, chain_recv, a_send, a_recv,
    *reduce_scratch,
):
    me = lax.axis_index("tm")
    vid = lax.axis_index("video")
    chips = owners // 2
    bits = chips.bit_length() - 1
    chip, core = me // 2, lax.rem(me, 2)
    peers = [chip + (1 - 2 * lax.rem(lax.div(chip, 2 ** b), 2)) * 2 ** b for b in range(bits)]
    rows, features = mem_ref.shape
    length = keyin_ref.shape[0]
    head = features // heads
    pairs = heads // 2
    pw = 2 * head
    members = 2 * groups
    g_me = vid * 2 + lax.rem(me, 2)
    scale = head ** (-0.5)

    barrier = pltpu.get_barrier_semaphore()
    for off in range(1, members):
        pl.semaphore_signal(barrier, inc=1, device_id=group_member(groups, lax.rem(g_me + off, members)), device_id_type=MESH)

    for peer in peers:
        pl.semaphore_signal(barrier, inc=1, device_id={"tm": peer * 2 + core}, device_id_type=MESH)

    @pl.when(me > 0)
    def _():
        pl.semaphore_signal(barrier, inc=1, device_id={"tm": me - 1}, device_id_type=MESH)

    @pl.when(me < owners - 1)
    def _():
        pl.semaphore_signal(barrier, inc=1, device_id={"tm": me + 1}, device_id_type=MESH)

    ends = jnp.where(me > 0, 1, 0) + jnp.where(me < owners - 1, 1, 0)
    pl.semaphore_wait(barrier, members - 1 + bits + ends)

    def a_copy(which, src, dst, off):
        g = lax.rem(g_me + off, members)
        return pltpu.make_async_remote_copy(
            src_ref=src, dst_ref=dst.at[g_me], send_sem=a_send.at[which, off], recv_sem=a_recv.at[which, g_me],
            device_id=group_member(groups, g), device_id_type=MESH,
        )

    for off in range(1, members):
        a_copy(0, keyin_ref, a1_ref, off).start()
    a1_ref[g_me] = keyin_ref[...]

    mem = mem_ref[...].astype(F32)
    inv = lax.rsqrt(jnp.mean(mem * mem, axis=-1, keepdims=True) + NORM_EPSILON)
    unit = mem * inv
    unit_ref[...] = unit
    inv_ref[...] = jnp.broadcast_to(inv, inv_ref.shape)
    normed = (unit * gain_ref[...]).astype(BF16)
    mine[1] = normed.astype(F32)
    keyin = keyin_ref[...].astype(BF16)
    query = dot(normed, wq_ref[...], NN).astype(BF16)
    qp[...] = query
    kp = dot(keyin, wk_ref[...], NN).astype(BF16)
    vp = dot(keyin, wv_ref[...], NN).astype(BF16)
    low = lax.broadcasted_iota(jnp.int32, (length, pw), 1) < head
    zero = jnp.zeros((length, pw), BF16)
    for p in range(pairs):
        kk = kp[:, p * pw:(p + 1) * pw]
        vv = vp[:, p * pw:(p + 1) * pw]
        kbd[p, :length] = jnp.where(low, kk, zero)
        kbd[p, length:] = jnp.where(low, zero, kk)
        vbd[p, :length] = jnp.where(low, vv, zero)
        vbd[p, length:] = jnp.where(low, zero, vv)
    wot[...] = jnp.transpose(wo_ref[...])
    wqt[...] = jnp.transpose(wq_ref[...])
    scores = [dot(query[:, p * pw:(p + 1) * pw], kbd[p], NT) for p in range(pairs)]
    for p in range(pairs):
        halves = []
        for q in range(2):
            h = 2 * p + q
            s = scores[p][:, q * length:(q + 1) * length] * scale + bias_ref[h:h + 1, :]
            e = jnp.exp(s - jnp.max(s, axis=-1, keepdims=True))
            pr = e / jnp.sum(e, axis=-1, keepdims=True)
            prob[:, h * length:(h + 1) * length] = pr
            halves.append(pr.astype(BF16))
        both = jnp.concatenate(halves, axis=-1)
        half[:, p * 2 * length:(p + 1) * 2 * length] = both
        mine[0, :, p * pw:(p + 1) * pw] = dot(both, vbd[p], NN).astype(BF16).astype(F32)

    for off in range(1, members):
        g = lax.rem(g_me + off, members)
        a_copy(1, mine.at[lax.rem(g, 2)], a2_ref, off).start()
    a2_ref[g_me] = mine[lax.rem(me, 2)]

    live = slot_ref[0].astype(F32)
    step = rows // CHUNKS

    def chain_copy(c):
        return pltpu.make_async_remote_copy(
            src_ref=grad_ref.at[pl.ds(c * step, step)], dst_ref=incoming.at[pl.ds(c * step, step)],
            send_sem=chain_send.at[c], recv_sem=chain_recv.at[c],
            device_id={"tm": jnp.maximum(me - 1, 0)}, device_id_type=MESH,
        )

    @pl.when(me == owners - 1)
    def _():
        incoming[...] = jnp.zeros_like(incoming)

    gain_total = jnp.zeros((1, features), F32)
    for c in range(CHUNKS):
        r = slice(c * step, (c + 1) * step)

        @pl.when(me < owners - 1)
        def _():
            chain_copy(c).wait_recv()

        grad_in = incoming[r, :] + cot_ref[r, :].astype(F32)
        og = (live * grad_in).astype(BF16)
        att = dot(og, wot[...], NN).astype(BF16)
        prob_grads = [dot(att[:, p * pw:(p + 1) * pw], vbd[p], NT) for p in range(pairs)]
        query_grads = []
        score_grads = []
        for p in range(pairs):
            for q in range(2):
                h = 2 * p + q
                pg = prob_grads[p][:, q * length:(q + 1) * length]
                pr = prob[r, h * length:(h + 1) * length]
                inner = jnp.sum(pr * pg, axis=-1, keepdims=True)
                score_grads.append((pr * (pg - inner) * scale).astype(BF16))
            query_grads.append(dot(jnp.concatenate(score_grads[-2:], axis=-1), kbd[p], NN).astype(BF16))
        qg = jnp.concatenate(query_grads, axis=-1)
        ng = dot(qg, wqt[...], NN)
        un = unit_ref[r, :]
        gain_total = gain_total + jnp.sum(ng * un, axis=0, keepdims=True)
        sc = ng * gain_ref[...]
        grad_ref[r, :] = grad_in + inv_ref[r, 0:1] * (sc - un * jnp.mean(sc * un, axis=-1, keepdims=True))

        @pl.when(me > 0)
        def _():
            chain_copy(c).start()

        og_all[r, :] = og
        att_all[r, :] = att
        qg_all[r, :] = qg
        for h in range(heads):
            sg_all[r, h * length:(h + 1) * length] = score_grads[h]

    gsum_ref[...] = gain_total

    width = features // groups
    lowr = lax.broadcasted_iota(jnp.int32, (rows, pw), 1) < head
    zr = jnp.zeros((rows, pw), BF16)

    def put(out, which, p, value):
        for v in range(groups):
            lo, hi = max(p * pw, v * width), min((p + 1) * pw, (v + 1) * width)
            if lo < hi:
                out[which, v, :, lo - v * width:hi - v * width] = value[:, lo - p * pw:hi - p * pw]

    for p in range(pairs):
        for which, (left_ref, right_ref) in enumerate(((sg_all, qp), (half, att_all))):
            right = right_ref[:, p * pw:(p + 1) * pw]
            right = jnp.concatenate([jnp.where(lowr, right, zr), jnp.where(lowr, zr, right)], axis=0)
            base = 2 * p * length
            left = jnp.concatenate([left_ref[:, base:base + length], left_ref[:, base + length:base + 2 * length]], axis=0)
            put(b1_ref, which, p, dot(left, right, TN).astype(BF16).astype(F32))
        put(b2_ref, 0, p, og_all[:, p * pw:(p + 1) * pw].astype(F32))
        put(b2_ref, 1, p, qg_all[:, p * pw:(p + 1) * pw].astype(F32))

    def a_arrive():
        for off in range(1, members):
            g = lax.rem(g_me + members - off, members)
            for which, dst in ((0, a1_ref), (1, a2_ref)):
                a_copy(which, dst.at[g_me], dst, off).wait_send()
                pltpu.make_async_remote_copy(
                    src_ref=dst.at[g], dst_ref=dst.at[g], send_sem=a_send.at[which, off], recv_sem=a_recv.at[which, g],
                    device_id=group_member(groups, g), device_id_type=MESH,
                ).wait_recv()

    reduce_part(
        owners, groups, peers, a_arrive, a1_ref, a2_ref, b1_ref, b2_ref, gsum_ref, out_ref, gain_out_ref, *reduce_scratch
    )

    @pl.when(me > 0)
    def _():
        for c in range(CHUNKS):
            chain_copy(c).wait_send()


def reduce_part(
    owners, groups, peers, a_arrive,
    a1_ref, a2_ref, b1_ref, b2_ref, gsum_ref,
    out_ref, gain_ref,
    s1, s2, t1, t2, acc, final, gslot, gacc, gland, *rest,
):
    me = lax.axis_index("tm")
    vid = lax.axis_index("video")
    members = 2 * groups
    chips = owners // 2
    bits = chips.bit_length() - 1
    lands = rest[:bits]
    b_send, b_recv, r_send, r_recv, q_send, q_recv, f_send, f_recv = rest[bits:]
    chip, core = me // 2, lax.rem(me, 2)
    g_me = vid * 2 + core
    pieces, features, pw = acc.shape
    per = pieces // 2
    block = features // chips
    part = block // 2
    scale = 1.0 / (owners * groups)
    length, rows = a1_ref.shape[1], a2_ref.shape[1]

    def b_copy(which, off):
        g = lax.rem(g_me + off, members)
        v, c = lax.div(g, 2), lax.rem(g, 2)
        src, dst = ((b1_ref.at[c, v], s1), (b2_ref.at[c, v], s2), (gsum_ref, gslot))[which]
        return pltpu.make_async_remote_copy(
            src_ref=src, dst_ref=dst.at[g_me], send_sem=b_send.at[which, off], recv_sem=b_recv.at[which, g_me],
            device_id=group_member(groups, g), device_id_type=MESH,
        )

    def b_arrive(which, off):
        g = lax.rem(g_me + members - off, members)
        dst = (s1, s2, gslot)[which]
        return pltpu.make_async_remote_copy(
            src_ref=dst.at[g], dst_ref=dst.at[g], send_sem=b_send.at[which, off], recv_sem=b_recv.at[which, g],
            device_id=group_member(groups, g), device_id_type=MESH,
        )

    for which in (2, 1, 0):
        for off in range(1, members):
            b_copy(which, off).start()
    s1[g_me] = b1_ref[core, vid]
    s2[g_me] = b2_ref[core, vid]
    gslot[g_me] = gsum_ref[...]
    a_arrive()
    for g in range(members):
        t1[:, g * length:(g + 1) * length] = jnp.transpose(a1_ref[g]).astype(BF16)
    for g in range(0, members, 2):
        both = jnp.concatenate([a2_ref[g], a2_ref[g + 1]], axis=0)
        t2[:, g * rows:(g + 2) * rows] = jnp.transpose(both).astype(BF16)

    order = [int(format(i, "b").zfill(bits)[::-1], 2) if bits else 0 for i in range(chips)]

    def products(which):
        slots, left = ((s2, t2), (s1, t1))[which]
        for off in range(1, members):
            b_arrive(1 - which, off).wait_recv()
        for i in range(per):
            right = slots[:, :, i * pw:(i + 1) * pw].reshape(left.shape[1], pw).astype(BF16)
            value = dot(left[...], right, NN)
            for pos in range(chips):
                k = order[pos]
                acc[which * per + i, pos * block:(pos + 1) * block, :] = value[k * block:(k + 1) * block, :]

    starts = []
    lo = 0
    for s in range(bits):
        span = features >> (s + 1)
        bit = lax.rem(lax.div(chip, 2 ** s), 2)
        starts.append((lo + (1 - bit) * span, lo + bit * span, span, peers[s]))
        lo = lo + bit * span

    def r_copy(p, s):
        give, _, span, peer = starts[s]
        return pltpu.make_async_remote_copy(
            src_ref=acc.at[p, pl.ds(pl.multiple_of(give, 8), span)], dst_ref=lands[s].at[p],
            send_sem=r_send.at[p, s], recv_sem=r_recv.at[p, s],
            device_id={"tm": peer * 2 + core}, device_id_type=MESH,
        )

    def g_copy(s):
        return pltpu.make_async_remote_copy(
            src_ref=gacc.at[s], dst_ref=gland.at[s], send_sem=q_send.at[s], recv_sem=q_recv.at[s],
            device_id={"tm": peers[s] * 2 + core}, device_id_type=MESH,
        )

    def r_finish(p, s):
        _, keep, span, _ = starts[s]
        r_copy(p, s).wait_recv()
        at = pl.ds(pl.multiple_of(keep, 8), span)
        acc[p, at, :] = acc[p, at, :] + lands[s][p]

    def f_copy(p):
        theirs = pl.ds(pl.multiple_of(lo + (1 - core) * part, 8), part)
        return pltpu.make_async_remote_copy(
            src_ref=acc.at[p, theirs], dst_ref=final.at[p], send_sem=f_send.at[p], recv_sem=f_recv.at[p],
            device_id={"tm": chip * 2 + 1 - core}, device_id_type=MESH,
        )

    for wave in range(pieces + bits):
        if wave == 0:
            products(0)
        if wave == per:
            products(1)
        for s in reversed(range(bits + 1)):
            p = wave - s
            if 0 <= p < pieces:
                if s > 0:
                    r_finish(p, s - 1)
                if s < bits:
                    r_copy(p, s).start()
                else:
                    f_copy(p).start()
        if wave == 0:
            for off in range(1, members):
                b_arrive(2, off).wait_recv()
            gacc[0] = jnp.sum(gslot[...], axis=0)
        if 0 < wave <= bits:
            g_copy(wave - 1).wait_recv()
            gacc[wave] = gacc[wave - 1] + gland[wave - 1]
        if wave < bits:
            g_copy(wave).start()

    mine_rows = pl.ds(pl.multiple_of(lo + core * part, 8), part)
    for p in range(pieces):
        which, i = p // per, p % per
        cols = slice(i * pw, (i + 1) * pw)
        out_ref[2 * which + core, :, cols] = acc[p, mine_rows, :] * scale
    for p in range(pieces):
        which, i = p // per, p % per
        cols = slice(i * pw, (i + 1) * pw)
        f_copy(p).wait_recv()
        out_ref[2 * which + 1 - core, :, cols] = final[p] * scale

    gain_ref[...] = gacc[bits] * scale
    for s in range(bits):
        g_copy(s).wait_send()
    for which in range(3):
        for off in range(1, members):
            b_copy(which, off).wait_send()
    for p in range(pieces):
        for s in range(bits):
            r_copy(p, s).wait_send()
        f_copy(p).wait_send()


QUAD = 4


def xor_bits(value, bits):
    high, low = lax.div(value, 2), lax.rem(value, 2)
    if bits & 2:
        high = 1 - high
    if bits & 1:
        low = 1 - low
    return high * 2 + low


def encoded(frames_ref, first_time, put):
    length, features = frames_ref.shape
    half_width = features // 2
    index = lax.broadcasted_iota(jnp.int32, (1, half_width), 1).astype(F32)
    frequency = 0.0625 * jnp.exp(-math.log(1000.0) * index / half_width)
    groups_of = length // 8
    outer = first_time + 8 * lax.broadcasted_iota(jnp.int32, (groups_of, half_width), 0)
    inner = lax.broadcasted_iota(jnp.int32, (8, half_width), 0)
    outer, inner = outer.astype(F32) * frequency, inner.astype(F32) * frequency
    so, co, si, ci = jnp.sin(outer), jnp.cos(outer), jnp.sin(inner), jnp.cos(inner)
    for a in range(groups_of):
        s, c = so[a:a + 1], co[a:a + 1]
        r = slice(a * 8, (a + 1) * 8)
        put(r, slice(0, half_width), frames_ref[r, :half_width] + (s * ci + c * si))
        put(r, slice(half_width, features), frames_ref[r, half_width:] + (c * ci - s * si))


def quad_kernel(owners, groups, heads, names, *refs):
    b = types.SimpleNamespace(**dict(zip(names, refs)))
    me = lax.axis_index("tm")
    vid = lax.axis_index("video")
    planes = owners // QUAD
    plane, q = lax.div(me, QUAD), lax.rem(me, QUAD)
    y = lax.div(q, 2)
    members = groups * QUAD
    mine = vid * QUAD + q
    rows, features = b.mem.shape
    length = b.frames.shape[0]
    head = features // heads
    pairs = heads // 2
    pw = 2 * head
    blk = rows // QUAD
    pieces = pairs // groups
    span = features // planes
    part = features // owners
    scale = head ** (-0.5)
    q1, q2, q3 = xor_bits(q, 1), xor_bits(q, 2), xor_bits(q, 3)
    core = lax.rem(q, 2)
    last, rest = plane == planes - 1, plane < planes - 1
    last_low = jnp.logical_and(last, y == 0)
    last_high = jnp.logical_and(last, y == 1)
    own_half, other_half = pl.ds(2 * core, 2), pl.ds(2 * (1 - core), 2)
    pending = []

    def dev(v, at, qq):
        return {"video": v, "tm": at * QUAD + qq}

    def member(g):
        return dev(lax.div(g, QUAD), plane, lax.rem(g, QUAD))

    def remote(src, dst, ss, rs, to):
        return pltpu.make_async_remote_copy(
            src_ref=src, dst_ref=dst, send_sem=ss, recv_sem=rs, device_id=to, device_id_type=MESH
        )

    def guarded(cond, act):
        if cond is None:
            act()
        else:
            pl.when(cond)(act)

    def send(cond, *copy):
        guarded(cond, lambda: remote(*copy).start())
        pending.append((cond, copy))

    def arrived(dst, rs):
        remote(dst, dst, b.dummy.at[0], rs, dev(vid, plane, q1)).wait_recv()

    weights = [(b.wq_hbm, b.wq), (b.wk_hbm, b.wk), (b.wv_hbm, b.wv), (b.wo_hbm, b.wo)]

    def load(k):
        return pltpu.make_async_copy(weights[k][0], weights[k][1], b.w_sem.at[k])

    for k in (1, 2, 0, 3):
        load(k).start()

    barrier = pltpu.get_barrier_semaphore()
    for off in range(1, members):
        pl.semaphore_signal(barrier, inc=1, device_id=member(lax.rem(mine + off, members)), device_id_type=MESH)
    for off in range(1, planes):
        pl.semaphore_signal(
            barrier, inc=1, device_id=dev(vid, lax.rem(plane + off, planes), q), device_id_type=MESH
        )

    @pl.when(plane == planes - 2)
    def _():
        pl.semaphore_signal(
            barrier, inc=1, device_id=dev(vid, jnp.minimum(plane + 1, planes - 1), y), device_id_type=MESH
        )

    def put_key(r, cols, value):
        b.kin[vid, q, r, cols] = value

    encoded(b.frames, b.offset[0] + me * length, put_key)
    for h in range(heads):
        b.misc[vid, q, h:h + 1, :] = b.bias[h]
    b.misc[vid, q, heads:heads + 1, :] = jnp.zeros((1, length), F32) + b.slot[0].astype(F32)
    for j in range(QUAD):
        b.pack_out[j, :blk] = b.mem[j * blk:(j + 1) * blk, :].astype(F32)
        b.pack_out[j, blk:] = b.cot[j * blk:(j + 1) * blk, :].astype(F32)

    @pl.when(rest)
    def _():
        b.pack[q] = b.pack_out[q]

    @pl.when(last)
    def _():
        b.pack[own_half] = b.pack_out[own_half]

    pl.semaphore_wait(barrier, members - 1 + planes - 1 + jnp.where(last_low, 2 if planes > 1 else 0, 0))

    def send_key(cond, slot, sem, to):
        send(cond, b.kin.at[vid, slot], b.kin.at[vid, slot], b.kin_send.at[sem], b.kin_recv.at[vid, slot], to)

    def send_misc(cond, sem, to):
        send(cond, b.misc.at[vid, q], b.misc.at[vid, q], b.misc_send.at[sem], b.misc_recv.at[vid, q], to)

    send_key(rest, q, 0, dev(vid, plane, q2))
    send_key(None, q, 1, dev(vid, plane, q1))
    for k, other in ((0, q1), (1, q2), (2, q3)):
        to = dev(vid, plane, other)
        send_misc(None, k, to)
        send(rest, b.pack_out.at[other], b.pack.at[q], b.pack_send.at[k], b.pack_recv.at[q], to)
    send(
        last, b.pack_out.at[other_half], b.pack.at[own_half], b.pack_send.at[0], b.pack_recv.at[q],
        dev(vid, plane, q1),
    )
    for off in range(1, groups):
        send_key(y == 0, q, 3 * off, dev(lax.rem(vid + off, groups), plane, q))
        send_misc(None, 2 + off, dev(lax.rem(vid + off, groups), plane, core))

    low = lax.broadcasted_iota(jnp.int32, (length, pw), 1) < head
    zero = jnp.zeros((length, pw), BF16)

    def project(slot):
        keyin = b.kin[vid, slot].astype(BF16)
        kp = dot(keyin, b.wk[...], NN).astype(BF16)
        vp = dot(keyin, b.wv[...], NN).astype(BF16)
        for p in range(pairs):
            kk = kp[:, p * pw:(p + 1) * pw]
            vv = vp[:, p * pw:(p + 1) * pw]
            b.kbd[slot, p, :length] = jnp.where(low, kk, zero)
            b.kbd[slot, p, length:] = jnp.where(low, zero, kk)
            b.vbd[slot, p, :length] = jnp.where(low, vv, zero)
            b.vbd[slot, p, length:] = jnp.where(low, zero, vv)

    for k in (1, 2, 0, 3):
        load(k).wait()
    project(q)
    b.wot[...] = jnp.transpose(b.wo[...])
    b.wqt[...] = jnp.transpose(b.wq[...])
    arrived(b.kin.at[vid, q1], b.kin_recv.at[vid, q1])
    project(q1)
    for other in (q1, q2, q3):
        arrived(b.misc.at[vid, other], b.misc_recv.at[vid, other])

    def pass_on(cond):
        guarded(cond, lambda: arrived(b.kin.at[vid, q2], b.kin_recv.at[vid, q2]))
        send_key(cond, q2, 2, dev(vid, plane, q1))

    def cross(cond):
        for off in range(1, groups):
            send_key(cond, q, 3 * off + 1, dev(lax.rem(vid + off, groups), plane, core))

    pass_on(rest)

    @pl.when(rest)
    def _():
        project(q2)
        arrived(b.kin.at[vid, q3], b.kin_recv.at[vid, q3])
        project(q3)
        for other in (q1, q2, q3):
            arrived(b.pack.at[other], b.pack_recv.at[other])

    @pl.when(last)
    def _():
        arrived(b.pack.at[other_half], b.pack_recv.at[q1])

    cross(jnp.logical_and(rest, y == 1))

    gain = jnp.concatenate([b.gain[k:k + 1, :] for k in range(b.gain.shape[0])], axis=-1)
    mem = jnp.concatenate([b.pack[j, :blk] for j in range(QUAD)], axis=0)
    inv = lax.rsqrt(jnp.mean(mem * mem, axis=-1, keepdims=True) + NORM_EPSILON)
    unit = mem * inv
    b.unit[...] = unit
    b.inv[...] = jnp.broadcast_to(inv, b.inv.shape)
    normed = (unit * gain).astype(BF16)
    b.normed[...] = normed.astype(F32)
    query = dot(normed, b.wq[...], NN).astype(BF16)
    for p in range(pairs):
        b.qp[p] = query[:, p * pw:(p + 1) * pw].astype(F32)
    def attend(r, slot):
        scores = [dot(query[r, p * pw:(p + 1) * pw], b.kbd[slot, p], NT) for p in range(pairs)]
        for p in range(pairs):
            halves = []
            for k in range(2):
                h = 2 * p + k
                sc = scores[p][:, k * length:(k + 1) * length] * scale + b.misc[vid, slot, h:h + 1, :]
                e = jnp.exp(sc - jnp.max(sc, axis=-1, keepdims=True))
                pr = e / jnp.sum(e, axis=-1, keepdims=True)
                b.prob[r, h * length:(h + 1) * length] = pr
                halves.append(pr.astype(BF16))
            both = jnp.concatenate(halves, axis=-1)
            b.attended[r, p * pw:(p + 1) * pw] = dot(both, b.vbd[slot, p], NN).astype(BF16).astype(F32)

    singles = [(slice(j * blk, (j + 1) * blk), (j,)) for j in reversed(range(QUAD))]
    doubles = [(slice(2 * a * blk, 2 * (a + 1) * blk), (2 * a, 2 * a + 1)) for a in (1, 0)]

    @pl.when(rest)
    def _():
        for r, (j,) in singles:
            attend(r, j)

    @pl.when(last)
    def _():
        for r, (k, _) in doubles:
            attend(r, 2 * y + k // 2)

    def qp_of(v):
        return b.qp.at[pl.ds(v * pieces, pieces)]

    for off in range(groups):
        v = lax.rem(vid + off, groups)
        send(
            y != 0 if off == 0 else None, qp_of(v), b.query.at[mine], b.early_send.at[0, off],
            b.early_recv.at[mine], dev(v, plane, core),
        )
    for off in range(groups):
        v = lax.rem(vid + off, groups)
        for role, src in ((2, b.attended), (3, b.normed)):
            send(
                q != role if off == 0 else None, src, b.early.at[mine], b.early_send.at[role, off],
                b.early_recv.at[mine], dev(v, plane, role),
            )

    @pl.when(y == 0)
    def _():
        b.query[mine] = qp_of(vid)[...]

    for role, src in ((2, b.attended), (3, b.normed)):
        @pl.when(q == role)
        def _():
            b.early[mine] = src[...]

    def same_core(side):
        return [
            (off, e, lax.rem(vid + off, groups) * QUAD + 2 * e + side) for off in range(groups) for e in range(2)
        ]

    def share(ref, index, recv, ss, stage):
        for off, e, g in same_core(core):
            at = ref.at[(g, *index)]
            copy = remote(at, at, ss.at[(off, e, *index)], recv.at[(g, *index)], dev(vid, plane, q1))
            if stage == 0 and (off, e) != (0, 0):
                arrived(at, recv.at[(g, *index)])
            if stage == 0:
                copy.start()
            if stage == 2:
                copy.wait_send()
        if stage == 1:
            for off, e, g in same_core(1 - core):
                arrived(ref.at[(g, *index)], recv.at[(g, *index)])

    def forward(off, k, v, slot):
        at, to = b.kin.at[v, slot], dev(vid, plane, q1)
        small = b.misc.at[v, slot]
        return (
            remote(at, at, b.fwd_send.at[off, k], b.kin_recv.at[v, slot], to),
            remote(small, small, b.fwdm_send.at[off, k], b.misc_recv.at[v, slot], to),
        )

    def gather(ref, v, i, j):
        parts = []
        for k in range(QUAD):
            g = v * QUAD + jnp.where(last, 2 * (j // 2) + k // 2, k)
            at = jnp.where(last, (2 * (j % 2) + k % 2) * blk, j * blk)
            parts.append(ref[g, i, pl.ds(pl.multiple_of(at, blk), blk), :])
        return jnp.concatenate(parts, axis=0).astype(BF16)

    half_cols = pl.ds(pl.multiple_of(vid * pieces * pw, 128), pieces * pw)

    def apart(value, p, out, g):
        vv = value[:, p * pw:(p + 1) * pw]
        out[g, p, :length] = jnp.where(low, vv, zero)
        out[g, p, length:] = jnp.where(low, zero, vv)

    def prepare(v):
        @pl.loop(0, QUAD // 2)
        def _(n):
            pair = [v * QUAD + 2 * n + k for k in range(2)]
            keyin = jnp.concatenate([b.kin[v, 2 * n + k].astype(BF16) for k in range(2)], axis=0)
            at = pl.ds(pl.multiple_of(pair[0] * length, 128), 2 * length)
            b.left[:, at] = jnp.transpose(keyin)

            def halves_of(weight, out):
                value = dot(keyin, weight[:, half_cols], NN).astype(BF16)
                for k in range(2):
                    for p in range(pieces):
                        apart(value[k * length:(k + 1) * length], p, out, pair[k])

            halves_of(b.wk, b.khalf)
            pl.when(q == 0)(lambda: halves_of(b.wv, b.vhalf))

    @pl.when(jnp.logical_and(y == 0, plane < planes // 2))
    def _():
        prepare(vid)

    def early_keys():
        guarded(last, lambda: arrived(b.kin.at[vid, q3], b.kin_recv.at[vid, q3]))
        for off in range(1, groups):
            v = lax.rem(vid + off, groups)
            for k, slot in ((0, q), (1, q2)):
                arrived(b.kin.at[v, slot], b.kin_recv.at[v, slot])
                arrived(b.misc.at[v, slot], b.misc_recv.at[v, slot])
                for copy in forward(off, k, v, slot):
                    copy.start()

        @pl.when(plane >= planes // 2)
        def _():
            prepare(vid)

        for off in range(1, groups):
            v = lax.rem(vid + off, groups)
            for slot in (q1, q3):
                arrived(b.kin.at[v, slot], b.kin_recv.at[v, slot])
                arrived(b.misc.at[v, slot], b.misc_recv.at[v, slot])
            prepare(v)

    @pl.when(jnp.logical_and(y == 0, plane < planes // 4))
    def _():
        early_keys()

    def early_low():
        share(b.query, (), b.early_recv, b.query_send, 0)

        @pl.when(plane >= planes // 4)
        def _():
            early_keys()

        share(b.query, (), b.early_recv, b.query_send, 1)

        @pl.loop(0, pieces)
        def _(i):
            clips = [(v, j) for v in range(groups) for j in range(QUAD)]
            found = []
            for v, j in clips:
                scores = dot(gather(b.query, v, i, j), b.khalf[v * QUAD + j, i], NT)
                for k in range(2):
                    h = 2 * (vid * pieces + i) + k
                    sc = scores[:, k * length:(k + 1) * length] * scale + b.misc[v, j, pl.ds(h, 1), :]
                    e = jnp.exp(sc - jnp.max(sc, axis=-1, keepdims=True))
                    found.append(e / jnp.sum(e, axis=-1, keepdims=True))
            for n, (v, j) in enumerate(clips):
                for k in range(2):
                    b.wide[v * QUAD + j, i, :, k * length:(k + 1) * length] = found[2 * n + k]

    def early_high():
        for off in range(1, members):
            g = lax.rem(mine + off, members)
            arrived(b.early.at[g], b.early_recv.at[g])
        for g in range(0, members, 2):
            both = jnp.concatenate([b.early[g], b.early[g + 1]], axis=0)
            b.left[:, g * rows:(g + 2) * rows] = jnp.transpose(both.astype(BF16))

    below = jnp.maximum(plane - 1, 0)
    single_to = (
        jnp.logical_and(rest, plane > 0),
        (b.passed.at[0], b.incoming, b.chain_send.at[0], b.chain_recv.at[0], dev(vid, below, q)),
    )
    across_to = (
        last_high,
        (b.passed.at[pl.ds(0, 2)], b.across, b.chain_send.at[0], b.across_recv.at[0], dev(vid, plane, q2)),
    )
    double_to = [
        (
            jnp.logical_and(last_low, plane > 0),
            (b.passed.at[k], b.incoming, b.chain_send.at[k], b.chain_recv.at[0], dev(vid, below, 2 * core + k)),
        )
        for k in range(2)
    ]

    def step(r, blocks, slot, carried, outgoing):
        grad_in = carried + jnp.concatenate([b.pack[k, blk:] for k in blocks], axis=0)
        live = jnp.concatenate([b.misc[vid, slot, heads:heads + 1, :]] * (features // length), axis=-1)
        og = (live * grad_in).astype(BF16)
        att = dot(og, b.wot[...], NN).astype(BF16)
        prob_grads = [dot(att[:, p * pw:(p + 1) * pw], b.vbd[slot, p], NT) for p in range(pairs)]
        query_grads = []
        for p in range(pairs):
            halves = []
            for k in range(2):
                h = 2 * p + k
                pg = prob_grads[p][:, k * length:(k + 1) * length]
                pr = b.prob[r, h * length:(h + 1) * length]
                inner = jnp.sum(pr * pg, axis=-1, keepdims=True)
                halves.append((pr * (pg - inner) * scale).astype(BF16))
            both = jnp.concatenate(halves, axis=-1)
            query_grads.append(dot(both, b.kbd[slot, p], NN).astype(BF16))
        qg = jnp.concatenate(query_grads, axis=-1)
        ng = dot(qg, b.wqt[...], NN)
        un = b.unit[r, :]
        sc = ng * gain
        carried = grad_in + b.inv[r, 0:1] * (sc - un * jnp.mean(sc * un, axis=-1, keepdims=True))
        for n, k in enumerate(blocks):
            b.passed[k] = carried[n * blk:(n + 1) * blk]
        for cond, copy in outgoing:
            pl.when(cond)(lambda: remote(*copy).start())
        for p in range(pairs):
            cols = slice(p * pw, (p + 1) * pw)
            b.att[p, r, :] = att[:, cols].astype(F32)
            b.og[p, r, :] = og[:, cols].astype(F32)
            b.qg[p, r, :] = qg[:, cols].astype(F32)
        return carried, jnp.sum(ng * un, axis=0, keepdims=True)

    pending.extend([single_to, across_to] + double_to)

    @pl.when(rest)
    def _():
        arrived(b.incoming, b.chain_recv.at[0])
        gain_total = jnp.zeros((1, features), F32)
        carried = b.incoming[...]
        for r, (j,) in singles:
            carried, gain_part = step(r, (j,), j, carried, [single_to] if j == 0 else [])
            gain_total = gain_total + gain_part
        b.gsum[mine] = gain_total

    @pl.when(last_high)
    def _():
        b.across[...] = jnp.zeros_like(b.across)

    @pl.when(last_low)
    def _():
        arrived(b.across, b.across_recv.at[0])

    @pl.when(last)
    def _():
        gain_total = jnp.zeros((1, features), F32)
        carried = jnp.concatenate([b.across[0], b.across[1]], axis=0)
        for r, blocks in doubles:
            outgoing = [across_to] + double_to if blocks[0] == 0 else []
            carried, gain_part = step(r, blocks, 2 * y + blocks[0] // 2, carried, outgoing)
            gain_total = gain_total + gain_part
        b.gsum[mine] = gain_total

    send_key(last_high, q, 0, dev(vid, plane, q2))
    cross(last_high)
    for off in range(1, members):
        g = lax.rem(mine + off, members)
        send(None, b.gsum.at[mine], b.gsum.at[mine], b.gsum_send.at[off], b.gsum_recv.at[mine], member(g))

    rounds = [(i, ((0, y != 0, b.att),)) for i in range(pieces)]
    rounds = rounds + [(i, ((2, q != 2, b.og), (3, q != 3, b.qg))) for i in range(pieces)]
    for i, sent in rounds:
        for off in reversed(range(groups)):
            v = lax.rem(vid + off, groups)
            for role, cond, src in sent:
                send(
                    cond if off == 0 else None, src.at[v * pieces + i], b.narrow.at[mine, i],
                    b.late_send.at[i, role, off], b.late_recv.at[mine, i],
                    dev(v, plane, core if role == 0 else role),
                )
    for cond, src in ((y == 0, b.att), (q == 2, b.og), (q == 3, b.qg)):
        @pl.when(cond)
        def _():
            b.narrow[mine] = src[pl.ds(vid * pieces, pieces)]

    for j in range(QUAD):
        send(
            jnp.logical_and(rest, q != j), b.passed.at[j], b.returned.at[q], b.ret_send.at[j], b.ret_recv.at[q],
            dev(vid, plane, j),
        )
    send(
        last, b.passed.at[other_half], b.returned.at[own_half], b.ret_send.at[0], b.ret_recv.at[q],
        dev(vid, plane, q1),
    )
    pass_on(last_low)

    @pl.when(y == 0)
    def _():
        early_low()

    @pl.when(y == 1)
    def _():
        early_high()

    lowr = lax.broadcasted_iota(jnp.int32, (rows, pw), 1) < head
    zr = jnp.zeros((rows, pw), BF16)

    def product(i):
        @pl.when(y == 0)
        def _():
            share(b.narrow, (i,), b.late_recv, b.att_send, 1)

        @pl.when(y == 1)
        def _():
            for off in range(1, members):
                g = lax.rem(mine + off, members)
                arrived(b.narrow.at[g, i], b.late_recv.at[g, i])

        def token_grads(role):
            found = []
            for v in range(groups):
                for j in range(QUAD):
                    g = v * QUAD + j
                    right = att = gather(b.narrow, v, i, j)
                    halves = []
                    if role == 0:
                        right = gather(b.query, v, i, j)
                        prob_grad = dot(att, b.vhalf[g, i], NT)
                    for k in range(2):
                        cols = slice(k * length, (k + 1) * length)
                        pr = b.wide[g, i, :, cols]
                        if role == 0:
                            pg = prob_grad[:, cols]
                            pr = pr * (pg - jnp.sum(pr * pg, axis=-1, keepdims=True)) * scale
                        halves.append(pr.astype(BF16))
                    stacked = jnp.concatenate(halves, axis=0)
                    right = jnp.concatenate([jnp.where(lowr, right, zr), jnp.where(lowr, zr, right)], axis=0)
                    found.append(dot(stacked, right, TN).astype(BF16))
            b.right[...] = jnp.concatenate(found, axis=0)

        for role in range(2):
            pl.when(q == role)(functools.partial(token_grads, role))

        @pl.when(jnp.logical_and(y == 0, i + 1 < pieces))
        def _():
            share(b.narrow, (i + 1,), b.late_recv, b.att_send, 0)

        @pl.when(y == 0)
        def _():
            b.acc[i] = dot(b.left[...], b.right[...], NN)

        @pl.when(y == 1)
        def _():
            right = jnp.concatenate([b.narrow[g, i] for g in range(members)], axis=0).astype(BF16)
            b.acc[i] = dot(b.left[:, :members * rows], right, NN)

    def block(at):
        return pl.ds(pl.multiple_of(at * span, 8), span)

    def flow(i, k, up):
        to = plane + k if up else plane - k
        ok = to < planes if up else to >= 0
        fed = plane > 0 if up else plane < planes - 1
        land, ss, rs = (b.up, b.up_send, b.up_recv) if up else (b.down, b.down_send, b.down_recv)
        to = jnp.clip(to, 0, planes - 1)
        at = block(to)
        step = jnp.clip(plane + 1 if up else plane - 1, 0, planes - 1)

        @pl.when(jnp.logical_and(ok, fed))
        def _():
            arrived(land.at[i, at], rs.at[i, to])
            b.acc[i, at, :] = b.acc[i, at, :] + land[i, at, :]

        return ok, (b.acc.at[i, at], land.at[i, at], ss.at[i, to], rs.at[i, to], dev(vid, step, q))

    def flow_all(i, up, near=1):
        for k in reversed(range(near, planes)):
            ok, copy = flow(i, k, up)
            pl.when(ok)(lambda: remote(*copy).start())

    mean = 1.0 / (owners * groups)

    def settle(i):
        at = block(plane)

        @pl.when(plane < planes - 1)
        def _():
            arrived(b.down.at[i, at], b.down_recv.at[i, plane])
            b.acc[i, at, :] = b.acc[i, at, :] + b.down[i, at, :]

        @pl.when(plane > 0)
        def _():
            arrived(b.up.at[i, at], b.up_recv.at[i, plane])
            b.acc[i, at, :] = b.acc[i, at, :] + b.up[i, at, :]

        b.final[i] = b.acc[i, at, :] * mean
        for k, other in ((0, q1), (1, q2), (2, q3)):
            to = dev(vid, plane, other)
            rows_of = pl.ds(pl.multiple_of(other * part, 8), part)
            send(None, b.final.at[i, rows_of], b.fin_land.at[q, i], b.fin_send.at[k, i], b.fin_recv.at[q, i], to)
        b.out[q, :, i * pw:(i + 1) * pw] = b.final[i, pl.ds(pl.multiple_of(q * part, 8), part), :]

    for off in range(1, members):
        g = lax.rem(mine + off, members)
        arrived(b.gsum.at[g], b.gsum_recv.at[g])
    b.gplane[plane] = jnp.sum(b.gsum[...], axis=0)
    for off in range(1, planes):
        to = dev(vid, lax.rem(plane + off, planes), q)
        send(None, b.gplane.at[plane], b.gplane.at[plane], b.gp_send.at[off], b.gp_recv.at[plane], to)

    @pl.when(y == 0)
    def _():
        share(b.narrow, (0,), b.late_recv, b.att_send, 0)

    @pl.loop(0, pieces)
    def _(i):
        product(i)
        pl.when(last)(lambda: flow_all(i, False, 2))
        pl.when(plane == 0)(lambda: flow_all(i, True, 2))

    @pl.when(jnp.logical_and(plane == 0, planes > 1))
    def _():
        for i in range(pieces):
            remote(*flow(i, 1, True)[1]).start()

    @pl.when(jnp.logical_and(last, planes > 1))
    def _():
        for i in range(pieces):
            remote(*flow(i, 1, False)[1]).start()

    @pl.when(jnp.logical_and(plane > 0, rest))
    def _():
        @pl.loop(0, pieces)
        def _(i):
            flow_all(i, False, 2)
            flow_all(i, True, 2)

        @pl.loop(0, pieces)
        def _(i):
            for up in (False, True):
                ok, copy = flow(i, 1, up)
                pl.when(ok)(lambda: remote(*copy).start())

    for i in range(pieces):
        settle(i)

    def block_rows(at):
        return pl.ds(pl.multiple_of(at * blk, 8), blk)

    @pl.when(rest)
    def _():
        b.grad[block_rows(q), :] = b.passed[q]
        for other in (q1, q2, q3):
            arrived(b.returned.at[other], b.ret_recv.at[other])
            b.grad[block_rows(other), :] = b.returned[other]

    @pl.when(last)
    def _():
        arrived(b.returned.at[other_half], b.ret_recv.at[q1])
        for k in range(2):
            mine_at, other_at = 2 * core + k, 2 * (1 - core) + k
            b.grad[block_rows(mine_at), :] = b.passed[mine_at]
            b.grad[block_rows(other_at), :] = b.returned[other_at]
    for off in range(1, planes):
        at = lax.rem(plane + off, planes)
        arrived(b.gplane.at[at], b.gp_recv.at[at])
    total = jnp.sum(b.gplane[...], axis=0) * mean
    for k in range(b.gain_out.shape[0]):
        b.gain_out[k:k + 1, :] = total[:, k * 128:(k + 1) * 128]
    for i in range(pieces):
        for other in (q1, q2, q3):
            arrived(b.fin_land.at[other, i], b.fin_recv.at[other, i])
            b.out[other, :, i * pw:(i + 1) * pw] = b.fin_land[other, i]

    for cond, copy in pending:
        guarded(cond, lambda: remote(*copy).wait_send())

    @pl.when(y == 0)
    def _():
        for off in range(1, groups):
            v = lax.rem(vid + off, groups)
            for k, slot in ((0, q), (1, q2)):
                for copy in forward(off, k, v, slot):
                    copy.wait_send()
        share(b.query, (), b.early_recv, b.query_send, 2)
        for i in range(pieces):
            share(b.narrow, (i,), b.late_recv, b.att_send, 2)

    for i in range(pieces):
        for up in (False, True):
            for k in range(1, planes):
                to = plane + k if up else plane - k
                ok = to < planes if up else to >= 0
                to = jnp.clip(to, 0, planes - 1)
                land, ss, rs = (b.up, b.up_send, b.up_recv) if up else (b.down, b.down_send, b.down_recv)

                @pl.when(ok)
                def _():
                    remote(
                        b.acc.at[i, block(to)], land.at[i, block(to)], ss.at[i, to], rs.at[i, to],
                        dev(vid, jnp.clip(plane + 1 if up else plane - 1, 0, planes - 1), q),
                    ).wait_send()


def hand_over(grad, weights, gain, grad_out, query_out, key_out, value_out, out_out, gain_out):
    grad_out[...] = grad[...]
    for k, ref in enumerate((key_out, value_out, out_out, query_out)):
        ref[...] = weights[k]
    gain_out[...] = gain[...]


def quad_fits(owners, groups, heads, rows, length, features):
    pw = 2 * features // heads
    return (
        owners % QUAD == 0 and rows % (16 * QUAD) == 0 and length % 128 == 0 and pw == 128 and length == pw
        and (heads // 2) % groups == 0 and features % (8 * owners) == 0 and features % 256 == 0
    )


def quad_call(memory, frames, mem_cot, slot_used, key_bias, start_offset, norm_gain, w_query, w_key, w_value, w_out):
    owners = lax.axis_size("tm")
    groups = lax.axis_size("video")
    rows, features = memory.shape[3:]
    length = frames.shape[3]
    heads = key_bias.shape[3]
    planes = owners // QUAD
    members = groups * QUAD
    pairs = heads // 2
    pieces = pairs // groups
    pw = 2 * features // heads
    blk = rows // QUAD
    part = features // owners
    width = features // groups
    vm, sds = pltpu.VMEM, jax.ShapeDtypeStruct
    sem = lambda *shape: pltpu.SemaphoreType.DMA(shape)
    scratch = dict(
        kin=vm((groups, QUAD, length, features), F32), misc=vm((groups, QUAD, 16, length), F32),
        pack_out=vm((QUAD, 2 * blk, features), F32), pack=vm((QUAD, 2 * blk, features), F32),
        wq=vm((features, features), BF16), wk=vm((features, features), BF16),
        wv=vm((features, features), BF16), wo=vm((features, features), BF16),
        wot=vm((features, features), BF16), wqt=vm((features, features), BF16),
        kbd=vm((QUAD, pairs, 2 * length, pw), BF16), vbd=vm((QUAD, pairs, 2 * length, pw), BF16),
        unit=vm((rows, features), F32), inv=vm((rows, 128), F32), prob=vm((rows, heads * length), F32),
        normed=vm((rows, features), F32), attended=vm((rows, features), F32),
        qp=vm((pairs, rows, pw), F32), att=vm((pairs, rows, pw), F32),
        og=vm((pairs, rows, pw), F32), qg=vm((pairs, rows, pw), F32),
        query=vm((members, pieces, rows, pw), F32), khalf=vm((members, pieces, 2 * length, pw), BF16),
        vhalf=vm((members, pieces, 2 * length, pw), BF16),
        wide=vm((members, pieces, rows, 2 * length), F32), narrow=vm((members, pieces, rows, pw), F32),
        early=vm((members, rows, features), F32), left=vm((features, members * length), BF16),
        right=vm((members * length, pw), BF16), acc=vm((pieces, features, pw), F32),
        up=vm((pieces, features, pw), F32), down=vm((pieces, features, pw), F32),
        final=vm((pieces, features // planes, pw), F32), fin_land=vm((QUAD, pieces, part, pw), F32),
        incoming=vm((blk, features), F32), across=vm((2, blk, features), F32), passed=vm((QUAD, blk, features), F32),
        returned=vm((QUAD, blk, features), F32),
        gsum=vm((members, 1, features), F32), gplane=vm((planes, 1, features), F32),
        dummy=sem(1), w_sem=sem(4), kin_send=sem(3 * groups), kin_recv=sem(groups, QUAD),
        misc_send=sem(2 + groups), misc_recv=sem(groups, QUAD), pack_send=sem(3), pack_recv=sem(QUAD),
        early_send=sem(QUAD, groups), early_recv=sem(members), fwd_send=sem(groups, 2), fwdm_send=sem(groups, 2), query_send=sem(groups, 2), att_send=sem(groups, 2, pieces),
        chain_send=sem(2), chain_recv=sem(1), across_recv=sem(1), gsum_send=sem(members), gsum_recv=sem(members),
        late_send=sem(pieces, QUAD, groups), late_recv=sem(members, pieces),
        ret_send=sem(QUAD), ret_recv=sem(QUAD), gp_send=sem(planes), gp_recv=sem(planes),
        up_send=sem(pieces, planes), up_recv=sem(pieces, planes),
        down_send=sem(pieces, planes), down_recv=sem(pieces, planes),
        fin_send=sem(3, pieces), fin_recv=sem(QUAD, pieces),
    )
    names = ["slot", "offset", "mem", "frames", "cot", "bias", "gain", "wq_hbm", "wk_hbm", "wv_hbm", "wo_hbm"]
    names = names + ["grad", "out", "gain_out"] + list(scratch)
    vmem = pl.BlockSpec(memory_space=pltpu.VMEM)
    smem = pl.BlockSpec(memory_space=pltpu.SMEM)
    hbm = pl.BlockSpec(memory_space=pl.ANY)
    grad, weights, gain = pl.pallas_call(
        functools.partial(quad_kernel, owners, groups, heads, tuple(names)),
        out_shape=(
            sds((rows, features), F32), sds((QUAD, part, width), F32), sds((features // 128, 128), F32),
        ),
        in_specs=[smem, smem] + [vmem] * 5 + [hbm] * 4,
        out_specs=(vmem,) * 3,
        scratch_shapes=list(scratch.values()),
        compiler_params=pltpu.CompilerParams(collective_id=0, has_side_effects=True, vmem_limit_bytes=58 * 1024 * 1024),
        name="quad",
    )(
        slot_used[0, 0], start_offset[0], memory[0, 0, 0], frames[0, 0, 0], mem_cot[0, 0, 0],
        key_bias[0, 0, 0][:, None, :], norm_gain.reshape(features // 128, 128), w_query, w_key, w_value, w_out,
    )
    matrix = sds((part, width), F32)
    grad, query, key, value, out, gain = pl.pallas_call(
        hand_over,
        out_shape=(sds((rows, features), F32), matrix, matrix, matrix, matrix, sds((features // 128, 128), F32)),
        in_specs=[vmem] * 3,
        out_specs=(vmem,) * 6,
        name="hand_over",
    )(grad, weights, gain)
    return (grad[None, None, None], query, key, value, out, gain.reshape(features))


def on_device(
    memory, frames, mem_cot, slot_used, key_bias, start_offset, norm_gain, w_query, w_key, w_value, w_out
):
    owners = lax.axis_size("tm")
    groups = lax.axis_size("video")
    position = lax.axis_index("tm")
    streams, rows, features = memory.shape[2:]
    length = frames.shape[3]
    heads = key_bias.shape[3]
    if quad_fits(owners, groups, heads, rows, length, features):
        return quad_call(
            memory, frames, mem_cot, slot_used, key_bias, start_offset, norm_gain, w_query, w_key, w_value, w_out
        )
    members = 2 * groups
    chips = owners // 2
    bits = chips.bit_length() - 1
    width = features // groups
    keyin = key_rows(frames[0, 0, 0], start_offset[0, 0], position)
    vmem = pl.BlockSpec(memory_space=pltpu.VMEM)
    smem = pl.BlockSpec(memory_space=pltpu.SMEM)
    sds = jax.ShapeDtypeStruct
    pw = 128 if width % 128 == 0 else width
    pieces = 2 * (width // pw)
    dma = pltpu.SemaphoreType.DMA
    grad, weights, gain = pl.pallas_call(
        functools.partial(whole_kernel, owners, groups, heads),
        out_shape=(
            sds((rows, features), F32),
            sds((4, features // owners, width), F32),
            sds((1, features), F32),
        ),
        in_specs=[smem] + [vmem] * 9,
        out_specs=(vmem,) * 3,
        scratch_shapes=[
            pltpu.VMEM((members, length, features), F32),
            pltpu.VMEM((members, rows, features), F32),
            pltpu.VMEM((2, groups, length, width), F32),
            pltpu.VMEM((2, groups, rows, width), F32),
            pltpu.VMEM((1, features), F32),
            pltpu.VMEM((rows, features), F32),
            pltpu.VMEM((2, rows, features), F32),
            pltpu.VMEM((rows, heads * length), F32),
            pltpu.VMEM((rows, heads * length), BF16),
            pltpu.VMEM((heads // 2, 2 * length, 2 * features // heads), BF16),
            pltpu.VMEM((heads // 2, 2 * length, 2 * features // heads), BF16),
            pltpu.VMEM((rows, features), BF16),
            pltpu.VMEM((rows, features), BF16),
            pltpu.VMEM((rows, heads * length), BF16),
            pltpu.VMEM((rows, features), BF16),
            pltpu.VMEM((rows, features), BF16),
            pltpu.VMEM((rows, features), F32),
            pltpu.VMEM((rows, 128), F32),
            pltpu.VMEM((features, features), BF16),
            pltpu.VMEM((features, features), BF16),
            dma((CHUNKS,)), dma((CHUNKS,)), dma((2, members)), dma((2, members)),
            pltpu.VMEM((members, length, width), F32),
            pltpu.VMEM((members, rows, width), F32),
            pltpu.VMEM((features, members * length), BF16),
            pltpu.VMEM((features, members * rows), BF16),
            pltpu.VMEM((pieces, features, pw), F32),
            pltpu.VMEM((pieces, features // owners, pw), F32),
            pltpu.VMEM((members, 1, features), F32),
            pltpu.VMEM((bits + 1, 1, features), F32),
            pltpu.VMEM((max(bits, 1), 1, features), F32),
        ]
        + [pltpu.VMEM((pieces, features >> (s + 1), pw), F32) for s in range(bits)]
        + [
            dma((3, members)), dma((3, members)), dma((pieces, bits)), dma((pieces, bits)),
            dma((bits,)), dma((bits,)), dma((pieces,)), dma((pieces,)),
        ],
        compiler_params=pltpu.CompilerParams(collective_id=0, has_side_effects=True, vmem_limit_bytes=58 * 1024 * 1024),
        name="whole",
    )(
        slot_used[0, 0], memory[0, 0, 0], keyin, mem_cot[0, 0, 0], key_bias[0, 0, 0],
        norm_gain[None, :], w_query, w_key, w_value, w_out,
    )
    return (grad[None, None, None], weights[1], weights[2], weights[3], weights[0], gain[0])


def solution(mesh):
    return jax.shard_map(
        on_device,
        mesh=mesh,
        in_specs=(
            P("video", "tm", None, None, None),
            P("video", "tm", None, None, None),
            P("video", "tm", None, None, None),
            P("video", "tm", None),
            P("video", "tm", None, None, None),
            P("video", None),
            P(),
            P(),
            P(),
            P(),
            P(),
        ),
        out_specs=(
            P("video", "tm", None, None, None),
            P("tm", "video"),
            P("tm", "video"),
            P("tm", "video"),
            P("tm", "video"),
            P(),
        ),
        check_vma=False,
    )
```

```python
import functools
import math
import types

import jax
import jax.numpy as jnp
from jax import lax
from jax.experimental import pallas as pl
from jax.experimental.pallas import tpu as pltpu
from jax.sharding import PartitionSpec as P

NORM_EPSILON = 1e-06
MESH = pl.DeviceIdType.MESH
F32 = jnp.float32
BF16 = jnp.bfloat16
NN = (((1,), (0,)), ((), ()))
NT = (((1,), (1,)), ((), ()))
TN = (((0,), (0,)), ((), ()))
CHUNKS = 4


def dot(left, right, form):
    return lax.dot_general(left, right, form, preferred_element_type=F32)


def key_rows(frame_rows, offset, position):
    length, features = frame_rows.shape
    within = jnp.arange(length, dtype=jnp.int32)
    frame_time = (offset + position * length + within).astype(F32)
    half_width = features // 2
    frequency = 0.0625 * jnp.exp(-math.log(1000.0) * jnp.arange(half_width, dtype=F32) / half_width)
    phases = frame_time[:, None] * frequency
    return frame_rows + jnp.concatenate([jnp.sin(phases), jnp.cos(phases)], axis=-1)


def group_member(groups, g):
    me = lax.axis_index("tm")
    return {"video": lax.div(g, 2), "tm": (me // 2) * 2 + lax.rem(g, 2)}


def whole_kernel(
    owners, groups, heads,
    slot_ref, mem_ref, keyin_ref, cot_ref, bias_ref, gain_ref, wq_ref, wk_ref, wv_ref, wo_ref,
    grad_ref, out_ref, gain_out_ref,
    a1_ref, a2_ref, b1_ref, b2_ref, gsum_ref,
    incoming, mine, prob, half, kbd, vbd, qp, att_all, sg_all, og_all, qg_all, unit_ref, inv_ref, wot, wqt,
    chain_send, chain_recv, a_send, a_recv,
    *reduce_scratch,
):
    me = lax.axis_index("tm")
    vid = lax.axis_index("video")
    chips = owners // 2
    bits = chips.bit_length() - 1
    chip, core = me // 2, lax.rem(me, 2)
    peers = [chip + (1 - 2 * lax.rem(lax.div(chip, 2 ** b), 2)) * 2 ** b for b in range(bits)]
    rows, features = mem_ref.shape
    length = keyin_ref.shape[0]
    head = features // heads
    pairs = heads // 2
    pw = 2 * head
    members = 2 * groups
    g_me = vid * 2 + lax.rem(me, 2)
    scale = head ** (-0.5)

    barrier = pltpu.get_barrier_semaphore()
    for off in range(1, members):
        pl.semaphore_signal(barrier, inc=1, device_id=group_member(groups, lax.rem(g_me + off, members)), device_id_type=MESH)

    for peer in peers:
        pl.semaphore_signal(barrier, inc=1, device_id={"tm": peer * 2 + core}, device_id_type=MESH)

    @pl.when(me > 0)
    def _():
        pl.semaphore_signal(barrier, inc=1, device_id={"tm": me - 1}, device_id_type=MESH)

    @pl.when(me < owners - 1)
    def _():
        pl.semaphore_signal(barrier, inc=1, device_id={"tm": me + 1}, device_id_type=MESH)

    ends = jnp.where(me > 0, 1, 0) + jnp.where(me < owners - 1, 1, 0)
    pl.semaphore_wait(barrier, members - 1 + bits + ends)

    def a_copy(which, src, dst, off):
        g = lax.rem(g_me + off, members)
        return pltpu.make_async_remote_copy(
            src_ref=src, dst_ref=dst.at[g_me], send_sem=a_send.at[which, off], recv_sem=a_recv.at[which, g_me],
            device_id=group_member(groups, g), device_id_type=MESH,
        )

    for off in range(1, members):
        a_copy(0, keyin_ref, a1_ref, off).start()
    a1_ref[g_me] = keyin_ref[...]

    mem = mem_ref[...].astype(F32)
    inv = lax.rsqrt(jnp.mean(mem * mem, axis=-1, keepdims=True) + NORM_EPSILON)
    unit = mem * inv
    unit_ref[...] = unit
    inv_ref[...] = jnp.broadcast_to(inv, inv_ref.shape)
    normed = (unit * gain_ref[...]).astype(BF16)
    mine[1] = normed.astype(F32)
    keyin = keyin_ref[...].astype(BF16)
    query = dot(normed, wq_ref[...], NN).astype(BF16)
    qp[...] = query
    kp = dot(keyin, wk_ref[...], NN).astype(BF16)
    vp = dot(keyin, wv_ref[...], NN).astype(BF16)
    low = lax.broadcasted_iota(jnp.int32, (length, pw), 1) < head
    zero = jnp.zeros((length, pw), BF16)
    for p in range(pairs):
        kk = kp[:, p * pw:(p + 1) * pw]
        vv = vp[:, p * pw:(p + 1) * pw]
        kbd[p, :length] = jnp.where(low, kk, zero)
        kbd[p, length:] = jnp.where(low, zero, kk)
        vbd[p, :length] = jnp.where(low, vv, zero)
        vbd[p, length:] = jnp.where(low, zero, vv)
    wot[...] = jnp.transpose(wo_ref[...])
    wqt[...] = jnp.transpose(wq_ref[...])
    scores = [dot(query[:, p * pw:(p + 1) * pw], kbd[p], NT) for p in range(pairs)]
    for p in range(pairs):
        halves = []
        for q in range(2):
            h = 2 * p + q
            s = scores[p][:, q * length:(q + 1) * length] * scale + bias_ref[h:h + 1, :]
            e = jnp.exp(s - jnp.max(s, axis=-1, keepdims=True))
            pr = e / jnp.sum(e, axis=-1, keepdims=True)
            prob[:, h * length:(h + 1) * length] = pr
            halves.append(pr.astype(BF16))
        both = jnp.concatenate(halves, axis=-1)
        half[:, p * 2 * length:(p + 1) * 2 * length] = both
        mine[0, :, p * pw:(p + 1) * pw] = dot(both, vbd[p], NN).astype(BF16).astype(F32)

    for off in range(1, members):
        g = lax.rem(g_me + off, members)
        a_copy(1, mine.at[lax.rem(g, 2)], a2_ref, off).start()
    a2_ref[g_me] = mine[lax.rem(me, 2)]

    live = slot_ref[0].astype(F32)
    step = rows // CHUNKS

    def chain_copy(c):
        return pltpu.make_async_remote_copy(
            src_ref=grad_ref.at[pl.ds(c * step, step)], dst_ref=incoming.at[pl.ds(c * step, step)],
            send_sem=chain_send.at[c], recv_sem=chain_recv.at[c],
            device_id={"tm": jnp.maximum(me - 1, 0)}, device_id_type=MESH,
        )

    @pl.when(me == owners - 1)
    def _():
        incoming[...] = jnp.zeros_like(incoming)

    gain_total = jnp.zeros((1, features), F32)
    for c in range(CHUNKS):
        r = slice(c * step, (c + 1) * step)

        @pl.when(me < owners - 1)
        def _():
            chain_copy(c).wait_recv()

        grad_in = incoming[r, :] + cot_ref[r, :].astype(F32)
        og = (live * grad_in).astype(BF16)
        att = dot(og, wot[...], NN).astype(BF16)
        prob_grads = [dot(att[:, p * pw:(p + 1) * pw], vbd[p], NT) for p in range(pairs)]
        query_grads = []
        score_grads = []
        for p in range(pairs):
            for q in range(2):
                h = 2 * p + q
                pg = prob_grads[p][:, q * length:(q + 1) * length]
                pr = prob[r, h * length:(h + 1) * length]
                inner = jnp.sum(pr * pg, axis=-1, keepdims=True)
                score_grads.append((pr * (pg - inner) * scale).astype(BF16))
            query_grads.append(dot(jnp.concatenate(score_grads[-2:], axis=-1), kbd[p], NN).astype(BF16))
        qg = jnp.concatenate(query_grads, axis=-1)
        ng = dot(qg, wqt[...], NN)
        un = unit_ref[r, :]
        gain_total = gain_total + jnp.sum(ng * un, axis=0, keepdims=True)
        sc = ng * gain_ref[...]
        grad_ref[r, :] = grad_in + inv_ref[r, 0:1] * (sc - un * jnp.mean(sc * un, axis=-1, keepdims=True))

        @pl.when(me > 0)
        def _():
            chain_copy(c).start()

        og_all[r, :] = og
        att_all[r, :] = att
        qg_all[r, :] = qg
        for h in range(heads):
            sg_all[r, h * length:(h + 1) * length] = score_grads[h]

    gsum_ref[...] = gain_total

    width = features // groups
    lowr = lax.broadcasted_iota(jnp.int32, (rows, pw), 1) < head
    zr = jnp.zeros((rows, pw), BF16)

    def put(out, which, p, value):
        for v in range(groups):
            lo, hi = max(p * pw, v * width), min((p + 1) * pw, (v + 1) * width)
            if lo < hi:
                out[which, v, :, lo - v * width:hi - v * width] = value[:, lo - p * pw:hi - p * pw]

    for p in range(pairs):
        for which, (left_ref, right_ref) in enumerate(((sg_all, qp), (half, att_all))):
            right = right_ref[:, p * pw:(p + 1) * pw]
            right = jnp.concatenate([jnp.where(lowr, right, zr), jnp.where(lowr, zr, right)], axis=0)
            base = 2 * p * length
            left = jnp.concatenate([left_ref[:, base:base + length], left_ref[:, base + length:base + 2 * length]], axis=0)
            put(b1_ref, which, p, dot(left, right, TN).astype(BF16).astype(F32))
        put(b2_ref, 0, p, og_all[:, p * pw:(p + 1) * pw].astype(F32))
        put(b2_ref, 1, p, qg_all[:, p * pw:(p + 1) * pw].astype(F32))

    def a_arrive():
        for off in range(1, members):
            g = lax.rem(g_me + members - off, members)
            for which, dst in ((0, a1_ref), (1, a2_ref)):
                a_copy(which, dst.at[g_me], dst, off).wait_send()
                pltpu.make_async_remote_copy(
                    src_ref=dst.at[g], dst_ref=dst.at[g], send_sem=a_send.at[which, off], recv_sem=a_recv.at[which, g],
                    device_id=group_member(groups, g), device_id_type=MESH,
                ).wait_recv()

    reduce_part(
        owners, groups, peers, a_arrive, a1_ref, a2_ref, b1_ref, b2_ref, gsum_ref, out_ref, gain_out_ref, *reduce_scratch
    )

    @pl.when(me > 0)
    def _():
        for c in range(CHUNKS):
            chain_copy(c).wait_send()


def reduce_part(
    owners, groups, peers, a_arrive,
    a1_ref, a2_ref, b1_ref, b2_ref, gsum_ref,
    out_ref, gain_ref,
    s1, s2, t1, t2, acc, final, gslot, gacc, gland, *rest,
):
    me = lax.axis_index("tm")
    vid = lax.axis_index("video")
    members = 2 * groups
    chips = owners // 2
    bits = chips.bit_length() - 1
    lands = rest[:bits]
    b_send, b_recv, r_send, r_recv, q_send, q_recv, f_send, f_recv = rest[bits:]
    chip, core = me // 2, lax.rem(me, 2)
    g_me = vid * 2 + core
    pieces, features, pw = acc.shape
    per = pieces // 2
    block = features // chips
    part = block // 2
    scale = 1.0 / (owners * groups)
    length, rows = a1_ref.shape[1], a2_ref.shape[1]

    def b_copy(which, off):
        g = lax.rem(g_me + off, members)
        v, c = lax.div(g, 2), lax.rem(g, 2)
        src, dst = ((b1_ref.at[c, v], s1), (b2_ref.at[c, v], s2), (gsum_ref, gslot))[which]
        return pltpu.make_async_remote_copy(
            src_ref=src, dst_ref=dst.at[g_me], send_sem=b_send.at[which, off], recv_sem=b_recv.at[which, g_me],
            device_id=group_member(groups, g), device_id_type=MESH,
        )

    def b_arrive(which, off):
        g = lax.rem(g_me + members - off, members)
        dst = (s1, s2, gslot)[which]
        return pltpu.make_async_remote_copy(
            src_ref=dst.at[g], dst_ref=dst.at[g], send_sem=b_send.at[which, off], recv_sem=b_recv.at[which, g],
            device_id=group_member(groups, g), device_id_type=MESH,
        )

    for which in (2, 1, 0):
        for off in range(1, members):
            b_copy(which, off).start()
    s1[g_me] = b1_ref[core, vid]
    s2[g_me] = b2_ref[core, vid]
    gslot[g_me] = gsum_ref[...]
    a_arrive()
    for g in range(members):
        t1[:, g * length:(g + 1) * length] = jnp.transpose(a1_ref[g]).astype(BF16)
    for g in range(0, members, 2):
        both = jnp.concatenate([a2_ref[g], a2_ref[g + 1]], axis=0)
        t2[:, g * rows:(g + 2) * rows] = jnp.transpose(both).astype(BF16)

    order = [int(format(i, "b").zfill(bits)[::-1], 2) if bits else 0 for i in range(chips)]

    def products(which):
        slots, left = ((s2, t2), (s1, t1))[which]
        for off in range(1, members):
            b_arrive(1 - which, off).wait_recv()
        for i in range(per):
            right = slots[:, :, i * pw:(i + 1) * pw].reshape(left.shape[1], pw).astype(BF16)
            value = dot(left[...], right, NN)
            for pos in range(chips):
                k = order[pos]
                acc[which * per + i, pos * block:(pos + 1) * block, :] = value[k * block:(k + 1) * block, :]

    starts = []
    lo = 0
    for s in range(bits):
        span = features >> (s + 1)
        bit = lax.rem(lax.div(chip, 2 ** s), 2)
        starts.append((lo + (1 - bit) * span, lo + bit * span, span, peers[s]))
        lo = lo + bit * span

    def r_copy(p, s):
        give, _, span, peer = starts[s]
        return pltpu.make_async_remote_copy(
            src_ref=acc.at[p, pl.ds(pl.multiple_of(give, 8), span)], dst_ref=lands[s].at[p],
            send_sem=r_send.at[p, s], recv_sem=r_recv.at[p, s],
            device_id={"tm": peer * 2 + core}, device_id_type=MESH,
        )

    def g_copy(s):
        return pltpu.make_async_remote_copy(
            src_ref=gacc.at[s], dst_ref=gland.at[s], send_sem=q_send.at[s], recv_sem=q_recv.at[s],
            device_id={"tm": peers[s] * 2 + core}, device_id_type=MESH,
        )

    def r_finish(p, s):
        _, keep, span, _ = starts[s]
        r_copy(p, s).wait_recv()
        at = pl.ds(pl.multiple_of(keep, 8), span)
        acc[p, at, :] = acc[p, at, :] + lands[s][p]

    def f_copy(p):
        theirs = pl.ds(pl.multiple_of(lo + (1 - core) * part, 8), part)
        return pltpu.make_async_remote_copy(
            src_ref=acc.at[p, theirs], dst_ref=final.at[p], send_sem=f_send.at[p], recv_sem=f_recv.at[p],
            device_id={"tm": chip * 2 + 1 - core}, device_id_type=MESH,
        )

    for wave in range(pieces + bits):
        if wave == 0:
            products(0)
        if wave == per:
            products(1)
        for s in reversed(range(bits + 1)):
            p = wave - s
            if 0 <= p < pieces:
                if s > 0:
                    r_finish(p, s - 1)
                if s < bits:
                    r_copy(p, s).start()
                else:
                    f_copy(p).start()
        if wave == 0:
            for off in range(1, members):
                b_arrive(2, off).wait_recv()
            gacc[0] = jnp.sum(gslot[...], axis=0)
        if 0 < wave <= bits:
            g_copy(wave - 1).wait_recv()
            gacc[wave] = gacc[wave - 1] + gland[wave - 1]
        if wave < bits:
            g_copy(wave).start()

    mine_rows = pl.ds(pl.multiple_of(lo + core * part, 8), part)
    for p in range(pieces):
        which, i = p // per, p % per
        cols = slice(i * pw, (i + 1) * pw)
        out_ref[2 * which + core, :, cols] = acc[p, mine_rows, :] * scale
    for p in range(pieces):
        which, i = p // per, p % per
        cols = slice(i * pw, (i + 1) * pw)
        f_copy(p).wait_recv()
        out_ref[2 * which + 1 - core, :, cols] = final[p] * scale

    gain_ref[...] = gacc[bits] * scale
    for s in range(bits):
        g_copy(s).wait_send()
    for which in range(3):
        for off in range(1, members):
            b_copy(which, off).wait_send()
    for p in range(pieces):
        for s in range(bits):
            r_copy(p, s).wait_send()
        f_copy(p).wait_send()


QUAD = 4


def xor_bits(value, bits):
    high, low = lax.div(value, 2), lax.rem(value, 2)
    if bits & 2:
        high = 1 - high
    if bits & 1:
        low = 1 - low
    return high * 2 + low


def encoded(frames_ref, first_time, put):
    length, features = frames_ref.shape
    half_width = features // 2
    index = lax.broadcasted_iota(jnp.int32, (1, half_width), 1).astype(F32)
    frequency = 0.0625 * jnp.exp(-math.log(1000.0) * index / half_width)
    groups_of = length // 8
    outer = first_time + 8 * lax.broadcasted_iota(jnp.int32, (groups_of, half_width), 0)
    inner = lax.broadcasted_iota(jnp.int32, (8, half_width), 0)
    outer, inner = outer.astype(F32) * frequency, inner.astype(F32) * frequency
    so, co, si, ci = jnp.sin(outer), jnp.cos(outer), jnp.sin(inner), jnp.cos(inner)
    for a in range(groups_of):
        s, c = so[a:a + 1], co[a:a + 1]
        r = slice(a * 8, (a + 1) * 8)
        put(r, slice(0, half_width), frames_ref[r, :half_width] + (s * ci + c * si))
        put(r, slice(half_width, features), frames_ref[r, half_width:] + (c * ci - s * si))


def quad_kernel(owners, groups, heads, names, *refs):
    b = types.SimpleNamespace(**dict(zip(names, refs)))
    me = lax.axis_index("tm")
    vid = lax.axis_index("video")
    planes = owners // QUAD
    plane, q = lax.div(me, QUAD), lax.rem(me, QUAD)
    y = lax.div(q, 2)
    members = groups * QUAD
    mine = vid * QUAD + q
    rows, features = b.mem.shape
    length = b.frames.shape[0]
    head = features // heads
    pairs = heads // 2
    pw = 2 * head
    blk = rows // QUAD
    pieces = pairs // groups
    span = features // planes
    part = features // owners
    scale = head ** (-0.5)
    q1, q2, q3 = xor_bits(q, 1), xor_bits(q, 2), xor_bits(q, 3)
    core = lax.rem(q, 2)
    last, rest = plane == planes - 1, plane < planes - 1
    last_low = jnp.logical_and(last, y == 0)
    last_high = jnp.logical_and(last, y == 1)
    own_half, other_half = pl.ds(2 * core, 2), pl.ds(2 * (1 - core), 2)
    pending = []

    def dev(v, at, qq):
        return {"video": v, "tm": at * QUAD + qq}

    def member(g):
        return dev(lax.div(g, QUAD), plane, lax.rem(g, QUAD))

    def remote(src, dst, ss, rs, to):
        return pltpu.make_async_remote_copy(
            src_ref=src, dst_ref=dst, send_sem=ss, recv_sem=rs, device_id=to, device_id_type=MESH
        )

    def guarded(cond, act):
        if cond is None:
            act()
        else:
            pl.when(cond)(act)

    def send(cond, *copy):
        guarded(cond, lambda: remote(*copy).start())
        pending.append((cond, copy))

    def arrived(dst, rs):
        remote(dst, dst, b.dummy.at[0], rs, dev(vid, plane, q1)).wait_recv()

    weights = [(b.wq_hbm, b.wq), (b.wk_hbm, b.wk), (b.wv_hbm, b.wv), (b.wo_hbm, b.wo)]

    def load(k):
        return pltpu.make_async_copy(weights[k][0], weights[k][1], b.w_sem.at[k])

    for k in (1, 2, 0, 3):
        load(k).start()

    barrier = pltpu.get_barrier_semaphore()
    for off in range(1, members):
        pl.semaphore_signal(barrier, inc=1, device_id=member(lax.rem(mine + off, members)), device_id_type=MESH)
    for off in range(1, planes):
        pl.semaphore_signal(
            barrier, inc=1, device_id=dev(vid, lax.rem(plane + off, planes), q), device_id_type=MESH
        )

    @pl.when(plane == planes - 2)
    def _():
        pl.semaphore_signal(
            barrier, inc=1, device_id=dev(vid, jnp.minimum(plane + 1, planes - 1), y), device_id_type=MESH
        )

    def put_key(r, cols, value):
        b.kin[vid, q, r, cols] = value

    encoded(b.frames, b.offset[0] + me * length, put_key)
    for h in range(heads):
        b.misc[vid, q, h:h + 1, :] = b.bias[h]
    b.misc[vid, q, heads:heads + 1, :] = jnp.zeros((1, length), F32) + b.slot[0].astype(F32)
    for j in range(QUAD):
        b.pack_out[j, :blk] = b.mem[j * blk:(j + 1) * blk, :].astype(F32)
        b.pack_out[j, blk:] = b.cot[j * blk:(j + 1) * blk, :].astype(F32)

    @pl.when(rest)
    def _():
        b.pack[q] = b.pack_out[q]

    @pl.when(last)
    def _():
        b.pack[own_half] = b.pack_out[own_half]

    pl.semaphore_wait(barrier, members - 1 + planes - 1 + jnp.where(last_low, 2 if planes > 1 else 0, 0))

    def send_key(cond, slot, sem, to):
        send(cond, b.kin.at[vid, slot], b.kin.at[vid, slot], b.kin_send.at[sem], b.kin_recv.at[vid, slot], to)

    def send_misc(cond, sem, to):
        send(cond, b.misc.at[vid, q], b.misc.at[vid, q], b.misc_send.at[sem], b.misc_recv.at[vid, q], to)

    send_key(rest, q, 0, dev(vid, plane, q2))
    send_key(None, q, 1, dev(vid, plane, q1))
    for k, other in ((0, q1), (1, q2), (2, q3)):
        to = dev(vid, plane, other)
        send_misc(None, k, to)
        send(rest, b.pack_out.at[other], b.pack.at[q], b.pack_send.at[k], b.pack_recv.at[q], to)
    send(
        last, b.pack_out.at[other_half], b.pack.at[own_half], b.pack_send.at[0], b.pack_recv.at[q],
        dev(vid, plane, q1),
    )
    for off in range(1, groups):
        send_key(y == 0, q, 3 * off, dev(lax.rem(vid + off, groups), plane, q))
        send_misc(None, 2 + off, dev(lax.rem(vid + off, groups), plane, core))

    low = lax.broadcasted_iota(jnp.int32, (length, pw), 1) < head
    zero = jnp.zeros((length, pw), BF16)

    def project(slot):
        keyin = b.kin[vid, slot].astype(BF16)
        kp = dot(keyin, b.wk[...], NN).astype(BF16)
        vp = dot(keyin, b.wv[...], NN).astype(BF16)
        for p in range(pairs):
            kk = kp[:, p * pw:(p + 1) * pw]
            vv = vp[:, p * pw:(p + 1) * pw]
            b.kbd[slot, p, :length] = jnp.where(low, kk, zero)
            b.kbd[slot, p, length:] = jnp.where(low, zero, kk)
            b.vbd[slot, p, :length] = jnp.where(low, vv, zero)
            b.vbd[slot, p, length:] = jnp.where(low, zero, vv)

    for k in (1, 2, 0, 3):
        load(k).wait()
    project(q)
    b.wot[...] = jnp.transpose(b.wo[...])
    b.wqt[...] = jnp.transpose(b.wq[...])
    arrived(b.kin.at[vid, q1], b.kin_recv.at[vid, q1])
    project(q1)
    for other in (q1, q2, q3):
        arrived(b.misc.at[vid, other], b.misc_recv.at[vid, other])

    def pass_on(cond):
        guarded(cond, lambda: arrived(b.kin.at[vid, q2], b.kin_recv.at[vid, q2]))
        send_key(cond, q2, 2, dev(vid, plane, q1))

    def cross(cond):
        for off in range(1, groups):
            send_key(cond, q, 3 * off + 1, dev(lax.rem(vid + off, groups), plane, core))

    pass_on(rest)

    @pl.when(rest)
    def _():
        project(q2)
        arrived(b.kin.at[vid, q3], b.kin_recv.at[vid, q3])
        project(q3)
        for other in (q1, q2, q3):
            arrived(b.pack.at[other], b.pack_recv.at[other])

    @pl.when(last)
    def _():
        arrived(b.pack.at[other_half], b.pack_recv.at[q1])

    cross(jnp.logical_and(rest, y == 1))

    gain = jnp.concatenate([b.gain[k:k + 1, :] for k in range(b.gain.shape[0])], axis=-1)
    mem = jnp.concatenate([b.pack[j, :blk] for j in range(QUAD)], axis=0)
    inv = lax.rsqrt(jnp.mean(mem * mem, axis=-1, keepdims=True) + NORM_EPSILON)
    unit = mem * inv
    b.unit[...] = unit
    b.inv[...] = jnp.broadcast_to(inv, b.inv.shape)
    normed = (unit * gain).astype(BF16)
    b.normed[...] = normed.astype(F32)
    query = dot(normed, b.wq[...], NN).astype(BF16)
    for p in range(pairs):
        b.qp[p] = query[:, p * pw:(p + 1) * pw].astype(F32)
    def attend(r, slot):
        scores = [dot(query[r, p * pw:(p + 1) * pw], b.kbd[slot, p], NT) for p in range(pairs)]
        for p in range(pairs):
            halves = []
            for k in range(2):
                h = 2 * p + k
                sc = scores[p][:, k * length:(k + 1) * length] * scale + b.misc[vid, slot, h:h + 1, :]
                e = jnp.exp(sc - jnp.max(sc, axis=-1, keepdims=True))
                pr = e / jnp.sum(e, axis=-1, keepdims=True)
                b.prob[r, h * length:(h + 1) * length] = pr
                halves.append(pr.astype(BF16))
            both = jnp.concatenate(halves, axis=-1)
            b.attended[r, p * pw:(p + 1) * pw] = dot(both, b.vbd[slot, p], NN).astype(BF16).astype(F32)

    singles = [(slice(j * blk, (j + 1) * blk), (j,)) for j in reversed(range(QUAD))]
    doubles = [(slice(2 * a * blk, 2 * (a + 1) * blk), (2 * a, 2 * a + 1)) for a in (1, 0)]

    @pl.when(rest)
    def _():
        for r, (j,) in singles:
            attend(r, j)

    @pl.when(last)
    def _():
        for r, (k, _) in doubles:
            attend(r, 2 * y + k // 2)

    def qp_of(v):
        return b.qp.at[pl.ds(v * pieces, pieces)]

    for off in range(groups):
        v = lax.rem(vid + off, groups)
        send(
            y != 0 if off == 0 else None, qp_of(v), b.query.at[mine], b.early_send.at[0, off],
            b.early_recv.at[mine], dev(v, plane, core),
        )
    for off in range(groups):
        v = lax.rem(vid + off, groups)
        for role, src in ((2, b.attended), (3, b.normed)):
            send(
                q != role if off == 0 else None, src, b.early.at[mine], b.early_send.at[role, off],
                b.early_recv.at[mine], dev(v, plane, role),
            )

    @pl.when(y == 0)
    def _():
        b.query[mine] = qp_of(vid)[...]

    for role, src in ((2, b.attended), (3, b.normed)):
        @pl.when(q == role)
        def _():
            b.early[mine] = src[...]

    def same_core(side):
        return [
            (off, e, lax.rem(vid + off, groups) * QUAD + 2 * e + side) for off in range(groups) for e in range(2)
        ]

    def share(ref, index, recv, ss, stage):
        for off, e, g in same_core(core):
            at = ref.at[(g, *index)]
            copy = remote(at, at, ss.at[(off, e, *index)], recv.at[(g, *index)], dev(vid, plane, q1))
            if stage == 0 and (off, e) != (0, 0):
                arrived(at, recv.at[(g, *index)])
            if stage == 0:
                copy.start()
            if stage == 2:
                copy.wait_send()
        if stage == 1:
            for off, e, g in same_core(1 - core):
                arrived(ref.at[(g, *index)], recv.at[(g, *index)])

    def forward(off, k, v, slot):
        at, to = b.kin.at[v, slot], dev(vid, plane, q1)
        small = b.misc.at[v, slot]
        return (
            remote(at, at, b.fwd_send.at[off, k], b.kin_recv.at[v, slot], to),
            remote(small, small, b.fwdm_send.at[off, k], b.misc_recv.at[v, slot], to),
        )

    def gather(ref, v, i, j):
        parts = []
        for k in range(QUAD):
            g = v * QUAD + jnp.where(last, 2 * (j // 2) + k // 2, k)
            at = jnp.where(last, (2 * (j % 2) + k % 2) * blk, j * blk)
            parts.append(ref[g, i, pl.ds(pl.multiple_of(at, blk), blk), :])
        return jnp.concatenate(parts, axis=0).astype(BF16)

    half_cols = pl.ds(pl.multiple_of(vid * pieces * pw, 128), pieces * pw)

    def apart(value, p, out, g):
        vv = value[:, p * pw:(p + 1) * pw]
        out[g, p, :length] = jnp.where(low, vv, zero)
        out[g, p, length:] = jnp.where(low, zero, vv)

    def prepare(v):
        @pl.loop(0, QUAD // 2)
        def _(n):
            pair = [v * QUAD + 2 * n + k for k in range(2)]
            keyin = jnp.concatenate([b.kin[v, 2 * n + k].astype(BF16) for k in range(2)], axis=0)
            at = pl.ds(pl.multiple_of(pair[0] * length, 128), 2 * length)
            b.left[:, at] = jnp.transpose(keyin)

            def halves_of(weight, out):
                value = dot(keyin, weight[:, half_cols], NN).astype(BF16)
                for k in range(2):
                    for p in range(pieces):
                        apart(value[k * length:(k + 1) * length], p, out, pair[k])

            halves_of(b.wk, b.khalf)
            pl.when(q == 0)(lambda: halves_of(b.wv, b.vhalf))

    @pl.when(jnp.logical_and(y == 0, plane < planes // 2))
    def _():
        prepare(vid)

    def early_keys():
        guarded(last, lambda: arrived(b.kin.at[vid, q3], b.kin_recv.at[vid, q3]))
        for off in range(1, groups):
            v = lax.rem(vid + off, groups)
            for k, slot in ((0, q), (1, q2)):
                arrived(b.kin.at[v, slot], b.kin_recv.at[v, slot])
                arrived(b.misc.at[v, slot], b.misc_recv.at[v, slot])
                for copy in forward(off, k, v, slot):
                    copy.start()

        @pl.when(plane >= planes // 2)
        def _():
            prepare(vid)

        for off in range(1, groups):
            v = lax.rem(vid + off, groups)
            for slot in (q1, q3):
                arrived(b.kin.at[v, slot], b.kin_recv.at[v, slot])
                arrived(b.misc.at[v, slot], b.misc_recv.at[v, slot])
            prepare(v)

    @pl.when(jnp.logical_and(y == 0, plane < planes // 4))
    def _():
        early_keys()

    def early_low():
        share(b.query, (), b.early_recv, b.query_send, 0)

        @pl.when(plane >= planes // 4)
        def _():
            early_keys()

        share(b.query, (), b.early_recv, b.query_send, 1)

        @pl.loop(0, pieces)
        def _(i):
            clips = [(v, j) for v in range(groups) for j in range(QUAD)]
            found = []
            for v, j in clips:
                scores = dot(gather(b.query, v, i, j), b.khalf[v * QUAD + j, i], NT)
                for k in range(2):
                    h = 2 * (vid * pieces + i) + k
                    sc = scores[:, k * length:(k + 1) * length] * scale + b.misc[v, j, pl.ds(h, 1), :]
                    e = jnp.exp(sc - jnp.max(sc, axis=-1, keepdims=True))
                    found.append(e / jnp.sum(e, axis=-1, keepdims=True))
            for n, (v, j) in enumerate(clips):
                for k in range(2):
                    b.wide[v * QUAD + j, i, :, k * length:(k + 1) * length] = found[2 * n + k]

    def early_high():
        for off in range(1, members):
            g = lax.rem(mine + off, members)
            arrived(b.early.at[g], b.early_recv.at[g])
        for g in range(0, members, 2):
            both = jnp.concatenate([b.early[g], b.early[g + 1]], axis=0)
            b.left[:, g * rows:(g + 2) * rows] = jnp.transpose(both.astype(BF16))

    below = jnp.maximum(plane - 1, 0)
    single_to = (
        jnp.logical_and(rest, plane > 0),
        (b.passed.at[0], b.incoming, b.chain_send.at[0], b.chain_recv.at[0], dev(vid, below, q)),
    )
    across_to = (
        last_high,
        (b.passed.at[pl.ds(0, 2)], b.across, b.chain_send.at[0], b.across_recv.at[0], dev(vid, plane, q2)),
    )
    double_to = [
        (
            jnp.logical_and(last_low, plane > 0),
            (b.passed.at[k], b.incoming, b.chain_send.at[k], b.chain_recv.at[0], dev(vid, below, 2 * core + k)),
        )
        for k in range(2)
    ]

    def step(r, blocks, slot, carried, outgoing):
        grad_in = carried + jnp.concatenate([b.pack[k, blk:] for k in blocks], axis=0)
        live = jnp.concatenate([b.misc[vid, slot, heads:heads + 1, :]] * (features // length), axis=-1)
        og = (live * grad_in).astype(BF16)
        att = dot(og, b.wot[...], NN).astype(BF16)
        prob_grads = [dot(att[:, p * pw:(p + 1) * pw], b.vbd[slot, p], NT) for p in range(pairs)]
        query_grads = []
        for p in range(pairs):
            halves = []
            for k in range(2):
                h = 2 * p + k
                pg = prob_grads[p][:, k * length:(k + 1) * length]
                pr = b.prob[r, h * length:(h + 1) * length]
                inner = jnp.sum(pr * pg, axis=-1, keepdims=True)
                halves.append((pr * (pg - inner) * scale).astype(BF16))
            both = jnp.concatenate(halves, axis=-1)
            query_grads.append(dot(both, b.kbd[slot, p], NN).astype(BF16))
        qg = jnp.concatenate(query_grads, axis=-1)
        ng = dot(qg, b.wqt[...], NN)
        un = b.unit[r, :]
        sc = ng * gain
        carried = grad_in + b.inv[r, 0:1] * (sc - un * jnp.mean(sc * un, axis=-1, keepdims=True))
        for n, k in enumerate(blocks):
            b.passed[k] = carried[n * blk:(n + 1) * blk]
        for cond, copy in outgoing:
            pl.when(cond)(lambda: remote(*copy).start())
        for p in range(pairs):
            cols = slice(p * pw, (p + 1) * pw)
            b.att[p, r, :] = att[:, cols].astype(F32)
            b.og[p, r, :] = og[:, cols].astype(F32)
            b.qg[p, r, :] = qg[:, cols].astype(F32)
        return carried, jnp.sum(ng * un, axis=0, keepdims=True)

    pending.extend([single_to, across_to] + double_to)

    @pl.when(rest)
    def _():
        arrived(b.incoming, b.chain_recv.at[0])
        gain_total = jnp.zeros((1, features), F32)
        carried = b.incoming[...]
        for r, (j,) in singles:
            carried, gain_part = step(r, (j,), j, carried, [single_to] if j == 0 else [])
            gain_total = gain_total + gain_part
        b.gsum[mine] = gain_total

    @pl.when(last_high)
    def _():
        b.across[...] = jnp.zeros_like(b.across)

    @pl.when(last_low)
    def _():
        arrived(b.across, b.across_recv.at[0])

    @pl.when(last)
    def _():
        gain_total = jnp.zeros((1, features), F32)
        carried = jnp.concatenate([b.across[0], b.across[1]], axis=0)
        for r, blocks in doubles:
            outgoing = [across_to] + double_to if blocks[0] == 0 else []
            carried, gain_part = step(r, blocks, 2 * y + blocks[0] // 2, carried, outgoing)
            gain_total = gain_total + gain_part
        b.gsum[mine] = gain_total

    send_key(last_high, q, 0, dev(vid, plane, q2))
    cross(last_high)
    for off in range(1, members):
        g = lax.rem(mine + off, members)
        send(None, b.gsum.at[mine], b.gsum.at[mine], b.gsum_send.at[off], b.gsum_recv.at[mine], member(g))

    rounds = [(i, ((0, y != 0, b.att),)) for i in range(pieces)]
    rounds = rounds + [(i, ((2, q != 2, b.og), (3, q != 3, b.qg))) for i in range(pieces)]
    for i, sent in rounds:
        for off in reversed(range(groups)):
            v = lax.rem(vid + off, groups)
            for role, cond, src in sent:
                send(
                    cond if off == 0 else None, src.at[v * pieces + i], b.narrow.at[mine, i],
                    b.late_send.at[i, role, off], b.late_recv.at[mine, i],
                    dev(v, plane, core if role == 0 else role),
                )
    for cond, src in ((y == 0, b.att), (q == 2, b.og), (q == 3, b.qg)):
        @pl.when(cond)
        def _():
            b.narrow[mine] = src[pl.ds(vid * pieces, pieces)]

    for j in range(QUAD):
        send(
            jnp.logical_and(rest, q != j), b.passed.at[j], b.returned.at[q], b.ret_send.at[j], b.ret_recv.at[q],
            dev(vid, plane, j),
        )
    send(
        last, b.passed.at[other_half], b.returned.at[own_half], b.ret_send.at[0], b.ret_recv.at[q],
        dev(vid, plane, q1),
    )
    pass_on(last_low)

    @pl.when(y == 0)
    def _():
        early_low()

    @pl.when(y == 1)
    def _():
        early_high()

    lowr = lax.broadcasted_iota(jnp.int32, (rows, pw), 1) < head
    zr = jnp.zeros((rows, pw), BF16)

    def product(i):
        @pl.when(y == 0)
        def _():
            share(b.narrow, (i,), b.late_recv, b.att_send, 1)

        @pl.when(y == 1)
        def _():
            for off in range(1, members):
                g = lax.rem(mine + off, members)
                arrived(b.narrow.at[g, i], b.late_recv.at[g, i])

        def token_grads(role):
            found = []
            for v in range(groups):
                for j in range(QUAD):
                    g = v * QUAD + j
                    right = att = gather(b.narrow, v, i, j)
                    halves = []
                    if role == 0:
                        right = gather(b.query, v, i, j)
                        prob_grad = dot(att, b.vhalf[g, i], NT)
                    for k in range(2):
                        cols = slice(k * length, (k + 1) * length)
                        pr = b.wide[g, i, :, cols]
                        if role == 0:
                            pg = prob_grad[:, cols]
                            pr = pr * (pg - jnp.sum(pr * pg, axis=-1, keepdims=True)) * scale
                        halves.append(pr.astype(BF16))
                    stacked = jnp.concatenate(halves, axis=0)
                    right = jnp.concatenate([jnp.where(lowr, right, zr), jnp.where(lowr, zr, right)], axis=0)
                    found.append(dot(stacked, right, TN).astype(BF16))
            b.right[...] = jnp.concatenate(found, axis=0)

        for role in range(2):
            pl.when(q == role)(functools.partial(token_grads, role))

        if i + 1 < pieces:
            pl.when(y == 0)(lambda: share(b.narrow, (i + 1,), b.late_recv, b.att_send, 0))

        @pl.when(y == 0)
        def _():
            b.acc[i] = dot(b.left[...], b.right[...], NN)

        @pl.when(y == 1)
        def _():
            right = jnp.concatenate([b.narrow[g, i] for g in range(members)], axis=0).astype(BF16)
            b.acc[i] = dot(b.left[:, :members * rows], right, NN)

    def block(at):
        return pl.ds(pl.multiple_of(at * span, 8), span)

    def flow(i, k, up):
        to = plane + k if up else plane - k
        ok = to < planes if up else to >= 0
        fed = plane > 0 if up else plane < planes - 1
        land, ss, rs = (b.up, b.up_send, b.up_recv) if up else (b.down, b.down_send, b.down_recv)
        to = jnp.clip(to, 0, planes - 1)
        at = block(to)
        step = jnp.clip(plane + 1 if up else plane - 1, 0, planes - 1)

        @pl.when(jnp.logical_and(ok, fed))
        def _():
            arrived(land.at[i, at], rs.at[i, to])
            b.acc[i, at, :] = b.acc[i, at, :] + land[i, at, :]

        return ok, (b.acc.at[i, at], land.at[i, at], ss.at[i, to], rs.at[i, to], dev(vid, step, q))

    def flow_all(i, up, near=1):
        for k in reversed(range(near, planes)):
            ok, copy = flow(i, k, up)
            pl.when(ok)(lambda: remote(*copy).start())

    mean = 1.0 / (owners * groups)

    def settle(i):
        at = block(plane)

        @pl.when(plane < planes - 1)
        def _():
            arrived(b.down.at[i, at], b.down_recv.at[i, plane])
            b.acc[i, at, :] = b.acc[i, at, :] + b.down[i, at, :]

        @pl.when(plane > 0)
        def _():
            arrived(b.up.at[i, at], b.up_recv.at[i, plane])
            b.acc[i, at, :] = b.acc[i, at, :] + b.up[i, at, :]

        b.final[i] = b.acc[i, at, :] * mean
        for k, other in ((0, q1), (1, q2), (2, q3)):
            to = dev(vid, plane, other)
            rows_of = pl.ds(pl.multiple_of(other * part, 8), part)
            send(None, b.final.at[i, rows_of], b.fin_land.at[q, i], b.fin_send.at[k, i], b.fin_recv.at[q, i], to)
        b.out[q, :, i * pw:(i + 1) * pw] = b.final[i, pl.ds(pl.multiple_of(q * part, 8), part), :]

    for off in range(1, members):
        g = lax.rem(mine + off, members)
        arrived(b.gsum.at[g], b.gsum_recv.at[g])
    b.gplane[plane] = jnp.sum(b.gsum[...], axis=0)
    for off in range(1, planes):
        to = dev(vid, lax.rem(plane + off, planes), q)
        send(None, b.gplane.at[plane], b.gplane.at[plane], b.gp_send.at[off], b.gp_recv.at[plane], to)

    @pl.when(y == 0)
    def _():
        share(b.narrow, (0,), b.late_recv, b.att_send, 0)

    for i in range(pieces):
        product(i)
        pl.when(last)(lambda: flow_all(i, False, 2))
        pl.when(plane == 0)(lambda: flow_all(i, True, 2))

    @pl.when(jnp.logical_and(plane == 0, planes > 1))
    def _():
        for i in range(pieces):
            remote(*flow(i, 1, True)[1]).start()

    @pl.when(jnp.logical_and(last, planes > 1))
    def _():
        for i in range(pieces):
            remote(*flow(i, 1, False)[1]).start()

    @pl.when(jnp.logical_and(plane > 0, rest))
    def _():
        @pl.loop(0, pieces)
        def _(i):
            flow_all(i, False, 2)
            flow_all(i, True, 2)

        @pl.loop(0, pieces)
        def _(i):
            for up in (False, True):
                ok, copy = flow(i, 1, up)
                pl.when(ok)(lambda: remote(*copy).start())

    for i in range(pieces):
        settle(i)

    def block_rows(at):
        return pl.ds(pl.multiple_of(at * blk, 8), blk)

    @pl.when(rest)
    def _():
        b.grad[block_rows(q), :] = b.passed[q]
        for other in (q1, q2, q3):
            arrived(b.returned.at[other], b.ret_recv.at[other])
            b.grad[block_rows(other), :] = b.returned[other]

    @pl.when(last)
    def _():
        arrived(b.returned.at[other_half], b.ret_recv.at[q1])
        for k in range(2):
            mine_at, other_at = 2 * core + k, 2 * (1 - core) + k
            b.grad[block_rows(mine_at), :] = b.passed[mine_at]
            b.grad[block_rows(other_at), :] = b.returned[other_at]
    for off in range(1, planes):
        at = lax.rem(plane + off, planes)
        arrived(b.gplane.at[at], b.gp_recv.at[at])
    total = jnp.sum(b.gplane[...], axis=0) * mean
    for k in range(b.gain_out.shape[0]):
        b.gain_out[k:k + 1, :] = total[:, k * 128:(k + 1) * 128]
    for i in range(pieces):
        for other in (q1, q2, q3):
            arrived(b.fin_land.at[other, i], b.fin_recv.at[other, i])
            b.out[other, :, i * pw:(i + 1) * pw] = b.fin_land[other, i]

    for cond, copy in pending:
        guarded(cond, lambda: remote(*copy).wait_send())

    @pl.when(y == 0)
    def _():
        for off in range(1, groups):
            v = lax.rem(vid + off, groups)
            for k, slot in ((0, q), (1, q2)):
                for copy in forward(off, k, v, slot):
                    copy.wait_send()
        share(b.query, (), b.early_recv, b.query_send, 2)
        for i in range(pieces):
            share(b.narrow, (i,), b.late_recv, b.att_send, 2)

    for i in range(pieces):
        for up in (False, True):
            for k in range(1, planes):
                to = plane + k if up else plane - k
                ok = to < planes if up else to >= 0
                to = jnp.clip(to, 0, planes - 1)
                land, ss, rs = (b.up, b.up_send, b.up_recv) if up else (b.down, b.down_send, b.down_recv)

                @pl.when(ok)
                def _():
                    remote(
                        b.acc.at[i, block(to)], land.at[i, block(to)], ss.at[i, to], rs.at[i, to],
                        dev(vid, jnp.clip(plane + 1 if up else plane - 1, 0, planes - 1), q),
                    ).wait_send()


def hand_over(grad, weights, gain, grad_out, query_out, key_out, value_out, out_out, gain_out):
    grad_out[...] = grad[...]
    for k, ref in enumerate((key_out, value_out, out_out, query_out)):
        ref[...] = weights[k]
    gain_out[...] = gain[...]


def quad_fits(owners, groups, heads, rows, length, features):
    pw = 2 * features // heads
    return (
        owners % QUAD == 0 and rows % (16 * QUAD) == 0 and length % 128 == 0 and pw == 128 and length == pw
        and (heads // 2) % groups == 0 and features % (8 * owners) == 0 and features % 256 == 0
    )


def quad_call(memory, frames, mem_cot, slot_used, key_bias, start_offset, norm_gain, w_query, w_key, w_value, w_out):
    owners = lax.axis_size("tm")
    groups = lax.axis_size("video")
    rows, features = memory.shape[3:]
    length = frames.shape[3]
    heads = key_bias.shape[3]
    planes = owners // QUAD
    members = groups * QUAD
    pairs = heads // 2
    pieces = pairs // groups
    pw = 2 * features // heads
    blk = rows // QUAD
    part = features // owners
    width = features // groups
    vm, sds = pltpu.VMEM, jax.ShapeDtypeStruct
    sem = lambda *shape: pltpu.SemaphoreType.DMA(shape)
    scratch = dict(
        kin=vm((groups, QUAD, length, features), F32), misc=vm((groups, QUAD, 16, length), F32),
        pack_out=vm((QUAD, 2 * blk, features), F32), pack=vm((QUAD, 2 * blk, features), F32),
        wq=vm((features, features), BF16), wk=vm((features, features), BF16),
        wv=vm((features, features), BF16), wo=vm((features, features), BF16),
        wot=vm((features, features), BF16), wqt=vm((features, features), BF16),
        kbd=vm((QUAD, pairs, 2 * length, pw), BF16), vbd=vm((QUAD, pairs, 2 * length, pw), BF16),
        unit=vm((rows, features), F32), inv=vm((rows, 128), F32), prob=vm((rows, heads * length), F32),
        normed=vm((rows, features), F32), attended=vm((rows, features), F32),
        qp=vm((pairs, rows, pw), F32), att=vm((pairs, rows, pw), F32),
        og=vm((pairs, rows, pw), F32), qg=vm((pairs, rows, pw), F32),
        query=vm((members, pieces, rows, pw), F32), khalf=vm((members, pieces, 2 * length, pw), BF16),
        vhalf=vm((members, pieces, 2 * length, pw), BF16),
        wide=vm((members, pieces, rows, 2 * length), F32), narrow=vm((members, pieces, rows, pw), F32),
        early=vm((members, rows, features), F32), left=vm((features, members * length), BF16),
        right=vm((members * length, pw), BF16), acc=vm((pieces, features, pw), F32),
        up=vm((pieces, features, pw), F32), down=vm((pieces, features, pw), F32),
        final=vm((pieces, features // planes, pw), F32), fin_land=vm((QUAD, pieces, part, pw), F32),
        incoming=vm((blk, features), F32), across=vm((2, blk, features), F32), passed=vm((QUAD, blk, features), F32),
        returned=vm((QUAD, blk, features), F32),
        gsum=vm((members, 1, features), F32), gplane=vm((planes, 1, features), F32),
        dummy=sem(1), w_sem=sem(4), kin_send=sem(3 * groups), kin_recv=sem(groups, QUAD),
        misc_send=sem(2 + groups), misc_recv=sem(groups, QUAD), pack_send=sem(3), pack_recv=sem(QUAD),
        early_send=sem(QUAD, groups), early_recv=sem(members), fwd_send=sem(groups, 2), fwdm_send=sem(groups, 2), query_send=sem(groups, 2), att_send=sem(groups, 2, pieces),
        chain_send=sem(2), chain_recv=sem(1), across_recv=sem(1), gsum_send=sem(members), gsum_recv=sem(members),
        late_send=sem(pieces, QUAD, groups), late_recv=sem(members, pieces),
        ret_send=sem(QUAD), ret_recv=sem(QUAD), gp_send=sem(planes), gp_recv=sem(planes),
        up_send=sem(pieces, planes), up_recv=sem(pieces, planes),
        down_send=sem(pieces, planes), down_recv=sem(pieces, planes),
        fin_send=sem(3, pieces), fin_recv=sem(QUAD, pieces),
    )
    names = ["slot", "offset", "mem", "frames", "cot", "bias", "gain", "wq_hbm", "wk_hbm", "wv_hbm", "wo_hbm"]
    names = names + ["grad", "out", "gain_out"] + list(scratch)
    vmem = pl.BlockSpec(memory_space=pltpu.VMEM)
    smem = pl.BlockSpec(memory_space=pltpu.SMEM)
    hbm = pl.BlockSpec(memory_space=pl.ANY)
    grad, weights, gain = pl.pallas_call(
        functools.partial(quad_kernel, owners, groups, heads, tuple(names)),
        out_shape=(
            sds((rows, features), F32), sds((QUAD, part, width), F32), sds((features // 128, 128), F32),
        ),
        in_specs=[smem, smem] + [vmem] * 5 + [hbm] * 4,
        out_specs=(vmem,) * 3,
        scratch_shapes=list(scratch.values()),
        compiler_params=pltpu.CompilerParams(collective_id=0, has_side_effects=True, vmem_limit_bytes=58 * 1024 * 1024),
        name="quad",
    )(
        slot_used[0, 0], start_offset[0], memory[0, 0, 0], frames[0, 0, 0], mem_cot[0, 0, 0],
        key_bias[0, 0, 0][:, None, :], norm_gain.reshape(features // 128, 128), w_query, w_key, w_value, w_out,
    )
    matrix = sds((part, width), F32)
    grad, query, key, value, out, gain = pl.pallas_call(
        hand_over,
        out_shape=(sds((rows, features), F32), matrix, matrix, matrix, matrix, sds((features // 128, 128), F32)),
        in_specs=[vmem] * 3,
        out_specs=(vmem,) * 6,
        name="hand_over",
    )(grad, weights, gain)
    return (grad[None, None, None], query, key, value, out, gain.reshape(features))


def on_device(
    memory, frames, mem_cot, slot_used, key_bias, start_offset, norm_gain, w_query, w_key, w_value, w_out
):
    owners = lax.axis_size("tm")
    groups = lax.axis_size("video")
    position = lax.axis_index("tm")
    streams, rows, features = memory.shape[2:]
    length = frames.shape[3]
    heads = key_bias.shape[3]
    if quad_fits(owners, groups, heads, rows, length, features):
        return quad_call(
            memory, frames, mem_cot, slot_used, key_bias, start_offset, norm_gain, w_query, w_key, w_value, w_out
        )
    members = 2 * groups
    chips = owners // 2
    bits = chips.bit_length() - 1
    width = features // groups
    keyin = key_rows(frames[0, 0, 0], start_offset[0, 0], position)
    vmem = pl.BlockSpec(memory_space=pltpu.VMEM)
    smem = pl.BlockSpec(memory_space=pltpu.SMEM)
    sds = jax.ShapeDtypeStruct
    pw = 128 if width % 128 == 0 else width
    pieces = 2 * (width // pw)
    dma = pltpu.SemaphoreType.DMA
    grad, weights, gain = pl.pallas_call(
        functools.partial(whole_kernel, owners, groups, heads),
        out_shape=(
            sds((rows, features), F32),
            sds((4, features // owners, width), F32),
            sds((1, features), F32),
        ),
        in_specs=[smem] + [vmem] * 9,
        out_specs=(vmem,) * 3,
        scratch_shapes=[
            pltpu.VMEM((members, length, features), F32),
            pltpu.VMEM((members, rows, features), F32),
            pltpu.VMEM((2, groups, length, width), F32),
            pltpu.VMEM((2, groups, rows, width), F32),
            pltpu.VMEM((1, features), F32),
            pltpu.VMEM((rows, features), F32),
            pltpu.VMEM((2, rows, features), F32),
            pltpu.VMEM((rows, heads * length), F32),
            pltpu.VMEM((rows, heads * length), BF16),
            pltpu.VMEM((heads // 2, 2 * length, 2 * features // heads), BF16),
            pltpu.VMEM((heads // 2, 2 * length, 2 * features // heads), BF16),
            pltpu.VMEM((rows, features), BF16),
            pltpu.VMEM((rows, features), BF16),
            pltpu.VMEM((rows, heads * length), BF16),
            pltpu.VMEM((rows, features), BF16),
            pltpu.VMEM((rows, features), BF16),
            pltpu.VMEM((rows, features), F32),
            pltpu.VMEM((rows, 128), F32),
            pltpu.VMEM((features, features), BF16),
            pltpu.VMEM((features, features), BF16),
            dma((CHUNKS,)), dma((CHUNKS,)), dma((2, members)), dma((2, members)),
            pltpu.VMEM((members, length, width), F32),
            pltpu.VMEM((members, rows, width), F32),
            pltpu.VMEM((features, members * length), BF16),
            pltpu.VMEM((features, members * rows), BF16),
            pltpu.VMEM((pieces, features, pw), F32),
            pltpu.VMEM((pieces, features // owners, pw), F32),
            pltpu.VMEM((members, 1, features), F32),
            pltpu.VMEM((bits + 1, 1, features), F32),
            pltpu.VMEM((max(bits, 1), 1, features), F32),
        ]
        + [pltpu.VMEM((pieces, features >> (s + 1), pw), F32) for s in range(bits)]
        + [
            dma((3, members)), dma((3, members)), dma((pieces, bits)), dma((pieces, bits)),
            dma((bits,)), dma((bits,)), dma((pieces,)), dma((pieces,)),
        ],
        compiler_params=pltpu.CompilerParams(collective_id=0, has_side_effects=True, vmem_limit_bytes=58 * 1024 * 1024),
        name="whole",
    )(
        slot_used[0, 0], memory[0, 0, 0], keyin, mem_cot[0, 0, 0], key_bias[0, 0, 0],
        norm_gain[None, :], w_query, w_key, w_value, w_out,
    )
    return (grad[None, None, None], weights[1], weights[2], weights[3], weights[0], gain[0])


def solution(mesh):
    return jax.shard_map(
        on_device,
        mesh=mesh,
        in_specs=(
            P("video", "tm", None, None, None),
            P("video", "tm", None, None, None),
            P("video", "tm", None, None, None),
            P("video", "tm", None),
            P("video", "tm", None, None, None),
            P("video", None),
            P(),
            P(),
            P(),
            P(),
            P(),
        ),
        out_specs=(
            P("video", "tm", None, None, None),
            P("tm", "video"),
            P("tm", "video"),
            P("tm", "video"),
            P("tm", "video"),
            P(),
        ),
        check_vma=False,
    )
```
